512 devices in a mesh: head: 16 (over z_hi, y, core), seq: 32 (over z_lo, x).
Axes of the slice: x: 4, y: 4, z: 16 (z_hi: 2, z_lo: 8; z = z_hi * 8 + z_lo), core: 2. Of those that a mesh axis runs over, the one named last changes fastest.
Arguments:
- query_rows: bfloat16 [4096, 3072], P(('seq', 'head')), may hold values from -6 to 6
- key_rows: bfloat16 [4096, 3072], P(('seq', 'head')), may hold values from -6 to 6
- value_rows: bfloat16 [4096, 3072], P(('seq', 'head')), may hold values from -6 to 6
- gate_rows: bfloat16 [4096, 3072], P(('seq', 'head')), may hold values from -1 to 1
- step_rates: float32 [4096, 48], P('seq', 'head'), may hold values from 5e-05 to 0.0005
- first_weight: float32 [48, 64, 256], P('head'), may hold values from -0.75 to 0.75
- first_bias: float32 [48, 256], P('head'), may hold values from -3 to 3
- second_weight: float32 [48, 256, 64], P('head'), may hold values from -0.375 to 0.375
- second_bias: float32 [48, 64], P('head'), may hold values from -3 to 3
- norm_gain: float32 [48, 64], P('head'), may hold values from 0.5 to 1.5
- norm_shift: float32 [48, 64], P('head'), may hold values from -3 to 3
Outputs:
- layer_output: bfloat16 [4096, 3072], P(('seq', 'head'))
The draws below stay inside these ranges and needn't reach their ends.
All inputs are finite; a program needn't handle non-finite values.
Results may differ from the reference program's by a relative error of at most 0.0049.
Values may be sent and summed in bfloat16 or wider, within the bound.
A program may use at most 64 MiB of HBM per device.

```python
import math
import jax
import jax.numpy as jnp
from jax import lax

D_HEAD = 64
INNER = 256
MINI = 64
TOKENS = 4096
HEADS = 48


def block_scale(rng, dims, split, least, largest):
    loudness = 1.0
    for axis_at, shards_of in split:
        steps = jax.random.uniform(jax.random.fold_in(jax.random.fold_in(rng, 6), axis_at), (shards_of,), jnp.float32, least / len(split), largest / len(split))
        loudness = loudness * jnp.repeat(jnp.exp(steps), dims[axis_at] // shards_of).reshape((-1,) + (1,) * (len(dims) - 1 - axis_at))
    return loudness


def bell_draw(own_key, extent, width, bound, pieces=(), held_as=jnp.bfloat16):
    values = width * jax.random.normal(own_key, extent, jnp.float32)
    if pieces:
        values = values * block_scale(own_key, extent, pieces, -0.22, 0.18)
    return jnp.clip(values, -bound, bound).astype(held_as)


def setup_inputs(seed: int = 0) -> dict:
    arg_keys = jax.random.split(jax.random.key(seed), 12)
    return {
        "query_rows": bell_draw(arg_keys[0], (TOKENS, HEADS * D_HEAD), 1.0, 6.0, ((0, 512),)),
        "key_rows": bell_draw(arg_keys[1], (TOKENS, HEADS * D_HEAD), 1.0, 6.0, ((0, 512),)),
        "value_rows": bell_draw(arg_keys[2], (TOKENS, HEADS * D_HEAD), 1.0, 6.0, ((0, 512),)),
        "gate_rows": jnp.clip(jax.random.uniform(arg_keys[3], (TOKENS, HEADS * D_HEAD), jnp.float32, -1.0, 1.0) * block_scale(arg_keys[3], (TOKENS, HEADS * D_HEAD), ((0, 512),), -0.4, 0.0), -1.0, 1.0).astype(jnp.bfloat16),
        "step_rates": jnp.clip(jnp.exp(math.log(0.0005) - 2.3025852 * jax.random.uniform(arg_keys[4], (TOKENS, HEADS), jnp.float32) ** block_scale(arg_keys[4], (TOKENS, HEADS), ((0, 32), (1, 16)), -0.2, 0.2)), 4.999999873689376e-05, 0.0005),
        "first_weight": bell_draw(arg_keys[5], (HEADS, D_HEAD, INNER), D_HEAD ** -0.5, 0.75, ((0, 16),), jnp.float32),
        "first_bias": bell_draw(arg_keys[6], (HEADS, INNER), 0.5, 3.0, ((0, 16),), jnp.float32),
        "second_weight": bell_draw(arg_keys[7], (HEADS, INNER, D_HEAD), INNER ** -0.5, 0.375, ((0, 16),), jnp.float32),
        "second_bias": bell_draw(arg_keys[8], (HEADS, D_HEAD), 0.5, 3.0, ((0, 16),), jnp.float32),
        "norm_gain": jnp.clip(0.5 + 1.0 * jax.random.uniform(arg_keys[9], (HEADS, D_HEAD), jnp.float32) ** block_scale(arg_keys[9], (HEADS, D_HEAD), ((0, 16),), -0.2, 0.2), 0.5, 1.5),
        "norm_shift": bell_draw(arg_keys[10], (HEADS, D_HEAD), 0.5, 3.0, ((0, 16),), jnp.float32),
    }


highest = lax.Precision.HIGHEST
eps_norm = 1e-06
root_factor = 0.7978845608028654
cube_factor = 0.044715

def gelu_tanh(values):
    tanh_term = jnp.tanh(root_factor * (values + cube_factor * values * values * values))
    return 0.5 * values * (1.0 + tanh_term)

def gelu_slope(values):
    tanh_term = jnp.tanh(root_factor * (values + cube_factor * values * values * values))
    return 0.5 * (1.0 + tanh_term) + 0.5 * values * (1.0 - tanh_term * tanh_term) * root_factor * (1.0 + 3.0 * cube_factor * values * values)

def layer_norm(values, gain_row, shift_row):
    centred = values - lax.optimization_barrier(jnp.mean(values, axis=-1, keepdims=True))
    spread = jnp.sqrt(lax.optimization_barrier(jnp.mean(centred * centred, axis=-1, keepdims=True)) + eps_norm)
    normed = centred / spread
    return (normed, spread, gain_row * normed + shift_row)

def mini_step(fast_state, block_data, gain_row, shift_row):
    first_weight, bias_one, second_weight, bias_two = fast_state
    query_block = block_data[0].astype(jnp.float32)
    key_block = block_data[1].astype(jnp.float32)
    value_block = block_data[2].astype(jnp.float32)
    rate_row = block_data[3]
    pre_one = jnp.dot(key_block, first_weight, precision=highest) + bias_one
    act_one = gelu_tanh(pre_one)
    pre_two = jnp.dot(act_one, second_weight, precision=highest) + bias_two
    normed, spread, fitted = layer_norm(pre_two, gain_row, shift_row)
    scaled = gain_row * (fitted - (value_block - key_block))
    grad_two = (scaled - lax.optimization_barrier(jnp.mean(scaled, axis=-1, keepdims=True)) - normed * lax.optimization_barrier(jnp.mean(scaled * normed, axis=-1, keepdims=True))) / spread
    grad_one = jnp.dot(grad_two, second_weight.T, precision=highest) * gelu_slope(pre_one)
    lower_mask = jnp.arange(MINI)[:, None] >= jnp.arange(MINI)[None, :]
    step_matrix = jnp.where(lower_mask, rate_row[None, :], 0.0)
    attend_one = (jnp.dot(query_block, key_block.T, precision=highest) + 1.0) * step_matrix
    dual_one = jnp.dot(query_block, first_weight, precision=highest) + bias_one - jnp.dot(attend_one, grad_one, precision=highest)
    dual_act = gelu_tanh(dual_one)
    attend_two = (jnp.dot(dual_act, act_one.T, precision=highest) + 1.0) * step_matrix
    dual_two = jnp.dot(dual_act, second_weight, precision=highest) + bias_two - jnp.dot(attend_two, grad_two, precision=highest)
    result = layer_norm(dual_two, gain_row, shift_row)[2]
    weighted_one = rate_row[:, None] * grad_one
    weighted_two = rate_row[:, None] * grad_two
    updated = (first_weight - jnp.dot(key_block.T, weighted_one, precision=highest), bias_one - lax.optimization_barrier(jnp.sum(weighted_one, axis=0)), second_weight - jnp.dot(act_one.T, weighted_two, precision=highest), bias_two - lax.optimization_barrier(jnp.sum(weighted_two, axis=0)))
    return (updated, result)

def run_direction(queries, keys_all, values_all, rates_all, first_weight, first_bias, second_weight, second_bias, norm_gain, norm_shift):
    block_count = TOKENS // MINI

    def to_blocks(array_in):
        return array_in.reshape((block_count, MINI) + array_in.shape[1:])

    def one_head(query_head, key_head, value_head, rate_head, weight_one, bias_one, weight_two, bias_two, gain_row, shift_row):

        def advance(fast_state, block_data):
            return mini_step(fast_state, block_data, gain_row, shift_row)
        finished, emitted = lax.scan(advance, (weight_one, bias_one, weight_two, bias_two), (query_head, key_head, value_head, rate_head))
        return emitted
    mapped = jax.vmap(one_head, in_axes=(2, 2, 2, 2, 0, 0, 0, 0, 0, 0), out_axes=2)
    emitted = mapped(to_blocks(queries), to_blocks(keys_all), to_blocks(values_all), to_blocks(rates_all), first_weight, first_bias, second_weight, second_bias, norm_gain, norm_shift)
    return emitted.reshape(TOKENS, HEADS, D_HEAD)

def reference(query_rows, key_rows, value_rows, gate_rows, step_rates, first_weight, first_bias, second_weight, second_bias, norm_gain, norm_shift):

    def by_heads(array_in):
        return array_in.reshape(TOKENS, HEADS, D_HEAD)
    queries = by_heads(query_rows)
    keys_all = by_heads(key_rows)
    values_all = by_heads(value_rows)
    forward = run_direction(queries, keys_all, values_all, step_rates, first_weight, first_bias, second_weight, second_bias, norm_gain, norm_shift)
    backward = run_direction(jnp.flip(queries, 0), jnp.flip(keys_all, 0), jnp.flip(values_all, 0), jnp.flip(step_rates, 0), first_weight, first_bias, second_weight, second_bias, norm_gain, norm_shift)
    backward = jnp.flip(backward, 0)
    summed = (forward + backward).reshape(TOKENS, HEADS * D_HEAD).astype(jnp.bfloat16)
    summed = lax.optimization_barrier(summed)
    return (gate_rows.astype(jnp.float32) * summed.astype(jnp.float32)).astype(jnp.bfloat16)
```

```python
import functools

import jax
import jax.numpy as jnp
from jax import lax
from jax.experimental import pallas as pl
from jax.experimental.pallas import tpu as pltpu
from jax.sharding import PartitionSpec as P

D_HEAD = 64
INNER = 256
MINI = 64
STEPS = 64
LANES = 128
GROUP = 16
CHAIN = 32
HEADS_LOCAL = 3
TILES = 24

EPS = 1e-06
ROOT = 0.7978845608028654
CUBE = 0.044715
MESH = pl.DeviceIdType.MESH
F32 = jnp.float32
BF16 = jnp.bfloat16

SEATS = ((4, 18, 24), (6, 12, 26))


def dot(left, right, dims):
    return lax.dot_general(
        left, right, (((dims[0],), (dims[1],)), ((), ())), preferred_element_type=F32
    )


def gelu(values):
    squared = values * values
    tanh_term = jnp.tanh(values * (ROOT + (ROOT * CUBE) * squared))
    return values * (0.5 + 0.5 * tanh_term)


def gelu_and_slope(values):
    squared = values * values
    tanh_term = jnp.tanh(values * (ROOT + (ROOT * CUBE) * squared))
    half = 0.5 + 0.5 * tanh_term
    slope = half + values * (half * (1.0 - tanh_term)) * (ROOT + (3.0 * ROOT * CUBE) * squared)
    return (values * half, slope)


def row_mean(values):
    return jnp.sum(values, axis=0, keepdims=True) * (1.0 / D_HEAD)


def lanes_left(rows):
    return lax.broadcasted_iota(jnp.int32, (rows, LANES), 1) < D_HEAD


def own_half(stacked):
    return jnp.where(lanes_left(D_HEAD), stacked[:D_HEAD], stacked[D_HEAD:])


def spread_halves(rows):
    left = lanes_left(D_HEAD)
    zero = jnp.zeros_like(rows)
    return jnp.concatenate([jnp.where(left, rows, zero), jnp.where(left, zero, rows)], axis=0)


def seat_of(core, place):
    return SEATS[0][place] + core * (SEATS[1][place] - SEATS[0][place])


def kernel(
    query_ref,
    key_ref,
    value_ref,
    gate_ref,
    rates_ref,
    first_ref,
    first_bias_ref,
    second_ref,
    second_bias_ref,
    gain_ref,
    shift_ref,
    out_ref,
    staged,
    gathered,
    packed,
    tokens,
    blocks_out,
    returned,
    relay_out,
    landed,
    kept_rows,
    bd_key,
    bd_query,
    rate_rows,
    target_rows,
    causal,
    halves,
    state_one,
    bias_one,
    state_two,
    state_two_turned,
    bias_two,
    gain_rows,
    shift_rows,
    pre_one_ref,
    dual_ref,
    act_ref,
    grad_two_ref,
    second_used,
    bias_used,
    send_a,
    recv_a,
    send_b,
    recv_b,
    send_c,
    recv_c,
    send_d,
    recv_d,
):
    head = lax.axis_index("head")
    seq = lax.axis_index("seq")
    core = lax.rem(head, 2)
    seats = [seat_of(core, place) for place in range(HEADS_LOCAL)]

    def is_seat(index):
        return jnp.logical_or(
            index == seats[0], jnp.logical_or(index == seats[1], index == seats[2])
        )

    seated = is_seat(seq)
    my_place = jnp.where(seq == seats[1], 1, 0) + jnp.where(seq == seats[2], 2, 0)

    barrier = pltpu.get_barrier_semaphore()

    @pl.loop(1, GROUP)
    def _(step):
        pl.semaphore_signal(
            barrier,
            inc=1,
            device_id=(lax.rem(head + step, GROUP), seq),
            device_id_type=MESH,
        )

    @pl.when(seated)
    def _():
        @pl.loop(1, CHAIN)
        def _(step):
            pl.semaphore_signal(
                barrier,
                inc=1,
                device_id=(head, lax.rem(seq + step, CHAIN)),
                device_id_type=MESH,
            )

    @pl.when(jnp.logical_not(seated))
    def _():
        for place in range(HEADS_LOCAL):
            pl.semaphore_signal(
                barrier, inc=1, device_id=(head, seats[place]), device_id_type=MESH
            )

    for tile in range(TILES):
        columns = slice(tile * LANES, (tile + 1) * LANES)
        staged[tile, 0] = query_ref[:, columns].astype(F32)
        staged[tile, 1] = key_ref[:, columns].astype(F32)
        staged[tile, 2] = value_ref[:, columns].astype(F32)

    @pl.when(seated)
    def _():
        pl.semaphore_wait(barrier, GROUP - 1 + CHAIN - 1)

    @pl.when(jnp.logical_not(seated))
    def _():
        pl.semaphore_wait(barrier, GROUP - 1 + HEADS_LOCAL)

    def first_tile(group):
        return (3 * group) // 2

    def exchange_copy(step):
        target = lax.rem(head + step, GROUP)
        return pltpu.make_async_remote_copy(
            src_ref=staged.at[pl.ds(first_tile(target), 2)],
            dst_ref=gathered.at[head],
            send_sem=send_a.at[target],
            recv_sem=recv_a.at[head],
            device_id=(target, seq),
            device_id_type=MESH,
        )

    @pl.loop(1, GROUP)
    def _(step):
        exchange_copy(step).start()

    gathered[head] = staged[pl.ds(first_tile(head), 2)]

    @pl.loop(1, GROUP)
    def _(step):
        source = lax.rem(head + GROUP - step, GROUP)
        pltpu.make_async_remote_copy(
            src_ref=staged.at[pl.ds(0, 2)],
            dst_ref=gathered.at[source],
            send_sem=send_a.at[source],
            recv_sem=recv_a.at[source],
            device_id=(source, seq),
            device_id_type=MESH,
        ).wait_recv()

    tall = CHAIN * 4
    lane = lax.broadcasted_iota(jnp.int32, (tall, LANES), 1)
    parity = core
    for place in range(HEADS_LOCAL):
        column = place + parity
        tile = column // 2
        half = lax.rem(column, 2)
        keys = gathered[:, tile, 1].reshape(tall, LANES)
        values = gathered[:, tile, 2].reshape(tall, LANES)
        queries = gathered[:, tile, 0].reshape(tall, LANES)
        at_left = half == 0
        keys_left = jnp.where(at_left, keys, pltpu.roll(keys, D_HEAD, 1))
        values_right = jnp.where(at_left, pltpu.roll(values, D_HEAD, 1), values)
        queries_left = jnp.where(at_left, queries, pltpu.roll(queries, D_HEAD, 1))
        rates = jnp.broadcast_to(rates_ref[:, place : place + 1], (tall, LANES))
        rates_high = rates.astype(BF16).astype(F32)
        rates_low = rates - rates_high
        rates_lanes = jnp.where(
            lane == D_HEAD, rates_high, jnp.where(lane == D_HEAD + 1, rates_low, 0.0)
        )
        packed[place, :, :LANES] = jnp.where(lane < D_HEAD, keys_left, values_right).astype(BF16)
        packed[place, :, LANES:] = jnp.where(lane < D_HEAD, queries_left, rates_lanes).astype(BF16)

    def relay_copy(place):
        return pltpu.make_async_remote_copy(
            src_ref=packed.at[place],
            dst_ref=tokens.at[seq],
            send_sem=send_b.at[place],
            recv_sem=recv_b.at[seq],
            device_id=(head, seats[place]),
            device_id_type=MESH,
        )

    for place in range(HEADS_LOCAL):

        @pl.when(seq != seats[place])
        def _():
            relay_copy(place).start()

    @pl.when(seated)
    def _():
        tokens[seq] = packed[my_place]

        row = lax.broadcasted_iota(jnp.int32, (LANES, LANES), 0)
        col = lax.broadcasted_iota(jnp.int32, (LANES, LANES), 1)
        ahead = jnp.logical_and(jnp.logical_and(row < 64, col < 64), row <= col)
        back = jnp.logical_and(jnp.logical_and(row >= 64, col >= 64), row >= col)
        causal[...] = jnp.where(jnp.logical_or(ahead, back), 1.0, 0.0)
        halves[...] = jnp.where((row < 64) == (col < 64), 1.0, 0.0)

        first = first_ref[my_place]
        both = jnp.concatenate([first, first], axis=0)
        state_one[...] = both.T
        second = second_ref[my_place]
        second = second - jnp.mean(second, axis=1, keepdims=True)
        doubled = jnp.concatenate([second, second], axis=1)
        state_two[...] = doubled
        state_two_turned[...] = doubled.T

        def spread_column(row_values, length):
            return jnp.broadcast_to(row_values, (LANES, length)).T

        bias_one[...] = spread_column(first_bias_ref[pl.ds(my_place, 1), :], INNER)
        second_bias = second_bias_ref[pl.ds(my_place, 1), :]
        second_bias = second_bias - jnp.mean(second_bias, axis=1, keepdims=True)
        bias_two[...] = spread_column(second_bias, D_HEAD)
        gain_rows[...] = spread_column(gain_ref[pl.ds(my_place, 1), :], D_HEAD)
        shift_rows[...] = spread_column(shift_ref[pl.ds(my_place, 1), :], D_HEAD)

        def await_block(block):
            @pl.when(block != seq)
            def _():
                pltpu.make_async_remote_copy(
                    src_ref=packed.at[0],
                    dst_ref=tokens.at[block],
                    send_sem=send_b.at[0],
                    recv_sem=recv_b.at[block],
                    device_id=(head, block),
                    device_id_type=MESH,
                ).wait_recv()

        def block_rows(step):
            return (step // 2, pl.multiple_of(lax.rem(step, 2) * MINI, MINI))

        sub = lax.broadcasted_iota(jnp.int32, (D_HEAD, LANES), 0)
        lan = lax.broadcasted_iota(jnp.int32, (D_HEAD, LANES), 1)
        minus_key = jnp.where(
            lan == sub + D_HEAD, 1.0, jnp.where(lan == sub, -1.0, 0.0)
        ).astype(BF16)
        pick_rate = jnp.where(
            jnp.logical_or(lan == D_HEAD, lan == D_HEAD + 1), 1.0, 0.0
        ).astype(BF16)
        eye_left = jnp.where(row == col, 1.0, 0.0).astype(BF16)

        def load_step(step):
            block_f, rows_f = block_rows(step)
            block_b, rows_b = block_rows(STEPS - 1 - step)
            kv_f = tokens[block_f, pl.ds(rows_f, MINI), :LANES]
            qr_f = tokens[block_f, pl.ds(rows_f, MINI), LANES:]
            kv_b = tokens[block_b, pl.ds(rows_b, MINI), :LANES]
            qr_b = tokens[block_b, pl.ds(rows_b, MINI), LANES:]
            left = lanes_left(MINI)

            def diagonal(ahead_rows, back_rows):
                turned = pltpu.roll(back_rows.astype(F32), D_HEAD, 1)
                return jnp.concatenate(
                    [jnp.where(left, ahead_rows.astype(F32), 0.0), jnp.where(left, 0.0, turned)],
                    axis=0,
                ).astype(BF16)

            keys_bd = diagonal(kv_f, kv_b)
            queries_bd = diagonal(qr_f, qr_b)
            target = dot(minus_key, jnp.concatenate([kv_f, kv_b], axis=0), (1, 1))
            rate = dot(pick_rate, jnp.concatenate([qr_f, qr_b], axis=0), (1, 1))
            return (keys_bd, queries_bd, target, rate)

        def store_step(loaded):
            bd_key[...] = loaded[0]
            bd_query[...] = loaded[1]
            target_rows[...] = gain_rows[...] * (shift_rows[...] - loaded[2])
            rate_rows[...] = loaded[3]

        def emit(step):
            dual_act = gelu(dual_ref[...]).astype(BF16)
            act = act_ref[...]
            attend = dot(act, dual_act, (0, 0))
            mask = causal[...]
            attend = (attend * mask + mask).astype(BF16)
            dual_two = (
                own_half(dot(second_used[...], dual_act, (1, 0)))
                + bias_used[...]
                - dot(grad_two_ref[...], attend, (1, 0))
            )
            centred = dual_two - row_mean(dual_two)
            spread = lax.rsqrt(row_mean(centred * centred) + EPS)
            fitted = gain_rows[...] * (centred * spread) + shift_rows[...]
            kept_rows[step] = fitted
            total = fitted + pltpu.roll(kept_rows[STEPS - 1 - step], D_HEAD, 1)
            total = jnp.concatenate([total, jnp.zeros_like(total)], axis=0).astype(BF16)
            turned = dot(eye_left, total, (1, 1)).astype(BF16)
            blocks_out[step] = turned[:MINI]
            blocks_out[STEPS - 1 - step] = turned[MINI:]

        def gradient(step):
            keys_bd = bd_key[...]
            queries_bd = bd_query[...]
            target = target_rows[...]
            rate = rate_rows[...]
            gain = gain_rows[...]
            second_now = state_two_turned[...]
            second_now_bf = second_now.astype(BF16)
            bias_two_now = bias_two[...]

            act, slope = gelu_and_slope(pre_one_ref[...])
            act = act.astype(BF16)
            pre_two = own_half(dot(second_now_bf, act, (1, 0))) + bias_two_now
            gain_sq = gain * gain
            mean_two = row_mean(pre_two)
            centred = pre_two - mean_two
            scaled = gain_sq * centred
            inverse = lax.rsqrt(row_mean(centred * centred) + EPS)
            mean_a = inverse * row_mean(scaled) + row_mean(target)
            mean_an = inverse * (
                inverse * row_mean(scaled * centred) + row_mean(target * centred)
            )
            grad_two = (
                scaled * inverse + target - mean_a - centred * (inverse * mean_an)
            ) * (inverse * rate)
            grad_two = grad_two.astype(BF16)
            grad_two_bd = spread_halves(grad_two)
            state_two_now = state_two[...]
            grad_one = dot(state_two_now.astype(BF16), grad_two_bd, (1, 0)) * slope
            grad_one = grad_one.astype(BF16)

            later = jnp.minimum(step + 1, STEPS - 1)
            loaded = load_step(later)
            ones_bd = halves[...]
            mask = causal[...]
            between = (dot(keys_bd, loaded[0], (1, 1)) + ones_bd).astype(BF16)
            within = (dot(keys_bd, queries_bd, (1, 1)) * mask + mask).astype(BF16)
            ones_bf = ones_bd.astype(BF16)
            fall = dot(grad_one, jnp.concatenate([between, keys_bd], axis=1), (1, 0))
            fall_out = dot(grad_one, jnp.concatenate([within, ones_bf], axis=1), (1, 0))

            state_one_now = state_one[...]
            high = state_one_now.astype(BF16)
            low = (state_one_now - high.astype(F32)).astype(BF16)
            reads = jnp.concatenate([loaded[0], queries_bd], axis=0)
            seen = dot(
                jnp.concatenate([high, low], axis=1),
                jnp.concatenate([reads, reads], axis=1),
                (1, 1),
            )
            bias_one_now = bias_one[...]
            pre_one_ref[...] = seen[:, :LANES] + bias_one_now - fall[:, :LANES]
            dual_ref[...] = seen[:, LANES:] + bias_one_now - fall_out[:, :LANES]
            state_one[...] = state_one_now - fall[:, LANES:]
            bias_one[...] = bias_one_now - fall_out[:, LANES:]
            state_two[...] = state_two_now - dot(act, grad_two_bd, (1, 1))
            state_two_turned[...] = second_now - dot(grad_two_bd, act, (1, 1))
            bias_two[...] = bias_two_now - dot(grad_two, ones_bf, (1, 0))
            act_ref[...] = act
            grad_two_ref[...] = grad_two
            second_used[...] = second_now_bf
            bias_used[...] = bias_two_now
            store_step(loaded)

        def return_copy(block):
            return pltpu.make_async_remote_copy(
                src_ref=blocks_out.at[pl.ds(2 * block, 2)],
                dst_ref=returned.at[my_place],
                send_sem=send_c.at[block],
                recv_sem=recv_c.at[my_place],
                device_id=(head, block),
                device_id_type=MESH,
            )

        def give_back(block):
            @pl.when(block != seq)
            def _():
                return_copy(block).start()

            @pl.when(block == seq)
            def _():
                returned[my_place] = blocks_out[pl.ds(2 * block, 2)]

        await_block(0)
        await_block(CHAIN - 1)
        begun = load_step(0)
        store_step(begun)
        high = state_one[...].astype(BF16)
        low = (state_one[...] - high.astype(F32)).astype(BF16)
        pre_one_ref[...] = (
            dot(high, begun[0], (1, 1)) + dot(low, begun[0], (1, 1)) + bias_one[...]
        )

        @pl.loop(0, STEPS)
        def _(step):
            later = step + 1

            @pl.when(jnp.logical_and(lax.rem(later, 2) == 0, later < STEPS // 2))
            def _():
                await_block(later // 2)
                await_block(CHAIN - 1 - later // 2)

            emit(jnp.maximum(step - 1, 0))
            gradient(step)

            done = step - 1

            @pl.when(jnp.logical_and(lax.rem(done, 2) == 1, done > STEPS // 2))
            def _():
                give_back(done // 2)
                give_back(CHAIN - 1 - done // 2)

        emit(STEPS - 1)
        give_back(CHAIN - 1)
        give_back(0)

        @pl.loop(1, CHAIN)
        def _(step):
            return_copy(lax.rem(seq + step, CHAIN)).wait_send()

    for place in range(HEADS_LOCAL):

        @pl.when(seq != seats[place])
        def _():
            pltpu.make_async_remote_copy(
                src_ref=blocks_out.at[pl.ds(0, 2)],
                dst_ref=returned.at[place],
                send_sem=send_c.at[0],
                recv_sem=recv_c.at[place],
                device_id=(head, seats[place]),
                device_id_type=MESH,
            ).wait_recv()

    shape = (GROUP, 8, LANES)
    zeros = jnp.zeros(shape, F32)
    parts = [returned[place].reshape(tall, LANES).astype(F32) for place in range(HEADS_LOCAL)]
    turned = [pltpu.roll(part, D_HEAD, 1) for part in parts]
    even = parity == 0
    relay_out[:, 0] = jnp.where(even, parts[0] + turned[1], turned[0]).reshape(shape)
    relay_out[:, 1] = jnp.where(even, parts[2], parts[1] + turned[2]).reshape(shape)

    def spread_copy(step):
        target = lax.rem(head + step, GROUP)
        return pltpu.make_async_remote_copy(
            src_ref=relay_out.at[target],
            dst_ref=landed.at[head],
            send_sem=send_d.at[target],
            recv_sem=recv_d.at[head],
            device_id=(target, seq),
            device_id_type=MESH,
        )

    @pl.loop(1, GROUP)
    def _(step):
        spread_copy(step).start()

    landed[head] = relay_out[head]

    @pl.loop(1, GROUP)
    def _(step):
        source = lax.rem(head + GROUP - step, GROUP)
        pltpu.make_async_remote_copy(
            src_ref=relay_out.at[source],
            dst_ref=landed.at[source],
            send_sem=send_d.at[source],
            recv_sem=recv_d.at[source],
            device_id=(source, seq),
            device_id_type=MESH,
        ).wait_recv()

    for pair in range(GROUP // 2):
        summed = (
            landed[2 * pair, 0],
            landed[2 * pair, 1] + landed[2 * pair + 1, 0],
            landed[2 * pair + 1, 1],
        )
        for tile in range(3):
            columns = slice((3 * pair + tile) * LANES, (3 * pair + tile + 1) * LANES)
            out_ref[:, columns] = (gate_ref[:, columns].astype(F32) * summed[tile]).astype(BF16)

    @pl.loop(1, GROUP)
    def _(step):
        exchange_copy(step).wait_send()
        spread_copy(step).wait_send()

    for place in range(HEADS_LOCAL):

        @pl.when(seq != seats[place])
        def _():
            relay_copy(place).wait_send()


def local(*arrays):
    vmem = pl.BlockSpec(memory_space=pltpu.VMEM)
    dma = pltpu.SemaphoreType.DMA
    return pl.pallas_call(
        kernel,
        out_shape=jax.ShapeDtypeStruct((8, TILES * LANES), BF16),
        in_specs=[vmem] * len(arrays),
        out_specs=vmem,
        scratch_shapes=[
            pltpu.VMEM((TILES, 3, 8, LANES), F32),
            pltpu.VMEM((GROUP, 2, 3, 8, LANES), F32),
            pltpu.VMEM((HEADS_LOCAL, 128, 2 * LANES), BF16),
            pltpu.VMEM((CHAIN, 128, 2 * LANES), BF16),
            pltpu.VMEM((STEPS, MINI, LANES), BF16),
            pltpu.VMEM((HEADS_LOCAL, 2, MINI, LANES), BF16),
            pltpu.VMEM((GROUP, 2, 8, LANES), F32),
            pltpu.VMEM((GROUP, 2, 8, LANES), F32),
            pltpu.VMEM((STEPS, D_HEAD, LANES), F32),
            pltpu.VMEM((LANES, LANES), BF16),
            pltpu.VMEM((LANES, LANES), BF16),
            pltpu.VMEM((D_HEAD, LANES), F32),
            pltpu.VMEM((D_HEAD, LANES), F32),
            pltpu.VMEM((LANES, LANES), F32),
            pltpu.VMEM((LANES, LANES), F32),
            pltpu.VMEM((INNER, LANES), F32),
            pltpu.VMEM((INNER, LANES), F32),
            pltpu.VMEM((INNER, LANES), F32),
            pltpu.VMEM((LANES, INNER), F32),
            pltpu.VMEM((D_HEAD, LANES), F32),
            pltpu.VMEM((D_HEAD, LANES), F32),
            pltpu.VMEM((D_HEAD, LANES), F32),
            pltpu.VMEM((INNER, LANES), F32),
            pltpu.VMEM((INNER, LANES), F32),
            pltpu.VMEM((INNER, LANES), BF16),
            pltpu.VMEM((D_HEAD, LANES), BF16),
            pltpu.VMEM((LANES, INNER), BF16),
            pltpu.VMEM((D_HEAD, LANES), F32),
            dma((GROUP,)),
            dma((GROUP,)),
            dma((HEADS_LOCAL,)),
            dma((CHAIN,)),
            dma((CHAIN,)),
            dma((HEADS_LOCAL,)),
            dma((GROUP,)),
            dma((GROUP,)),
        ],
        compiler_params=pltpu.CompilerParams(collective_id=0, has_side_effects=True),
    )(*arrays)


def solution(mesh):
    rows = P(("seq", "head"), None)
    in_specs = (
        rows,
        rows,
        rows,
        rows,
        P("seq", "head"),
        P("head", None, None),
        P("head", None),
        P("head", None, None),
        P("head", None),
        P("head", None),
        P("head", None),
    )
    return jax.shard_map(local, mesh=mesh, in_specs=in_specs, out_specs=rows, check_vma=False)
```

```python
import functools

import jax
import jax.numpy as jnp
from jax import lax
from jax.experimental import pallas as pl
from jax.experimental.pallas import tpu as pltpu
from jax.sharding import PartitionSpec as P

D_HEAD = 64
INNER = 256
MINI = 64
STEPS = 64
LANES = 128
GROUP = 16
CHAIN = 32
HEADS_LOCAL = 3
TILES = 24

EPS = 1e-06
ROOT = 0.7978845608028654
CUBE = 0.044715
MESH = pl.DeviceIdType.MESH
F32 = jnp.float32
BF16 = jnp.bfloat16

SEATS = ((4, 18, 24), (6, 12, 26))


def dot(left, right, dims):
    return lax.dot_general(
        left, right, (((dims[0],), (dims[1],)), ((), ())), preferred_element_type=F32
    )


def gelu(values):
    squared = values * values
    tanh_term = jnp.tanh(values * (ROOT + (ROOT * CUBE) * squared))
    return values * (0.5 + 0.5 * tanh_term)


def gelu_and_slope(values):
    squared = values * values
    tanh_term = jnp.tanh(values * (ROOT + (ROOT * CUBE) * squared))
    half = 0.5 + 0.5 * tanh_term
    slope = half + values * (half * (1.0 - tanh_term)) * (ROOT + (3.0 * ROOT * CUBE) * squared)
    return (values * half, slope)


def row_mean(values):
    rows = values.shape[0]
    while rows > 8:
        rows //= 2
        values = values[:rows] + values[rows:]
    return jnp.sum(values, axis=0, keepdims=True) * (1.0 / D_HEAD)


def lanes_left(rows):
    return lax.broadcasted_iota(jnp.int32, (rows, LANES), 1) < D_HEAD


def own_half(stacked):
    return jnp.where(lanes_left(D_HEAD), stacked[:D_HEAD], stacked[D_HEAD:])


def spread_halves(rows):
    left = lanes_left(D_HEAD)
    zero = jnp.zeros_like(rows)
    return jnp.concatenate([jnp.where(left, rows, zero), jnp.where(left, zero, rows)], axis=0)


def seat_of(core, place):
    return SEATS[0][place] + core * (SEATS[1][place] - SEATS[0][place])


def kernel(
    query_ref,
    key_ref,
    value_ref,
    gate_ref,
    rates_ref,
    first_ref,
    first_bias_ref,
    second_ref,
    second_bias_ref,
    gain_ref,
    shift_ref,
    out_ref,
    staged,
    gathered,
    packed,
    tokens,
    blocks_out,
    returned,
    relay_out,
    landed,
    kept_rows,
    bd_key,
    turned_query,
    rate_rows,
    target_rows,
    causal,
    halves,
    state_one,
    bias_one,
    state_two,
    second_next,
    bias_two,
    gain_rows,
    shift_rows,
    pre_one_ref,
    dual_ref,
    act_ref,
    grad_two_ref,
    second_used,
    bias_used,
    send_a,
    recv_a,
    send_b,
    recv_b,
    send_c,
    recv_c,
    send_d,
    recv_d,
):
    head = lax.axis_index("head")
    seq = lax.axis_index("seq")
    core = lax.rem(head, 2)
    seats = [seat_of(core, place) for place in range(HEADS_LOCAL)]

    def is_seat(index):
        return jnp.logical_or(
            index == seats[0], jnp.logical_or(index == seats[1], index == seats[2])
        )

    seated = is_seat(seq)
    my_place = jnp.where(seq == seats[1], 1, 0) + jnp.where(seq == seats[2], 2, 0)

    barrier = pltpu.get_barrier_semaphore()

    @pl.loop(1, GROUP)
    def _(step):
        pl.semaphore_signal(
            barrier,
            inc=1,
            device_id=(lax.rem(head + step, GROUP), seq),
            device_id_type=MESH,
        )

    @pl.when(seated)
    def _():
        @pl.loop(1, CHAIN)
        def _(step):
            pl.semaphore_signal(
                barrier,
                inc=1,
                device_id=(head, lax.rem(seq + step, CHAIN)),
                device_id_type=MESH,
            )

    @pl.when(jnp.logical_not(seated))
    def _():
        for place in range(HEADS_LOCAL):
            pl.semaphore_signal(
                barrier, inc=1, device_id=(head, seats[place]), device_id_type=MESH
            )

    for tile in range(TILES):
        columns = slice(tile * LANES, (tile + 1) * LANES)
        staged[tile, 0] = query_ref[:, columns]
        staged[tile, 1] = key_ref[:, columns]
        staged[tile, 2] = value_ref[:, columns]

    @pl.when(seated)
    def _():
        pl.semaphore_wait(barrier, GROUP - 1 + CHAIN - 1)

    @pl.when(jnp.logical_not(seated))
    def _():
        pl.semaphore_wait(barrier, GROUP - 1 + HEADS_LOCAL)

    def first_tile(group):
        return (3 * group) // 2

    def exchange_copy(step):
        target = lax.rem(head + step, GROUP)
        return pltpu.make_async_remote_copy(
            src_ref=staged.at[pl.ds(first_tile(target), 2)],
            dst_ref=gathered.at[head],
            send_sem=send_a.at[target],
            recv_sem=recv_a.at[head],
            device_id=(target, seq),
            device_id_type=MESH,
        )

    @pl.loop(1, GROUP)
    def _(step):
        exchange_copy(step).start()

    gathered[head] = staged[pl.ds(first_tile(head), 2)]

    @pl.loop(1, GROUP)
    def _(step):
        source = lax.rem(head + GROUP - step, GROUP)
        pltpu.make_async_remote_copy(
            src_ref=staged.at[pl.ds(0, 2)],
            dst_ref=gathered.at[source],
            send_sem=send_a.at[source],
            recv_sem=recv_a.at[source],
            device_id=(source, seq),
            device_id_type=MESH,
        ).wait_recv()

    tall = CHAIN * 4
    lane = lax.broadcasted_iota(jnp.int32, (tall, LANES), 1)
    parity = core
    for place in range(HEADS_LOCAL):
        column = place + parity
        tile = column // 2
        half = lax.rem(column, 2)
        keys = gathered[:, tile, 1].reshape(tall, LANES).astype(F32)
        values = gathered[:, tile, 2].reshape(tall, LANES).astype(F32)
        queries = gathered[:, tile, 0].reshape(tall, LANES).astype(F32)
        at_left = half == 0
        keys_left = jnp.where(at_left, keys, pltpu.roll(keys, D_HEAD, 1))
        values_right = jnp.where(at_left, pltpu.roll(values, D_HEAD, 1), values)
        queries_left = jnp.where(at_left, queries, pltpu.roll(queries, D_HEAD, 1))
        rates = jnp.broadcast_to(rates_ref[place : place + 1], (LANES, tall)).T
        rates_high = rates.astype(BF16).astype(F32)
        rates_low = rates - rates_high
        rates_lanes = jnp.where(
            lane == D_HEAD, rates_high, jnp.where(lane == D_HEAD + 1, rates_low, 0.0)
        )
        packed[place, :, :LANES] = jnp.where(lane < D_HEAD, keys_left, values_right).astype(BF16)
        packed[place, :, LANES:] = jnp.where(lane < D_HEAD, queries_left, rates_lanes).astype(BF16)

    def relay_copy(place):
        return pltpu.make_async_remote_copy(
            src_ref=packed.at[place],
            dst_ref=tokens.at[seq],
            send_sem=send_b.at[place],
            recv_sem=recv_b.at[seq],
            device_id=(head, seats[place]),
            device_id_type=MESH,
        )

    for place in range(HEADS_LOCAL):

        @pl.when(seq != seats[place])
        def _():
            relay_copy(place).start()

    @pl.when(seated)
    def _():
        tokens[seq] = packed[my_place]

        row = lax.broadcasted_iota(jnp.int32, (LANES, LANES), 0)
        col = lax.broadcasted_iota(jnp.int32, (LANES, LANES), 1)
        ahead = jnp.logical_and(jnp.logical_and(row < 64, col < 64), row <= col)
        back = jnp.logical_and(jnp.logical_and(row >= 64, col >= 64), row >= col)
        causal[...] = jnp.where(jnp.logical_or(ahead, back), 1.0, 0.0)
        halves[...] = jnp.where((row < 64) == (col < 64), 1.0, 0.0)

        first = first_ref[my_place]
        both = jnp.concatenate([first, first], axis=0)
        state_one[...] = both.T
        second = second_ref[my_place]
        second = second - jnp.mean(second, axis=0, keepdims=True)
        doubled = jnp.concatenate([second, second], axis=0)
        state_two[...] = doubled.T
        second_next[...] = doubled.astype(BF16)

        def spread_column(row_values, length):
            return jnp.broadcast_to(row_values, (LANES, length)).T

        bias_one[...] = spread_column(first_bias_ref[pl.ds(my_place, 1), :], INNER)
        second_bias = second_bias_ref[pl.ds(my_place, 1), :]
        second_bias = second_bias - jnp.mean(second_bias, axis=1, keepdims=True)
        bias_two[...] = spread_column(second_bias, D_HEAD)
        gain_rows[...] = spread_column(gain_ref[pl.ds(my_place, 1), :], D_HEAD)
        shift_rows[...] = spread_column(shift_ref[pl.ds(my_place, 1), :], D_HEAD)

        def await_block(block):
            @pl.when(block != seq)
            def _():
                pltpu.make_async_remote_copy(
                    src_ref=packed.at[0],
                    dst_ref=tokens.at[block],
                    send_sem=send_b.at[0],
                    recv_sem=recv_b.at[block],
                    device_id=(head, block),
                    device_id_type=MESH,
                ).wait_recv()

        def block_rows(step):
            return (step // 2, pl.multiple_of(lax.rem(step, 2) * MINI, MINI))

        def load_step(step):
            block_f, rows_f = block_rows(step)
            block_b, rows_b = block_rows(STEPS - 1 - step)
            kv_f = tokens[block_f, pl.ds(rows_f, MINI), :LANES]
            qr_f = tokens[block_f, pl.ds(rows_f, MINI), LANES:]
            kv_b = tokens[block_b, pl.ds(rows_b, MINI), :LANES]
            qr_b = tokens[block_b, pl.ds(rows_b, MINI), LANES:]
            left = lanes_left(MINI)
            turned_b = pltpu.roll(kv_b.astype(F32), D_HEAD, 1)
            keys_bd = jnp.concatenate(
                [jnp.where(left, kv_f.astype(F32), 0.0), jnp.where(left, 0.0, turned_b)], axis=0
            ).astype(BF16)
            kv_turned = jnp.concatenate([kv_f, kv_b], axis=0).T.astype(F32)
            qr_turned = jnp.concatenate([qr_f, qr_b], axis=0).T.astype(F32)
            target = kv_turned[D_HEAD:] - kv_turned[:D_HEAD]
            rate = qr_turned[D_HEAD : D_HEAD + 1] + qr_turned[D_HEAD + 1 : D_HEAD + 2]
            keys_turned = spread_halves(kv_turned[:D_HEAD]).astype(BF16)
            queries_turned = spread_halves(qr_turned[:D_HEAD]).astype(BF16)
            return (keys_bd, keys_turned, queries_turned, target, rate)

        def store_step(loaded):
            bd_key[...] = loaded[0]
            turned_query[...] = loaded[2]
            target_rows[...] = gain_rows[...] * (shift_rows[...] - loaded[3])
            rate_rows[...] = jnp.broadcast_to(loaded[4], (8, LANES))

        def finish(step, dual_two):
            mean = row_mean(dual_two)
            spread = lax.rsqrt(row_mean(dual_two * dual_two) - mean * mean + EPS)
            fitted = gain_rows[...] * ((dual_two - mean) * spread) + shift_rows[...]
            kept_rows[step] = fitted
            total = fitted + pltpu.roll(kept_rows[STEPS - 1 - step], D_HEAD, 1)
            total = jnp.concatenate([total, jnp.zeros_like(total)], axis=0).astype(BF16)
            turned = total.T
            blocks_out[step] = turned[:MINI]
            blocks_out[STEPS - 1 - step] = turned[MINI:]

        def attend_dual(dual_act):
            mask = causal[...]
            read = dot(second_used[...], dual_act, (1, 0))
            attend = dot(act_ref[...].T, dual_act, (1, 0))
            return (own_half(read) + bias_used[...], (attend * mask + mask).astype(BF16))

        def advance(step):
            second_turned = second_next[...]
            target = target_rows[...]
            gain = gain_rows[...]
            gain_sq = gain * gain
            rate = rate_rows[0:1]
            bias_two_now = bias_two[...]

            act, slope = gelu_and_slope(pre_one_ref[...])
            act = act.astype(BF16)
            pre_two = (
                jnp.where(
                    lanes_left(D_HEAD),
                    dot(second_turned[:D_HEAD], act, (1, 0)),
                    dot(second_turned[D_HEAD:], act, (1, 0)),
                )
                + bias_two_now
            )

            dual_act = gelu(dual_ref[...]).astype(BF16)
            dual_read, attend = attend_dual(dual_act)

            later = jnp.minimum(step + 1, STEPS - 1)
            loaded = load_step(later)
            keys_bd = bd_key[...]
            queries_turned = turned_query[...]
            ones_bd = halves[...]
            ones_bf = ones_bd.astype(BF16)
            mask = causal[...]
            state_one_now = state_one[...]
            high = state_one_now.astype(BF16)
            low = (state_one_now - high.astype(F32)).astype(BF16)
            reads = jnp.concatenate([loaded[1], queries_turned], axis=1)
            reads = jnp.concatenate([reads, reads], axis=0)
            within_both = dot(
                jnp.concatenate([keys_bd, jnp.zeros_like(keys_bd)], axis=1), reads, (1, 0)
            )
            between = (within_both[:, :LANES] + ones_bd).astype(BF16)
            within = (within_both[:, LANES:] * mask + mask).astype(BF16)
            seen = dot(jnp.concatenate([high, low], axis=1), reads, (1, 0))

            scaled = gain_sq * pre_two
            mean = row_mean(pre_two)
            sum_scaled = row_mean(scaled)
            sum_square = row_mean(pre_two * pre_two)
            sum_scaled_sq = row_mean(scaled * pre_two)
            sum_target = row_mean(target * pre_two)
            mean_gain = row_mean(gain_sq)
            mean_target = row_mean(target)
            inverse = lax.rsqrt(sum_square - mean * mean + EPS)
            centred_scaled = sum_scaled - mean * mean_gain
            mean_a = inverse * centred_scaled + mean_target
            mean_an = inverse * (
                inverse * (sum_scaled_sq - mean * (sum_scaled + centred_scaled))
                + (sum_target - mean * mean_target)
            )
            weight = inverse * rate
            grad_two = (
                (pre_two - mean) * (inverse * gain_sq - inverse * mean_an) + (target - mean_a)
            ) * weight
            grad_two = grad_two.astype(BF16)
            grad_two_bd = spread_halves(grad_two)
            state_two_now = state_two[...]
            state_two_bf = state_two_now.astype(BF16)
            half = INNER // 2
            grad_top = (dot(state_two_bf[:half], grad_two_bd, (1, 0)) * slope[:half]).astype(BF16)
            grad_low = (dot(state_two_bf[half:], grad_two_bd, (1, 0)) * slope[half:]).astype(BF16)

            dual_two = dual_read - dot(grad_two_ref[...], attend, (1, 0))
            finish(jnp.maximum(step - 1, 0), dual_two)

            state_two_new = state_two_now - dot(act, grad_two_bd.T, (1, 0))
            bias_two[...] = bias_two_now - dot(grad_two, ones_bf, (1, 0))
            state_two[...] = state_two_new
            second_next[...] = state_two_new.astype(BF16).T

            moves = jnp.concatenate([between, keys_bd], axis=1)
            sums = jnp.concatenate([within, ones_bf], axis=1)
            for rows, part in ((slice(0, half), grad_top), (slice(half, INNER), grad_low)):
                fall = dot(part, moves, (1, 0))
                bias_one_now = bias_one[rows, :]
                pre_one_ref[rows, :] = seen[rows, :LANES] + bias_one_now - fall[:, :LANES]
                state_one[rows, :] = state_one_now[rows] - fall[:, LANES:]
            for rows, part in ((slice(0, half), grad_top), (slice(half, INNER), grad_low)):
                fall_out = dot(part, sums, (1, 0))
                bias_one_now = bias_one[rows, :]
                dual_ref[rows, :] = seen[rows, LANES:] + bias_one_now - fall_out[:, :LANES]
                bias_one[rows, :] = bias_one_now - fall_out[:, LANES:]

            act_ref[...] = act
            grad_two_ref[...] = grad_two
            second_used[...] = second_turned
            bias_used[...] = bias_two_now
            store_step(loaded)

        def return_copy(block):
            return pltpu.make_async_remote_copy(
                src_ref=blocks_out.at[pl.ds(2 * block, 2)],
                dst_ref=returned.at[my_place],
                send_sem=send_c.at[block],
                recv_sem=recv_c.at[my_place],
                device_id=(head, block),
                device_id_type=MESH,
            )

        def give_back(block):
            @pl.when(block != seq)
            def _():
                return_copy(block).start()

            @pl.when(block == seq)
            def _():
                returned[my_place] = blocks_out[pl.ds(2 * block, 2)]

        await_block(0)
        await_block(CHAIN - 1)
        begun = load_step(0)
        store_step(begun)
        high = state_one[...].astype(BF16)
        low = (state_one[...] - high.astype(F32)).astype(BF16)
        pre_one_ref[...] = (
            dot(high, begun[1], (1, 0)) + dot(low, begun[1], (1, 0)) + bias_one[...]
        )

        @pl.loop(0, STEPS)
        def _(step):
            later = step + 1

            @pl.when(jnp.logical_and(lax.rem(later, 2) == 0, later < STEPS // 2))
            def _():
                await_block(later // 2)
                await_block(CHAIN - 1 - later // 2)

            advance(step)

            done = step - 1

            @pl.when(jnp.logical_and(lax.rem(done, 2) == 1, done > STEPS // 2))
            def _():
                give_back(done // 2)
                give_back(CHAIN - 1 - done // 2)

        dual_read, attend = attend_dual(gelu(dual_ref[...]).astype(BF16))
        finish(STEPS - 1, dual_read - dot(grad_two_ref[...], attend, (1, 0)))
        give_back(CHAIN - 1)
        give_back(0)

        @pl.loop(1, CHAIN)
        def _(step):
            return_copy(lax.rem(seq + step, CHAIN)).wait_send()

    for place in range(HEADS_LOCAL):

        @pl.when(seq != seats[place])
        def _():
            pltpu.make_async_remote_copy(
                src_ref=blocks_out.at[pl.ds(0, 2)],
                dst_ref=returned.at[place],
                send_sem=send_c.at[0],
                recv_sem=recv_c.at[place],
                device_id=(head, seats[place]),
                device_id_type=MESH,
            ).wait_recv()

    shape = (GROUP, 8, LANES)
    parts = [returned[place].reshape(tall, LANES).astype(F32) for place in range(HEADS_LOCAL)]
    turned = [pltpu.roll(part, D_HEAD, 1) for part in parts]
    even = parity == 0
    relay_out[:, 0] = jnp.where(even, parts[0] + turned[1], turned[0]).astype(BF16).reshape(shape)
    relay_out[:, 1] = jnp.where(even, parts[2], parts[1] + turned[2]).astype(BF16).reshape(shape)

    def spread_copy(step):
        target = lax.rem(head + step, GROUP)
        return pltpu.make_async_remote_copy(
            src_ref=relay_out.at[target],
            dst_ref=landed.at[head],
            send_sem=send_d.at[target],
            recv_sem=recv_d.at[head],
            device_id=(target, seq),
            device_id_type=MESH,
        )

    @pl.loop(1, GROUP)
    def _(step):
        spread_copy(step).start()

    landed[head] = relay_out[head]

    @pl.loop(1, GROUP)
    def _(step):
        source = lax.rem(head + GROUP - step, GROUP)
        pltpu.make_async_remote_copy(
            src_ref=relay_out.at[source],
            dst_ref=landed.at[source],
            send_sem=send_d.at[source],
            recv_sem=recv_d.at[source],
            device_id=(source, seq),
            device_id_type=MESH,
        ).wait_recv()

    for pair in range(GROUP // 2):
        ends = [landed[2 * pair + side, tile].astype(F32) for side in (0, 1) for tile in (0, 1)]
        summed = (ends[0], ends[1] + ends[2], ends[3])
        for tile in range(3):
            columns = slice((3 * pair + tile) * LANES, (3 * pair + tile + 1) * LANES)
            out_ref[:, columns] = (gate_ref[:, columns].astype(F32) * summed[tile]).astype(BF16)

    @pl.loop(1, GROUP)
    def _(step):
        exchange_copy(step).wait_send()
        spread_copy(step).wait_send()

    for place in range(HEADS_LOCAL):

        @pl.when(seq != seats[place])
        def _():
            relay_copy(place).wait_send()


def local(*arrays):
    arrays = list(arrays)
    arrays[4] = arrays[4].T
    arrays[7] = jnp.swapaxes(arrays[7], 1, 2)
    vmem = pl.BlockSpec(memory_space=pltpu.VMEM)
    dma = pltpu.SemaphoreType.DMA
    return pl.pallas_call(
        kernel,
        out_shape=jax.ShapeDtypeStruct((8, TILES * LANES), BF16),
        in_specs=[vmem] * len(arrays),
        out_specs=vmem,
        scratch_shapes=[
            pltpu.VMEM((TILES, 3, 8, LANES), BF16),
            pltpu.VMEM((GROUP, 2, 3, 8, LANES), BF16),
            pltpu.VMEM((HEADS_LOCAL, 128, 2 * LANES), BF16),
            pltpu.VMEM((CHAIN, 128, 2 * LANES), BF16),
            pltpu.VMEM((STEPS, MINI, LANES), BF16),
            pltpu.VMEM((HEADS_LOCAL, 2, MINI, LANES), BF16),
            pltpu.VMEM((GROUP, 2, 8, LANES), BF16),
            pltpu.VMEM((GROUP, 2, 8, LANES), BF16),
            pltpu.VMEM((STEPS, D_HEAD, LANES), F32),
            pltpu.VMEM((LANES, LANES), BF16),
            pltpu.VMEM((LANES, LANES), BF16),
            pltpu.VMEM((8, LANES), F32),
            pltpu.VMEM((D_HEAD, LANES), F32),
            pltpu.VMEM((LANES, LANES), F32),
            pltpu.VMEM((LANES, LANES), F32),
            pltpu.VMEM((INNER, LANES), F32),
            pltpu.VMEM((INNER, LANES), F32),
            pltpu.VMEM((INNER, LANES), F32),
            pltpu.VMEM((LANES, INNER), BF16),
            pltpu.VMEM((D_HEAD, LANES), F32),
            pltpu.VMEM((D_HEAD, LANES), F32),
            pltpu.VMEM((D_HEAD, LANES), F32),
            pltpu.VMEM((INNER, LANES), F32),
            pltpu.VMEM((INNER, LANES), F32),
            pltpu.VMEM((INNER, LANES), BF16),
            pltpu.VMEM((D_HEAD, LANES), BF16),
            pltpu.VMEM((LANES, INNER), BF16),
            pltpu.VMEM((D_HEAD, LANES), F32),
            dma((GROUP,)),
            dma((GROUP,)),
            dma((HEADS_LOCAL,)),
            dma((CHAIN,)),
            dma((CHAIN,)),
            dma((HEADS_LOCAL,)),
            dma((GROUP,)),
            dma((GROUP,)),
        ],
        compiler_params=pltpu.CompilerParams(collective_id=0, has_side_effects=True),
    )(*arrays)


def solution(mesh):
    rows = P(("seq", "head"), None)
    in_specs = (
        rows,
        rows,
        rows,
        rows,
        P("seq", "head"),
        P("head", None, None),
        P("head", None),
        P("head", None, None),
        P("head", None),
        P("head", None),
        P("head", None),
    )
    return jax.shard_map(local, mesh=mesh, in_specs=in_specs, out_specs=rows, check_vma=False)
```

```python
import functools

import jax
import jax.numpy as jnp
from jax import lax
from jax.experimental import pallas as pl
from jax.experimental.pallas import tpu as pltpu
from jax.sharding import PartitionSpec as P

D_HEAD = 64
INNER = 256
MINI = 64
STEPS = 64
LANES = 128
NEAR = 8
CHAIN = 32
HEADS_LOCAL = 3
HEADS_NEAR = 6
WIDE = HEADS_NEAR * D_HEAD
TILES = 24

EPS = 1e-06
ROOT = 0.7978845608028654
CUBE = 0.044715
MESH = pl.DeviceIdType.MESH
F32 = jnp.float32
BF16 = jnp.bfloat16

PACKED = MINI + MINI // 2
HISTORY = 4
SPACING_NS = 700

SEATS = (((4, 17, 26), (15, 24, 5)), ((6, 19, 24), (13, 26, 7)))


def dot(left, right, dims):
    return lax.dot_general(
        left, right, (((dims[0],), (dims[1],)), ((), ())), preferred_element_type=F32
    )


def gelu(values):
    squared = values * values
    tanh_term = jnp.tanh(values * (ROOT + (ROOT * CUBE) * squared))
    return values * (0.5 + 0.5 * tanh_term)


def gelu_and_slope(values):
    squared = values * values
    tanh_term = jnp.tanh(values * (ROOT + (ROOT * CUBE) * squared))
    half = 0.5 + 0.5 * tanh_term
    slope = half + values * (half * (1.0 - tanh_term)) * (ROOT + (3.0 * ROOT * CUBE) * squared)
    return (values * half, slope)


def row_mean(values):
    rows = values.shape[0]
    while rows > 8:
        rows //= 2
        values = values[:rows] + values[rows:]
    return jnp.sum(values, axis=0, keepdims=True) * (1.0 / D_HEAD)


def lanes_left(rows):
    return lax.broadcasted_iota(jnp.int32, (rows, LANES), 1) < D_HEAD


def own_half(stacked):
    return jnp.where(lanes_left(D_HEAD), stacked[:D_HEAD], stacked[D_HEAD:])


def spread_halves(rows):
    left = lanes_left(D_HEAD)
    zero = jnp.zeros_like(rows)
    return jnp.concatenate([jnp.where(left, rows, zero), jnp.where(left, zero, rows)], axis=0)


def seat_of(upper, core, place):
    lower_seat = jnp.where(core == 0, SEATS[0][0][place], SEATS[0][1][place])
    upper_seat = jnp.where(core == 0, SEATS[1][0][place], SEATS[1][1][place])
    return jnp.where(upper == 0, lower_seat, upper_seat)


def kernel(
    query_ref,
    key_ref,
    value_ref,
    gate_ref,
    rates_ref,
    first_ref,
    first_bias_ref,
    second_ref,
    second_bias_ref,
    gain_ref,
    shift_ref,
    out_ref,
    gathered,
    packed,
    rates_out,
    rates_in,
    tokens,
    blocks_out,
    returned,
    relay_out,
    landed,
    kept_rows,
    bd_key,
    turned_query,
    rate_rows,
    target_rows,
    causal,
    halves,
    state_one,
    bias_one,
    state_two,
    second_hist,
    bias_two,
    gain_rows,
    shift_rows,
    slope_ref,
    dual_base,
    dual_act_ref,
    act_ref,
    grad_two_ref,
    grad_one_ref,
    within_ref,
    read_ref,
    attend_ref,
    send_a,
    recv_a,
    send_b,
    recv_b,
    send_r,
    recv_r,
    send_c,
    recv_c,
    send_d,
    recv_d,
):
    head = lax.axis_index("head")
    seq = lax.axis_index("seq")
    core = lax.rem(head, 2)
    upper = head // NEAR
    near = lax.rem(head, NEAR)
    own_mini = 2 * seq + upper
    seats = [seat_of(upper, core, place) for place in range(HEADS_LOCAL)]
    seated = jnp.logical_or(seq == seats[0], jnp.logical_or(seq == seats[1], seq == seats[2]))
    my_place = jnp.where(seq == seats[1], 1, 0) + jnp.where(seq == seats[2], 2, 0)
    my_slot = HEADS_LOCAL * core + my_place
    my_near = head // 2
    own_source = jnp.logical_and(seated, near == my_near)

    targets = [
        (
            2 * near + slot // HEADS_LOCAL,
            seat_of(near // 4, slot // HEADS_LOCAL, slot % HEADS_LOCAL),
        )
        for slot in range(HEADS_NEAR)
    ]

    def other(device):
        return jnp.logical_or(device[0] != head, device[1] != seq)

    def neighbour(step):
        return lax.rem(near + step, NEAR)

    barrier = pltpu.get_barrier_semaphore()

    def greet(device):
        pl.semaphore_signal(barrier, inc=1, device_id=device, device_id_type=MESH)

    @pl.when(seated)
    def _():
        @pl.loop(0, STEPS)
        def _(mini):
            device = (lax.rem(mini, 2) * NEAR + my_near, mini // 2)

            @pl.when(other(device))
            def _():
                greet(device)

        @pl.loop(1, CHAIN)
        def _(step):
            greet((head, lax.rem(seq + step, CHAIN)))

    for device in targets:

        @pl.when(other(device))
        def _():
            greet(device)

    @pl.loop(1, NEAR)
    def _(step):
        greet((upper * NEAR + neighbour(step), seq))

    left_lanes = lanes_left(MINI)
    for place in range(HEADS_LOCAL):
        row = jnp.broadcast_to(rates_ref[place : place + 1], (8, LANES))
        turned_row = pltpu.roll(row, D_HEAD, 1)
        rates_out[place, 0] = jnp.where(left_lanes[:8], row, turned_row)
        rates_out[place, 1] = jnp.where(left_lanes[:8], turned_row, row)

    expected = NEAR - 1 + HEADS_NEAR + HEADS_LOCAL
    expected = expected + jnp.where(seated, STEPS - 1, 0) - jnp.where(own_source, 2, 0)
    pl.semaphore_wait(barrier, expected)

    sources = (query_ref, key_ref, value_ref)

    def wide(index):
        return pl.ds(pl.multiple_of(index * WIDE, LANES), WIDE)

    def rows_of(index):
        return pl.ds(pl.multiple_of(index * 8, 8), 8)

    def exchange_copy(array, step):
        target = neighbour(step)
        return pltpu.make_async_remote_copy(
            src_ref=sources[array].at[:, wide(target)],
            dst_ref=gathered.at[array, rows_of(near)],
            send_sem=send_a.at[array],
            recv_sem=recv_a.at[array],
            device_id=(upper * NEAR + target, seq),
            device_id_type=MESH,
        )

    def own_exchange(array):
        return pltpu.make_async_copy(
            sources[array].at[:, wide(near)], gathered.at[array, rows_of(near)], recv_a.at[array]
        )

    @pl.loop(1, NEAR)
    def _(step):
        for array in range(3):
            exchange_copy(array, step).start()

    for array in range(3):
        own_exchange(array).start()

    def rates_copy(place):
        return pltpu.make_async_remote_copy(
            src_ref=rates_out.at[place],
            dst_ref=rates_in.at[pl.ds(2 * seq, 2)],
            send_sem=send_r.at[place],
            recv_sem=recv_r.at[seq],
            device_id=(head, seats[place]),
            device_id_type=MESH,
        )

    for place in range(HEADS_LOCAL):

        @pl.when(seq != seats[place])
        def _():
            rates_copy(place).start()

    for array in range(3):
        pltpu.make_async_remote_copy(
            src_ref=gathered.at[array],
            dst_ref=gathered.at[array],
            send_sem=send_a.at[array],
            recv_sem=recv_a.at[array],
            device_id=(upper * NEAR + neighbour(1), seq),
            device_id_type=MESH,
        ).wait_recv()

    def relay_copy(slot):
        return pltpu.make_async_remote_copy(
            src_ref=packed.at[slot],
            dst_ref=tokens.at[own_mini],
            send_sem=send_b.at[slot],
            recv_sem=recv_b.at[own_mini],
            device_id=targets[slot],
            device_id_type=MESH,
        )

    for tile in range(HEADS_NEAR // 2):
        columns = slice(tile * LANES, (tile + 1) * LANES)
        queries, keys, values = [gathered[array, :, columns].astype(F32) for array in range(3)]
        queries_turned, keys_turned, values_turned = [
            pltpu.roll(rows, D_HEAD, 1) for rows in (queries, keys, values)
        ]
        first_keys = jnp.where(left_lanes, keys, values_turned)
        second_keys = jnp.where(left_lanes, keys_turned, values)
        half = MINI // 2
        first_queries = jnp.where(left_lanes[:half], queries[:half], queries_turned[half:])
        second_queries = jnp.where(left_lanes[:half], queries_turned[:half], queries[half:])
        packed[2 * tile, :MINI] = first_keys.astype(BF16)
        packed[2 * tile, MINI:] = first_queries.astype(BF16)
        packed[2 * tile + 1, :MINI] = second_keys.astype(BF16)
        packed[2 * tile + 1, MINI:] = second_queries.astype(BF16)

    pl.delay(jnp.minimum(own_mini, STEPS - 1 - own_mini) * SPACING_NS)

    for slot in range(HEADS_NEAR):

        @pl.when(other(targets[slot]))
        def _():
            relay_copy(slot).start()

    @pl.when(seated)
    def _():
        @pl.when(own_source)
        def _():
            tokens[own_mini] = packed[my_slot]

        rates_in[pl.ds(2 * seq, 2)] = rates_out[my_place]

        row = lax.broadcasted_iota(jnp.int32, (LANES, LANES), 0)
        col = lax.broadcasted_iota(jnp.int32, (LANES, LANES), 1)
        ahead = jnp.logical_and(jnp.logical_and(row < 64, col < 64), row <= col)
        back = jnp.logical_and(jnp.logical_and(row >= 64, col >= 64), row >= col)
        causal[...] = jnp.where(jnp.logical_or(ahead, back), 1.0, 0.0)
        halves[...] = jnp.where((row < 64) == (col < 64), 1.0, 0.0)

        first = first_ref[my_place]
        both = jnp.concatenate([first, first], axis=0)
        state_one[...] = both.T
        second = second_ref[my_place]
        second = second - jnp.mean(second, axis=0, keepdims=True)
        doubled = jnp.concatenate([second, second], axis=0)
        state_two[...] = doubled.T
        second_hist[0] = doubled.astype(BF16)

        def spread_column(row_values, length):
            return jnp.broadcast_to(row_values, (LANES, length)).T

        bias_one[...] = spread_column(first_bias_ref[pl.ds(my_place, 1), :], INNER)
        second_bias = second_bias_ref[pl.ds(my_place, 1), :]
        second_bias = second_bias - jnp.mean(second_bias, axis=1, keepdims=True)
        bias_two[0] = spread_column(second_bias, D_HEAD)
        gain_rows[...] = spread_column(gain_ref[pl.ds(my_place, 1), :], D_HEAD)
        shift_rows[...] = spread_column(shift_ref[pl.ds(my_place, 1), :], D_HEAD)

        def await_step(step):
            for mini in (step, STEPS - 1 - step):

                @pl.when(jnp.logical_not(jnp.logical_and(own_source, mini == own_mini)))
                def _():
                    pltpu.make_async_remote_copy(
                        src_ref=packed.at[0],
                        dst_ref=tokens.at[mini],
                        send_sem=send_b.at[0],
                        recv_sem=recv_b.at[mini],
                        device_id=(lax.rem(mini, 2) * NEAR + my_near, mini // 2),
                        device_id_type=MESH,
                    ).wait_recv()

        def await_rates(block):
            @pl.when(block != seq)
            def _():
                pltpu.make_async_remote_copy(
                    src_ref=rates_out.at[0],
                    dst_ref=rates_in.at[pl.ds(2 * block, 2)],
                    send_sem=send_r.at[0],
                    recv_sem=recv_r.at[block],
                    device_id=(head, block),
                    device_id_type=MESH,
                ).wait_recv()

        def load_step(step):
            back = STEPS - 1 - step
            kv_f = tokens[step, :MINI]
            kv_b = tokens[back, :MINI]
            left = lanes_left(MINI)
            keys_back = pltpu.roll(kv_b.astype(F32), D_HEAD, 1)
            keys_bd = jnp.concatenate(
                [jnp.where(left, kv_f.astype(F32), 0.0), jnp.where(left, 0.0, keys_back)], axis=0
            ).astype(BF16)
            pieces = []
            for mini in (step, back):
                pair = tokens[mini, MINI:].astype(F32)
                pieces += [pair, pltpu.roll(pair, D_HEAD, 1)]
            kv_turned = jnp.concatenate([kv_f, kv_b], axis=0).T.astype(F32)
            queries = jnp.concatenate(pieces, axis=0).astype(BF16).T.astype(F32)[:D_HEAD]
            target = kv_turned[D_HEAD:] - kv_turned[:D_HEAD]
            rate = jnp.where(left[:8], rates_in[step], rates_in[back])
            keys_turned = spread_halves(kv_turned[:D_HEAD]).astype(BF16)
            queries_turned = spread_halves(queries).astype(BF16)
            return (keys_bd, keys_turned, queries_turned, target, rate)

        def store_step(loaded):
            bd_key[...] = loaded[0]
            turned_query[...] = loaded[2]
            target_rows[...] = gain_rows[...] * (shift_rows[...] - loaded[3])
            rate_rows[...] = loaded[4]

        def finish(step, dual_two):
            mean = row_mean(dual_two)
            spread = lax.rsqrt(row_mean(dual_two * dual_two) - mean * mean + EPS)
            fitted = gain_rows[...] * ((dual_two - mean) * spread) + shift_rows[...]
            kept_rows[step] = fitted
            total = fitted + pltpu.roll(kept_rows[STEPS - 1 - step], D_HEAD, 1)
            at_left = lax.rem(my_slot, 2) == 0
            total = jnp.concatenate(
                [jnp.where(at_left, total, 0.0), jnp.where(at_left, 0.0, total)], axis=0
            )
            turned = total.astype(BF16).T
            blocks_out[step] = turned[:MINI]
            blocks_out[STEPS - 1 - step] = turned[MINI:]

        def slot_of(step):
            return lax.rem(step, HISTORY)

        def attend_dual(step):
            slot = slot_of(step)
            dual_act = dual_act_ref[lax.rem(step, 2)]
            mask = causal[...]
            read = dot(second_hist[slot], dual_act, (1, 0))
            attend = dot(act_ref[slot].T, dual_act, (1, 0))
            return (own_half(read) + bias_two[slot], (attend * mask + mask).astype(BF16))

        half = INNER // 2
        row_halves = (slice(0, half), slice(half, INNER))

        def widen(grad_one, within, base, bias, ones_bf):
            sums = jnp.concatenate([within, ones_bf], axis=1)
            falls = [dot(grad_one[rows], sums, (1, 0)) for rows in row_halves]
            acts = [
                gelu(base[rows] - fall[:, :LANES]).astype(BF16)
                for rows, fall in zip(row_halves, falls)
            ]
            biases = [bias[rows] - fall[:, LANES:] for rows, fall in zip(row_halves, falls)]
            return (acts, biases)

        def advance(step):
            slot = slot_of(step)
            before = step + HISTORY - 2
            act = act_ref[slot]
            second_turned = second_hist[slot]
            target = target_rows[...]
            gain = gain_rows[...]
            gain_sq = gain * gain
            rate = rate_rows[0:1]
            bias_two_now = bias_two[slot]
            ones_bd = halves[...]
            ones_bf = ones_bd.astype(BF16)
            mask = causal[...]

            pre_two = (
                jnp.where(
                    lanes_left(D_HEAD),
                    dot(second_turned[:D_HEAD], act, (1, 0)),
                    dot(second_turned[D_HEAD:], act, (1, 0)),
                )
                + bias_two_now
            )

            last_read = read_ref[...]
            last_fall = dot(grad_two_ref[slot_of(step + HISTORY - 3)], attend_ref[...], (1, 0))
            dual_acts, biases = widen(
                grad_one_ref[...], within_ref[...], dual_base[...], bias_one[...], ones_bf
            )

            later = jnp.minimum(step + 1, STEPS - 1)
            loaded = load_step(later)
            keys_bd = bd_key[...]
            queries_turned = turned_query[...]
            state_one_now = state_one[...]
            high = state_one_now.astype(BF16)
            low = (state_one_now - high.astype(F32)).astype(BF16)
            reads = jnp.concatenate([loaded[1], queries_turned], axis=1)
            reads = jnp.concatenate([reads, reads], axis=0)
            within_both = dot(
                jnp.concatenate([keys_bd, jnp.zeros_like(keys_bd)], axis=1), reads, (1, 0)
            )
            between = (within_both[:, :LANES] + ones_bd).astype(BF16)
            within = (within_both[:, LANES:] * mask + mask).astype(BF16)

            scaled = gain_sq * pre_two
            mean = row_mean(pre_two)
            sum_scaled = row_mean(scaled)
            sum_square = row_mean(pre_two * pre_two)
            sum_scaled_sq = row_mean(scaled * pre_two)
            sum_target = row_mean(target * pre_two)
            mean_gain = row_mean(gain_sq)
            mean_target = row_mean(target)
            inverse = lax.rsqrt(sum_square - mean * mean + EPS)
            centred_scaled = sum_scaled - mean * mean_gain
            mean_a = inverse * centred_scaled + mean_target
            mean_an = inverse * (
                inverse * (sum_scaled_sq - mean * (sum_scaled + centred_scaled))
                + (sum_target - mean * mean_target)
            )
            weight = inverse * rate
            grad_two = (
                (pre_two - mean) * (inverse * gain_sq - inverse * mean_an) + (target - mean_a)
            ) * weight
            grad_two = grad_two.astype(BF16)
            grad_two_bd = spread_halves(grad_two)
            state_two_now = state_two[...]
            state_two_bf = state_two_now.astype(BF16)
            grads_one = [
                (dot(state_two_bf[rows], grad_two_bd, (1, 0)) * slope_ref[rows, :]).astype(BF16)
                for rows in row_halves
            ]

            finish(jnp.maximum(step - 3, 0), last_read - last_fall)

            state_two_new = state_two_now - dot(act, grad_two_bd.T, (1, 0))
            bias_two_new = bias_two_now - dot(grad_two, ones_bf, (1, 0))
            dual_read, attend = attend_dual(before)
            read_ref[...] = dual_read
            attend_ref[...] = attend

            seen = dot(jnp.concatenate([high, low], axis=1), reads, (1, 0))
            moves = jnp.concatenate([between, keys_bd], axis=1)
            next_slot = slot_of(step + 1)
            for part in range(2):
                rows = row_halves[part]
                fall = dot(grads_one[part], moves, (1, 0))
                state_one[rows, :] = state_one_now[rows] - fall[:, LANES:]
                pre_one = seen[rows, :LANES] + biases[part] - fall[:, :LANES]
                act_next, slope_next = gelu_and_slope(pre_one)
                act_ref[next_slot, rows, :] = act_next.astype(BF16)
                slope_ref[rows, :] = slope_next
                dual_base[rows, :] = seen[rows, LANES:] + biases[part]
                bias_one[rows, :] = biases[part]
                grad_one_ref[rows, :] = grads_one[part]
                dual_act_ref[lax.rem(step + 1, 2), rows, :] = dual_acts[part]

            state_two[...] = state_two_new
            second_hist[next_slot] = state_two_new.astype(BF16).T
            bias_two[next_slot] = bias_two_new
            grad_two_ref[slot] = grad_two
            within_ref[...] = within
            store_step(loaded)

        def emit(step, read, attend):
            finish(step, read - dot(grad_two_ref[slot_of(step)], attend, (1, 0)))
            give_back(step)
            give_back(STEPS - 1 - step)

        def return_copy(mini):
            return pltpu.make_async_remote_copy(
                src_ref=blocks_out.at[mini],
                dst_ref=returned.at[my_slot],
                send_sem=send_c.at[mini],
                recv_sem=recv_c.at[my_slot],
                device_id=(lax.rem(mini, 2) * NEAR + my_near, mini // 2),
                device_id_type=MESH,
            )

        def is_own(mini):
            return jnp.logical_and(own_source, mini == own_mini)

        def give_back(mini):
            @pl.when(jnp.logical_not(is_own(mini)))
            def _():
                return_copy(mini).start()

            @pl.when(is_own(mini))
            def _():
                returned[my_slot] = blocks_out[mini]

        await_rates(0)
        await_rates(CHAIN - 1)
        await_step(0)
        begun = load_step(0)
        store_step(begun)
        high = state_one[...].astype(BF16)
        low = (state_one[...] - high.astype(F32)).astype(BF16)
        act, slope = gelu_and_slope(
            dot(high, begun[1], (1, 0)) + dot(low, begun[1], (1, 0)) + bias_one[...]
        )
        act_ref[0] = act.astype(BF16)
        slope_ref[...] = slope
        grad_one_ref[...] = jnp.zeros_like(grad_one_ref)
        within_ref[...] = jnp.zeros_like(within_ref)

        @pl.loop(0, STEPS)
        def _(step):
            later = step + 1

            @pl.when(later < STEPS // 2)
            def _():
                await_step(later)

                @pl.when(lax.rem(later, 2) == 0)
                def _():
                    await_rates(later // 2)
                    await_rates(CHAIN - 1 - later // 2)

            advance(step)
            done = step - 3

            @pl.when(done >= STEPS // 2)
            def _():
                give_back(done)
                give_back(STEPS - 1 - done)

        last = STEPS - 1
        emit(last - 2, read_ref[...], attend_ref[...])
        dual_acts, _ = widen(
            grad_one_ref[...],
            within_ref[...],
            dual_base[...],
            bias_one[...],
            halves[...].astype(BF16),
        )
        for part in range(2):
            dual_act_ref[last % 2, row_halves[part], :] = dual_acts[part]
        for step in (last - 1, last):
            emit(step, *attend_dual(step))

    for slot in range(HEADS_NEAR):

        @pl.when(other(targets[slot]))
        def _():
            pltpu.make_async_remote_copy(
                src_ref=blocks_out.at[0],
                dst_ref=returned.at[slot],
                send_sem=send_c.at[0],
                recv_sem=recv_c.at[slot],
                device_id=targets[slot],
                device_id_type=MESH,
            ).wait_recv()

    for tile in range(HEADS_NEAR // 2):
        columns = slice(tile * LANES, (tile + 1) * LANES)
        relay_out[:, columns] = jnp.where(left_lanes, returned[2 * tile], returned[2 * tile + 1])

    def spread_copy(step):
        target = neighbour(step)
        return pltpu.make_async_remote_copy(
            src_ref=relay_out.at[rows_of(target)],
            dst_ref=landed.at[:, wide(near)],
            send_sem=send_d.at[0],
            recv_sem=recv_d.at[0],
            device_id=(upper * NEAR + target, seq),
            device_id_type=MESH,
        )

    @pl.loop(1, NEAR)
    def _(step):
        spread_copy(step).start()

    pltpu.make_async_copy(
        relay_out.at[rows_of(near)], landed.at[:, wide(near)], recv_d.at[0]
    ).start()
    pltpu.make_async_remote_copy(
        src_ref=landed,
        dst_ref=landed,
        send_sem=send_d.at[0],
        recv_sem=recv_d.at[0],
        device_id=(upper * NEAR + neighbour(1), seq),
        device_id_type=MESH,
    ).wait_recv()

    for tile in range(TILES):
        columns = slice(tile * LANES, (tile + 1) * LANES)
        out_ref[:, columns] = (
            gate_ref[:, columns].astype(F32) * landed[:, columns].astype(F32)
        ).astype(BF16)

    sent = pl.ds(0, (NEAR - 1) * WIDE)
    for array in range(3):
        pltpu.make_async_remote_copy(
            src_ref=sources[array].at[:, sent],
            dst_ref=sources[array].at[:, sent],
            send_sem=send_a.at[array],
            recv_sem=recv_a.at[array],
            device_id=(upper * NEAR + neighbour(1), seq),
            device_id_type=MESH,
        ).wait_send()
    pltpu.make_async_remote_copy(
        src_ref=relay_out.at[pl.ds(0, 8 * (NEAR - 1))],
        dst_ref=relay_out.at[pl.ds(0, 8 * (NEAR - 1))],
        send_sem=send_d.at[0],
        recv_sem=recv_d.at[0],
        device_id=(upper * NEAR + neighbour(1), seq),
        device_id_type=MESH,
    ).wait_send()

    for place in range(HEADS_LOCAL):

        @pl.when(seq != seats[place])
        def _():
            rates_copy(place).wait_send()

    for slot in range(HEADS_NEAR):

        @pl.when(other(targets[slot]))
        def _():
            relay_copy(slot).wait_send()

    @pl.when(seated)
    def _():
        @pl.loop(0, STEPS)
        def _(mini):
            device = (lax.rem(mini, 2) * NEAR + my_near, mini // 2)

            @pl.when(other(device))
            def _():
                pltpu.make_async_remote_copy(
                    src_ref=blocks_out.at[mini],
                    dst_ref=returned.at[my_slot],
                    send_sem=send_c.at[mini],
                    recv_sem=recv_c.at[my_slot],
                    device_id=device,
                    device_id_type=MESH,
                ).wait_send()


def local(*arrays):
    arrays = list(arrays)
    arrays[4] = arrays[4].T
    arrays[7] = jnp.swapaxes(arrays[7], 1, 2)
    vmem = pl.BlockSpec(memory_space=pltpu.VMEM)
    dma = pltpu.SemaphoreType.DMA
    return pl.pallas_call(
        kernel,
        out_shape=jax.ShapeDtypeStruct((8, TILES * LANES), BF16),
        in_specs=[vmem] * len(arrays),
        out_specs=vmem,
        scratch_shapes=[
            pltpu.VMEM((3, MINI, WIDE), BF16),
            pltpu.VMEM((HEADS_NEAR, PACKED, LANES), BF16),
            pltpu.VMEM((HEADS_LOCAL, 2, 8, LANES), F32),
            pltpu.VMEM((STEPS, 8, LANES), F32),
            pltpu.VMEM((STEPS, PACKED, LANES), BF16),
            pltpu.VMEM((STEPS, MINI, LANES), BF16),
            pltpu.VMEM((HEADS_NEAR, MINI, LANES), BF16),
            pltpu.VMEM((MINI, WIDE), BF16),
            pltpu.VMEM((8, TILES * LANES), BF16),
            pltpu.VMEM((STEPS, D_HEAD, LANES), F32),
            pltpu.VMEM((LANES, LANES), BF16),
            pltpu.VMEM((LANES, LANES), BF16),
            pltpu.VMEM((8, LANES), F32),
            pltpu.VMEM((D_HEAD, LANES), F32),
            pltpu.VMEM((LANES, LANES), F32),
            pltpu.VMEM((LANES, LANES), F32),
            pltpu.VMEM((INNER, LANES), F32),
            pltpu.VMEM((INNER, LANES), F32),
            pltpu.VMEM((INNER, LANES), F32),
            pltpu.VMEM((HISTORY, LANES, INNER), BF16),
            pltpu.VMEM((HISTORY, D_HEAD, LANES), F32),
            pltpu.VMEM((D_HEAD, LANES), F32),
            pltpu.VMEM((D_HEAD, LANES), F32),
            pltpu.VMEM((INNER, LANES), F32),
            pltpu.VMEM((INNER, LANES), F32),
            pltpu.VMEM((2, INNER, LANES), BF16),
            pltpu.VMEM((HISTORY, INNER, LANES), BF16),
            pltpu.VMEM((HISTORY, D_HEAD, LANES), BF16),
            pltpu.VMEM((INNER, LANES), BF16),
            pltpu.VMEM((LANES, LANES), BF16),
            pltpu.VMEM((D_HEAD, LANES), F32),
            pltpu.VMEM((LANES, LANES), BF16),
            dma((3,)),
            dma((3,)),
            dma((HEADS_NEAR,)),
            dma((STEPS,)),
            dma((HEADS_LOCAL,)),
            dma((CHAIN,)),
            dma((STEPS,)),
            dma((HEADS_NEAR,)),
            dma((1,)),
            dma((1,)),
        ],
        compiler_params=pltpu.CompilerParams(collective_id=0, has_side_effects=True),
    )(*arrays)


def solution(mesh):
    rows = P(("seq", "head"), None)
    in_specs = (
        rows,
        rows,
        rows,
        rows,
        P("seq", "head"),
        P("head", None, None),
        P("head", None),
        P("head", None, None),
        P("head", None),
        P("head", None),
        P("head", None),
    )
    return jax.shard_map(local, mesh=mesh, in_specs=in_specs, out_specs=rows, check_vma=False)
```

```python
import functools

import jax
import jax.numpy as jnp
from jax import lax
from jax.experimental import pallas as pl
from jax.experimental.pallas import tpu as pltpu
from jax.sharding import PartitionSpec as P

D_HEAD = 64
INNER = 256
MINI = 64
STEPS = 64
LANES = 128
NEAR = 8
CHAIN = 32
HEADS_LOCAL = 3
HEADS_NEAR = 6
WIDE = HEADS_NEAR * D_HEAD
TILES = 24

EPS = 1e-06
ROOT = 0.7978845608028654
CUBE = 0.044715
MESH = pl.DeviceIdType.MESH
F32 = jnp.float32
BF16 = jnp.bfloat16

PACKED = MINI + MINI // 2
HISTORY = 4
SPACING_NS = 700

SEATS = (((1, 7, 12), (2, 4, 15)), ((29, 26, 16), (30, 25, 19)))


def dot(left, right, dims):
    return lax.dot_general(
        left, right, (((dims[0],), (dims[1],)), ((), ())), preferred_element_type=F32
    )


def gelu(values):
    squared = values * values
    tanh_term = jnp.tanh(values * (ROOT + (ROOT * CUBE) * squared))
    return values * (0.5 + 0.5 * tanh_term)


def gelu_and_slope(values):
    squared = values * values
    tanh_term = jnp.tanh(values * (ROOT + (ROOT * CUBE) * squared))
    half = 0.5 + 0.5 * tanh_term
    slope = half + values * (half * (1.0 - tanh_term)) * (ROOT + (3.0 * ROOT * CUBE) * squared)
    return (values * half, slope)


def row_mean(values):
    rows = values.shape[0]
    while rows > 8:
        rows //= 2
        values = values[:rows] + values[rows:]
    return jnp.sum(values, axis=0, keepdims=True) * (1.0 / D_HEAD)


def lanes_left(rows):
    return lax.broadcasted_iota(jnp.int32, (rows, LANES), 1) < D_HEAD


def own_half(stacked):
    return jnp.where(lanes_left(D_HEAD), stacked[:D_HEAD], stacked[D_HEAD:])


def spread_halves(rows):
    left = lanes_left(D_HEAD)
    zero = jnp.zeros_like(rows)
    return jnp.concatenate([jnp.where(left, rows, zero), jnp.where(left, zero, rows)], axis=0)


def seat_of(upper, core, place):
    lower_seat = jnp.where(core == 0, SEATS[0][0][place], SEATS[0][1][place])
    upper_seat = jnp.where(core == 0, SEATS[1][0][place], SEATS[1][1][place])
    return jnp.where(upper == 0, lower_seat, upper_seat)


def kernel(
    query_ref,
    key_ref,
    value_ref,
    gate_far,
    rates_far,
    first_far,
    first_bias_far,
    second_far,
    second_bias_far,
    gain_far,
    shift_far,
    out_ref,
    gate_ref,
    rates_ref,
    first_ref,
    first_bias_ref,
    second_ref,
    second_bias_ref,
    gain_ref,
    shift_ref,
    gathered,
    packed,
    rates_out,
    rates_in,
    tokens,
    blocks_out,
    returned,
    relay_out,
    landed,
    kept_rows,
    bd_key,
    turned_query,
    rate_rows,
    target_rows,
    causal,
    halves,
    state_one,
    bias_one,
    state_two,
    second_hist,
    bias_two,
    gain_rows,
    shift_rows,
    slope_ref,
    dual_base,
    dual_act_ref,
    act_ref,
    grad_two_ref,
    grad_one_ref,
    within_ref,
    read_ref,
    attend_ref,
    load_sem,
    send_a,
    recv_a,
    send_b,
    recv_b,
    send_r,
    recv_r,
    send_c,
    recv_c,
    send_d,
    recv_d,
):
    fetches = [
        pltpu.make_async_copy(far, here, load_sem.at[place])
        for place, (far, here) in enumerate(
            (
                (rates_far, rates_ref),
                (gate_far, gate_ref),
                (first_far, first_ref),
                (first_bias_far, first_bias_ref),
                (second_far, second_ref),
                (second_bias_far, second_bias_ref),
                (gain_far, gain_ref),
                (shift_far, shift_ref),
            )
        )
    ]
    for fetch in fetches:
        fetch.start()

    head = lax.axis_index("head")
    seq = lax.axis_index("seq")
    core = lax.rem(head, 2)
    upper = head // NEAR
    near = lax.rem(head, NEAR)
    own_mini = 2 * seq + upper
    seats = [seat_of(upper, core, place) for place in range(HEADS_LOCAL)]
    seated = jnp.logical_or(seq == seats[0], jnp.logical_or(seq == seats[1], seq == seats[2]))
    my_place = jnp.where(seq == seats[1], 1, 0) + jnp.where(seq == seats[2], 2, 0)
    my_slot = HEADS_LOCAL * core + my_place
    my_near = head // 2
    own_source = jnp.logical_and(seated, near == my_near)

    targets = [
        (
            2 * near + slot // HEADS_LOCAL,
            seat_of(near // 4, slot // HEADS_LOCAL, slot % HEADS_LOCAL),
        )
        for slot in range(HEADS_NEAR)
    ]

    def other(device):
        return jnp.logical_or(device[0] != head, device[1] != seq)

    def neighbour(step):
        return lax.rem(near + step, NEAR)

    barrier = pltpu.get_barrier_semaphore()

    def greet(device):
        pl.semaphore_signal(barrier, inc=1, device_id=device, device_id_type=MESH)

    @pl.when(seated)
    def _():
        @pl.loop(0, STEPS)
        def _(mini):
            device = (lax.rem(mini, 2) * NEAR + my_near, mini // 2)

            @pl.when(other(device))
            def _():
                greet(device)

        @pl.loop(1, CHAIN)
        def _(step):
            greet((head, lax.rem(seq + step, CHAIN)))

    for device in targets:

        @pl.when(other(device))
        def _():
            greet(device)

    @pl.loop(1, NEAR)
    def _(step):
        greet((upper * NEAR + neighbour(step), seq))

    fetches[0].wait()
    left_lanes = lanes_left(MINI)
    for place in range(HEADS_LOCAL):
        row = jnp.broadcast_to(rates_ref[place : place + 1], (8, LANES))
        turned_row = pltpu.roll(row, D_HEAD, 1)
        rates_out[place, 0] = jnp.where(left_lanes[:8], row, turned_row)
        rates_out[place, 1] = jnp.where(left_lanes[:8], turned_row, row)

    expected = NEAR - 1 + HEADS_NEAR + HEADS_LOCAL
    expected = expected + jnp.where(seated, STEPS - 1, 0) - jnp.where(own_source, 2, 0)
    pl.semaphore_wait(barrier, expected)

    sources = (query_ref, key_ref, value_ref)

    def wide(index):
        return pl.ds(pl.multiple_of(index * WIDE, LANES), WIDE)

    def rows_of(index):
        return pl.ds(pl.multiple_of(index * 8, 8), 8)

    def exchange_copy(array, step):
        target = neighbour(step)
        return pltpu.make_async_remote_copy(
            src_ref=sources[array].at[:, wide(target)],
            dst_ref=gathered.at[array, rows_of(near)],
            send_sem=send_a.at[array],
            recv_sem=recv_a.at[array],
            device_id=(upper * NEAR + target, seq),
            device_id_type=MESH,
        )

    def own_exchange(array):
        return pltpu.make_async_copy(
            sources[array].at[:, wide(near)], gathered.at[array, rows_of(near)], recv_a.at[array]
        )

    @pl.loop(1, NEAR)
    def _(step):
        for array in range(3):
            exchange_copy(array, step).start()

    for array in range(3):
        own_exchange(array).start()

    def rates_copy(place):
        return pltpu.make_async_remote_copy(
            src_ref=rates_out.at[place],
            dst_ref=rates_in.at[pl.ds(2 * seq, 2)],
            send_sem=send_r.at[place],
            recv_sem=recv_r.at[seq],
            device_id=(head, seats[place]),
            device_id_type=MESH,
        )

    for place in range(HEADS_LOCAL):

        @pl.when(seq != seats[place])
        def _():
            rates_copy(place).start()

    for array in range(3):
        pltpu.make_async_remote_copy(
            src_ref=gathered.at[array],
            dst_ref=gathered.at[array],
            send_sem=send_a.at[array],
            recv_sem=recv_a.at[array],
            device_id=(upper * NEAR + neighbour(1), seq),
            device_id_type=MESH,
        ).wait_recv()

    def relay_copy(slot):
        return pltpu.make_async_remote_copy(
            src_ref=packed.at[slot],
            dst_ref=tokens.at[own_mini],
            send_sem=send_b.at[slot],
            recv_sem=recv_b.at[own_mini],
            device_id=targets[slot],
            device_id_type=MESH,
        )

    for tile in range(HEADS_NEAR // 2):
        columns = slice(tile * LANES, (tile + 1) * LANES)
        queries, keys, values = [gathered[array, :, columns].astype(F32) for array in range(3)]
        queries_turned, keys_turned, values_turned = [
            pltpu.roll(rows, D_HEAD, 1) for rows in (queries, keys, values)
        ]
        first_keys = jnp.where(left_lanes, keys, values_turned)
        second_keys = jnp.where(left_lanes, keys_turned, values)
        half = MINI // 2
        first_queries = jnp.where(left_lanes[:half], queries[:half], queries_turned[half:])
        second_queries = jnp.where(left_lanes[:half], queries_turned[:half], queries[half:])
        packed[2 * tile, :MINI] = first_keys.astype(BF16)
        packed[2 * tile, MINI:] = first_queries.astype(BF16)
        packed[2 * tile + 1, :MINI] = second_keys.astype(BF16)
        packed[2 * tile + 1, MINI:] = second_queries.astype(BF16)

    late = jnp.minimum(own_mini, STEPS - 1 - own_mini)
    pl.delay(jnp.where(seated, 0, late) * SPACING_NS)

    for slot in range(HEADS_NEAR):

        @pl.when(other(targets[slot]))
        def _():
            relay_copy(slot).start()

    for fetch in fetches[1:]:
        fetch.wait()

    @pl.when(seated)
    def _():
        @pl.when(own_source)
        def _():
            tokens[own_mini] = packed[my_slot]

        rates_in[pl.ds(2 * seq, 2)] = rates_out[my_place]

        row = lax.broadcasted_iota(jnp.int32, (LANES, LANES), 0)
        col = lax.broadcasted_iota(jnp.int32, (LANES, LANES), 1)
        ahead = jnp.logical_and(jnp.logical_and(row < 64, col < 64), row <= col)
        back = jnp.logical_and(jnp.logical_and(row >= 64, col >= 64), row >= col)
        causal[...] = jnp.where(jnp.logical_or(ahead, back), 1.0, 0.0)
        halves[...] = jnp.where((row < 64) == (col < 64), 1.0, 0.0)

        first = first_ref[my_place]
        both = jnp.concatenate([first, first], axis=0)
        state_one[...] = both.T
        second = second_ref[my_place]
        second = second - jnp.mean(second, axis=0, keepdims=True)
        doubled = jnp.concatenate([second, second], axis=0)
        state_two[...] = doubled.T
        second_hist[0] = doubled.astype(BF16)

        def spread_column(row_values, length):
            return jnp.broadcast_to(row_values, (LANES, length)).T

        bias_one[...] = spread_column(first_bias_ref[pl.ds(my_place, 1), :], INNER)
        second_bias = second_bias_ref[pl.ds(my_place, 1), :]
        second_bias = second_bias - jnp.mean(second_bias, axis=1, keepdims=True)
        bias_two[0] = spread_column(second_bias, D_HEAD)
        gain_rows[...] = spread_column(gain_ref[pl.ds(my_place, 1), :], D_HEAD)
        shift_rows[...] = spread_column(shift_ref[pl.ds(my_place, 1), :], D_HEAD)

        def await_step(step):
            for mini in (step, STEPS - 1 - step):

                @pl.when(jnp.logical_not(jnp.logical_and(own_source, mini == own_mini)))
                def _():
                    pltpu.make_async_remote_copy(
                        src_ref=packed.at[0],
                        dst_ref=tokens.at[mini],
                        send_sem=send_b.at[0],
                        recv_sem=recv_b.at[mini],
                        device_id=(lax.rem(mini, 2) * NEAR + my_near, mini // 2),
                        device_id_type=MESH,
                    ).wait_recv()

        def await_rates(block):
            @pl.when(block != seq)
            def _():
                pltpu.make_async_remote_copy(
                    src_ref=rates_out.at[0],
                    dst_ref=rates_in.at[pl.ds(2 * block, 2)],
                    send_sem=send_r.at[0],
                    recv_sem=recv_r.at[block],
                    device_id=(head, block),
                    device_id_type=MESH,
                ).wait_recv()

        def load_step(step):
            back = STEPS - 1 - step
            kv_f = tokens[step, :MINI]
            kv_b = tokens[back, :MINI]
            left = lanes_left(MINI)
            keys_back = pltpu.roll(kv_b.astype(F32), D_HEAD, 1)
            keys_bd = jnp.concatenate(
                [jnp.where(left, kv_f.astype(F32), 0.0), jnp.where(left, 0.0, keys_back)], axis=0
            ).astype(BF16)
            pieces = []
            for mini in (step, back):
                pair = tokens[mini, MINI:].astype(F32)
                pieces += [pair, pltpu.roll(pair, D_HEAD, 1)]
            kv_turned = jnp.concatenate([kv_f, kv_b], axis=0).T.astype(F32)
            queries = jnp.concatenate(pieces, axis=0).astype(BF16).T.astype(F32)[:D_HEAD]
            target = kv_turned[D_HEAD:] - kv_turned[:D_HEAD]
            rate = jnp.where(left[:8], rates_in[step], rates_in[back])
            keys_turned = spread_halves(kv_turned[:D_HEAD]).astype(BF16)
            queries_turned = spread_halves(queries).astype(BF16)
            return (keys_bd, keys_turned, queries_turned, target, rate)

        def store_step(loaded):
            bd_key[...] = loaded[0]
            turned_query[...] = loaded[2]
            target_rows[...] = gain_rows[...] * (shift_rows[...] - loaded[3])
            rate_rows[...] = loaded[4]

        def finish(step, dual_two):
            mean = row_mean(dual_two)
            spread = lax.rsqrt(row_mean(dual_two * dual_two) - mean * mean + EPS)
            fitted = gain_rows[...] * ((dual_two - mean) * spread) + shift_rows[...]
            kept_rows[step] = fitted
            total = fitted + pltpu.roll(kept_rows[STEPS - 1 - step], D_HEAD, 1)
            at_left = lax.rem(my_slot, 2) == 0
            total = jnp.concatenate(
                [jnp.where(at_left, total, 0.0), jnp.where(at_left, 0.0, total)], axis=0
            )
            turned = total.astype(BF16).T
            blocks_out[step] = turned[:MINI]
            blocks_out[STEPS - 1 - step] = turned[MINI:]

        def slot_of(step):
            return lax.rem(step, HISTORY)

        def attend_dual(step):
            slot = slot_of(step)
            dual_act = dual_act_ref[lax.rem(step, 2)]
            mask = causal[...]
            read = dot(second_hist[slot], dual_act, (1, 0))
            attend = dot(act_ref[slot].T, dual_act, (1, 0))
            return (own_half(read) + bias_two[slot], (attend * mask + mask).astype(BF16))

        half = INNER // 2
        row_halves = (slice(0, half), slice(half, INNER))

        def widen(grad_one, within, base, bias, ones_bf):
            sums = jnp.concatenate([within, ones_bf], axis=1)
            falls = [dot(grad_one[rows], sums, (1, 0)) for rows in row_halves]
            acts = [
                gelu(base[rows] - fall[:, :LANES]).astype(BF16)
                for rows, fall in zip(row_halves, falls)
            ]
            biases = [bias[rows] - fall[:, LANES:] for rows, fall in zip(row_halves, falls)]
            return (acts, biases)

        def advance(step):
            slot = slot_of(step)
            before = step + HISTORY - 2
            act = act_ref[slot]
            second_turned = second_hist[slot]
            target = target_rows[...]
            gain = gain_rows[...]
            gain_sq = gain * gain
            rate = rate_rows[0:1]
            bias_two_now = bias_two[slot]
            ones_bd = halves[...]
            ones_bf = ones_bd.astype(BF16)
            mask = causal[...]

            pre_two = (
                jnp.where(
                    lanes_left(D_HEAD),
                    dot(second_turned[:D_HEAD], act, (1, 0)),
                    dot(second_turned[D_HEAD:], act, (1, 0)),
                )
                + bias_two_now
            )

            last_read = read_ref[...]
            last_fall = dot(grad_two_ref[slot_of(step + HISTORY - 3)], attend_ref[...], (1, 0))
            dual_acts, biases = widen(
                grad_one_ref[...], within_ref[...], dual_base[...], bias_one[...], ones_bf
            )

            later = jnp.minimum(step + 1, STEPS - 1)
            loaded = load_step(later)
            keys_bd = bd_key[...]
            queries_turned = turned_query[...]
            state_one_now = state_one[...]
            high = state_one_now.astype(BF16)
            low = (state_one_now - high.astype(F32)).astype(BF16)
            reads = jnp.concatenate([loaded[1], queries_turned], axis=1)
            reads = jnp.concatenate([reads, reads], axis=0)
            within_both = dot(
                jnp.concatenate([keys_bd, jnp.zeros_like(keys_bd)], axis=1), reads, (1, 0)
            )
            between = (within_both[:, :LANES] + ones_bd).astype(BF16)
            within = (within_both[:, LANES:] * mask + mask).astype(BF16)

            scaled = gain_sq * pre_two
            mean = row_mean(pre_two)
            sum_scaled = row_mean(scaled)
            sum_square = row_mean(pre_two * pre_two)
            sum_scaled_sq = row_mean(scaled * pre_two)
            sum_target = row_mean(target * pre_two)
            mean_gain = row_mean(gain_sq)
            mean_target = row_mean(target)
            inverse = lax.rsqrt(sum_square - mean * mean + EPS)
            centred_scaled = sum_scaled - mean * mean_gain
            mean_a = inverse * centred_scaled + mean_target
            mean_an = inverse * (
                inverse * (sum_scaled_sq - mean * (sum_scaled + centred_scaled))
                + (sum_target - mean * mean_target)
            )
            weight = inverse * rate
            grad_two = (
                (pre_two - mean) * (inverse * gain_sq - inverse * mean_an) + (target - mean_a)
            ) * weight
            grad_two = grad_two.astype(BF16)
            grad_two_bd = spread_halves(grad_two)
            state_two_now = state_two[...]
            state_two_bf = state_two_now.astype(BF16)
            grads_one = [
                (dot(state_two_bf[rows], grad_two_bd, (1, 0)) * slope_ref[rows, :]).astype(BF16)
                for rows in row_halves
            ]

            finish(jnp.maximum(step - 3, 0), last_read - last_fall)

            state_two_new = state_two_now - dot(act, grad_two_bd.T, (1, 0))
            bias_two_new = bias_two_now - dot(grad_two, ones_bf, (1, 0))
            dual_read, attend = attend_dual(before)
            read_ref[...] = dual_read
            attend_ref[...] = attend

            seen = dot(jnp.concatenate([high, low], axis=1), reads, (1, 0))
            moves = jnp.concatenate([between, keys_bd], axis=1)
            next_slot = slot_of(step + 1)
            for part in range(2):
                rows = row_halves[part]
                fall = dot(grads_one[part], moves, (1, 0))
                state_one[rows, :] = state_one_now[rows] - fall[:, LANES:]
                pre_one = seen[rows, :LANES] + biases[part] - fall[:, :LANES]
                act_next, slope_next = gelu_and_slope(pre_one)
                act_ref[next_slot, rows, :] = act_next.astype(BF16)
                slope_ref[rows, :] = slope_next
                dual_base[rows, :] = seen[rows, LANES:] + biases[part]
                bias_one[rows, :] = biases[part]
                grad_one_ref[rows, :] = grads_one[part]
                dual_act_ref[lax.rem(step + 1, 2), rows, :] = dual_acts[part]

            state_two[...] = state_two_new
            second_hist[next_slot] = state_two_new.astype(BF16).T
            bias_two[next_slot] = bias_two_new
            grad_two_ref[slot] = grad_two
            within_ref[...] = within
            store_step(loaded)

        def emit(step, read, attend):
            finish(step, read - dot(grad_two_ref[slot_of(step)], attend, (1, 0)))
            give_back(step)
            give_back(STEPS - 1 - step)

        def return_copy(mini):
            return pltpu.make_async_remote_copy(
                src_ref=blocks_out.at[mini],
                dst_ref=returned.at[my_slot],
                send_sem=send_c.at[mini],
                recv_sem=recv_c.at[my_slot],
                device_id=(lax.rem(mini, 2) * NEAR + my_near, mini // 2),
                device_id_type=MESH,
            )

        def is_own(mini):
            return jnp.logical_and(own_source, mini == own_mini)

        def give_back(mini):
            @pl.when(jnp.logical_not(is_own(mini)))
            def _():
                return_copy(mini).start()

            @pl.when(is_own(mini))
            def _():
                returned[my_slot] = blocks_out[mini]

        await_rates(0)
        await_rates(CHAIN - 1)
        await_step(0)
        begun = load_step(0)
        store_step(begun)
        high = state_one[...].astype(BF16)
        low = (state_one[...] - high.astype(F32)).astype(BF16)
        act, slope = gelu_and_slope(
            dot(high, begun[1], (1, 0)) + dot(low, begun[1], (1, 0)) + bias_one[...]
        )
        act_ref[0] = act.astype(BF16)
        slope_ref[...] = slope
        grad_one_ref[...] = jnp.zeros_like(grad_one_ref)
        within_ref[...] = jnp.zeros_like(within_ref)

        @pl.loop(0, STEPS)
        def _(step):
            later = step + 1

            @pl.when(later < STEPS // 2)
            def _():
                await_step(later)

                @pl.when(lax.rem(later, 2) == 0)
                def _():
                    await_rates(later // 2)
                    await_rates(CHAIN - 1 - later // 2)

            advance(step)
            done = step - 3

            @pl.when(done >= STEPS // 2)
            def _():
                give_back(done)
                give_back(STEPS - 1 - done)

        last = STEPS - 1
        emit(last - 2, read_ref[...], attend_ref[...])
        dual_acts, _ = widen(
            grad_one_ref[...],
            within_ref[...],
            dual_base[...],
            bias_one[...],
            halves[...].astype(BF16),
        )
        for part in range(2):
            dual_act_ref[last % 2, row_halves[part], :] = dual_acts[part]
        for step in (last - 1, last):
            emit(step, *attend_dual(step))

    for slot in range(HEADS_NEAR):

        @pl.when(other(targets[slot]))
        def _():
            pltpu.make_async_remote_copy(
                src_ref=blocks_out.at[0],
                dst_ref=returned.at[slot],
                send_sem=send_c.at[0],
                recv_sem=recv_c.at[slot],
                device_id=targets[slot],
                device_id_type=MESH,
            ).wait_recv()

    for tile in range(HEADS_NEAR // 2):
        columns = slice(tile * LANES, (tile + 1) * LANES)
        relay_out[:, columns] = jnp.where(left_lanes, returned[2 * tile], returned[2 * tile + 1])

    def spread_copy(step):
        target = neighbour(step)
        return pltpu.make_async_remote_copy(
            src_ref=relay_out.at[rows_of(target)],
            dst_ref=landed.at[:, wide(near)],
            send_sem=send_d.at[0],
            recv_sem=recv_d.at[0],
            device_id=(upper * NEAR + target, seq),
            device_id_type=MESH,
        )

    @pl.loop(1, NEAR)
    def _(step):
        spread_copy(step).start()

    pltpu.make_async_copy(
        relay_out.at[rows_of(near)], landed.at[:, wide(near)], recv_d.at[0]
    ).start()
    pltpu.make_async_remote_copy(
        src_ref=landed,
        dst_ref=landed,
        send_sem=send_d.at[0],
        recv_sem=recv_d.at[0],
        device_id=(upper * NEAR + neighbour(1), seq),
        device_id_type=MESH,
    ).wait_recv()

    for tile in range(TILES):
        columns = slice(tile * LANES, (tile + 1) * LANES)
        out_ref[:, columns] = (
            gate_ref[:, columns].astype(F32) * landed[:, columns].astype(F32)
        ).astype(BF16)

    sent = pl.ds(0, (NEAR - 1) * WIDE)
    for array in range(3):
        pltpu.make_async_remote_copy(
            src_ref=sources[array].at[:, sent],
            dst_ref=sources[array].at[:, sent],
            send_sem=send_a.at[array],
            recv_sem=recv_a.at[array],
            device_id=(upper * NEAR + neighbour(1), seq),
            device_id_type=MESH,
        ).wait_send()
    pltpu.make_async_remote_copy(
        src_ref=relay_out.at[pl.ds(0, 8 * (NEAR - 1))],
        dst_ref=relay_out.at[pl.ds(0, 8 * (NEAR - 1))],
        send_sem=send_d.at[0],
        recv_sem=recv_d.at[0],
        device_id=(upper * NEAR + neighbour(1), seq),
        device_id_type=MESH,
    ).wait_send()

    for place in range(HEADS_LOCAL):

        @pl.when(seq != seats[place])
        def _():
            rates_copy(place).wait_send()

    for slot in range(HEADS_NEAR):

        @pl.when(other(targets[slot]))
        def _():
            relay_copy(slot).wait_send()

    @pl.when(seated)
    def _():
        @pl.loop(0, STEPS)
        def _(mini):
            device = (lax.rem(mini, 2) * NEAR + my_near, mini // 2)

            @pl.when(other(device))
            def _():
                pltpu.make_async_remote_copy(
                    src_ref=blocks_out.at[mini],
                    dst_ref=returned.at[my_slot],
                    send_sem=send_c.at[mini],
                    recv_sem=recv_c.at[my_slot],
                    device_id=device,
                    device_id_type=MESH,
                ).wait_send()


def local(*arrays):
    arrays = list(arrays)
    arrays[4] = arrays[4].T
    arrays[7] = jnp.swapaxes(arrays[7], 1, 2)
    vmem = pl.BlockSpec(memory_space=pltpu.VMEM)
    dma = pltpu.SemaphoreType.DMA
    return pl.pallas_call(
        kernel,
        out_shape=jax.ShapeDtypeStruct((8, TILES * LANES), BF16),
        in_specs=[pl.BlockSpec(memory_space=pl.ANY)] * len(arrays),
        out_specs=vmem,
        scratch_shapes=[
            *[pltpu.VMEM(array.shape, array.dtype) for array in arrays[3:]],
            pltpu.VMEM((3, MINI, WIDE), BF16),
            pltpu.VMEM((HEADS_NEAR, PACKED, LANES), BF16),
            pltpu.VMEM((HEADS_LOCAL, 2, 8, LANES), F32),
            pltpu.VMEM((STEPS, 8, LANES), F32),
            pltpu.VMEM((STEPS, PACKED, LANES), BF16),
            pltpu.VMEM((STEPS, MINI, LANES), BF16),
            pltpu.VMEM((HEADS_NEAR, MINI, LANES), BF16),
            pltpu.VMEM((MINI, WIDE), BF16),
            pltpu.VMEM((8, TILES * LANES), BF16),
            pltpu.VMEM((STEPS, D_HEAD, LANES), F32),
            pltpu.VMEM((LANES, LANES), BF16),
            pltpu.VMEM((LANES, LANES), BF16),
            pltpu.VMEM((8, LANES), F32),
            pltpu.VMEM((D_HEAD, LANES), F32),
            pltpu.VMEM((LANES, LANES), F32),
            pltpu.VMEM((LANES, LANES), F32),
            pltpu.VMEM((INNER, LANES), F32),
            pltpu.VMEM((INNER, LANES), F32),
            pltpu.VMEM((INNER, LANES), F32),
            pltpu.VMEM((HISTORY, LANES, INNER), BF16),
            pltpu.VMEM((HISTORY, D_HEAD, LANES), F32),
            pltpu.VMEM((D_HEAD, LANES), F32),
            pltpu.VMEM((D_HEAD, LANES), F32),
            pltpu.VMEM((INNER, LANES), F32),
            pltpu.VMEM((INNER, LANES), F32),
            pltpu.VMEM((2, INNER, LANES), BF16),
            pltpu.VMEM((HISTORY, INNER, LANES), BF16),
            pltpu.VMEM((HISTORY, D_HEAD, LANES), BF16),
            pltpu.VMEM((INNER, LANES), BF16),
            pltpu.VMEM((LANES, LANES), BF16),
            pltpu.VMEM((D_HEAD, LANES), F32),
            pltpu.VMEM((LANES, LANES), BF16),
            dma((8,)),
            dma((3,)),
            dma((3,)),
            dma((HEADS_NEAR,)),
            dma((STEPS,)),
            dma((HEADS_LOCAL,)),
            dma((CHAIN,)),
            dma((STEPS,)),
            dma((HEADS_NEAR,)),
            dma((1,)),
            dma((1,)),
        ],
        compiler_params=pltpu.CompilerParams(collective_id=0, has_side_effects=True),
    )(*arrays)


def solution(mesh):
    rows = P(("seq", "head"), None)
    in_specs = (
        rows,
        rows,
        rows,
        rows,
        P("seq", "head"),
        P("head", None, None),
        P("head", None),
        P("head", None, None),
        P("head", None),
        P("head", None),
        P("head", None),
    )
    return jax.shard_map(local, mesh=mesh, in_specs=in_specs, out_specs=rows, check_vma=False)
```

```python
import functools

import jax
import jax.numpy as jnp
from jax import lax
from jax.experimental import pallas as pl
from jax.experimental.pallas import tpu as pltpu
from jax.sharding import PartitionSpec as P

D_HEAD = 64
INNER = 256
MINI = 64
STEPS = 64
LANES = 128
NEAR = 8
CHAIN = 32
HEADS_LOCAL = 3
HEADS_NEAR = 6
WIDE = HEADS_NEAR * D_HEAD
TILES = 24

EPS = 1e-06
ROOT = 0.7978845608028654
CUBE = 0.044715
MESH = pl.DeviceIdType.MESH
F32 = jnp.float32
BF16 = jnp.bfloat16

PACKED = MINI + MINI // 2
HISTORY = 4
SPACING_NS = 665

SEATS = (((1, 7, 12), (2, 4, 15)), ((29, 26, 16), (30, 25, 19)))


def dot(left, right, dims):
    return lax.dot_general(
        left, right, (((dims[0],), (dims[1],)), ((), ())), preferred_element_type=F32
    )


def gelu(values):
    squared = values * values
    tanh_term = jnp.tanh(values * (ROOT + (ROOT * CUBE) * squared))
    return values * (0.5 + 0.5 * tanh_term)


def gelu_and_slope(values):
    squared = values * values
    tanh_term = jnp.tanh(values * (ROOT + (ROOT * CUBE) * squared))
    half = 0.5 + 0.5 * tanh_term
    slope = half + values * (half * (1.0 - tanh_term)) * (ROOT + (3.0 * ROOT * CUBE) * squared)
    return (values * half, slope)


def row_mean(values):
    rows = values.shape[0]
    while rows > 8:
        rows //= 2
        values = values[:rows] + values[rows:]
    return jnp.sum(values, axis=0, keepdims=True) * (1.0 / D_HEAD)


def lanes_left(rows):
    return lax.broadcasted_iota(jnp.int32, (rows, LANES), 1) < D_HEAD


def own_half(stacked):
    return jnp.where(lanes_left(D_HEAD), stacked[:D_HEAD], stacked[D_HEAD:])


def spread_halves(rows):
    left = lanes_left(D_HEAD)
    zero = jnp.zeros_like(rows)
    return jnp.concatenate([jnp.where(left, rows, zero), jnp.where(left, zero, rows)], axis=0)


def seat_of(upper, core, place):
    lower_seat = jnp.where(core == 0, SEATS[0][0][place], SEATS[0][1][place])
    upper_seat = jnp.where(core == 0, SEATS[1][0][place], SEATS[1][1][place])
    return jnp.where(upper == 0, lower_seat, upper_seat)


def kernel(
    query_ref,
    key_ref,
    value_ref,
    rates_far,
    first_far,
    first_bias_far,
    second_far,
    second_bias_far,
    gain_far,
    shift_far,
    landed,
    rates_ref,
    first_ref,
    first_bias_ref,
    second_ref,
    second_bias_ref,
    gain_ref,
    shift_ref,
    gathered,
    packed,
    rates_out,
    rates_in,
    tokens,
    blocks_out,
    returned,
    relay_out,
    kept_rows,
    bd_key,
    turned_query,
    rate_rows,
    target_rows,
    causal,
    halves,
    state_one,
    bias_one,
    state_two,
    second_hist,
    bias_two,
    gain_rows,
    shift_rows,
    slope_ref,
    dual_base,
    dual_act_ref,
    act_ref,
    grad_two_ref,
    grad_one_ref,
    within_ref,
    read_ref,
    attend_ref,
    load_sem,
    send_a,
    recv_a,
    send_b,
    recv_b,
    send_r,
    recv_r,
    send_c,
    recv_c,
    send_d,
    recv_d,
):
    fetches = [
        pltpu.make_async_copy(far, here, load_sem.at[place])
        for place, (far, here) in enumerate(
            (
                (rates_far, rates_ref),
                (first_far, first_ref),
                (first_bias_far, first_bias_ref),
                (second_far, second_ref),
                (second_bias_far, second_bias_ref),
                (gain_far, gain_ref),
                (shift_far, shift_ref),
            )
        )
    ]
    for fetch in fetches:
        fetch.start()

    head = lax.axis_index("head")
    seq = lax.axis_index("seq")
    core = lax.rem(head, 2)
    upper = head // NEAR
    near = lax.rem(head, NEAR)
    own_mini = 2 * seq + upper
    seats = [seat_of(upper, core, place) for place in range(HEADS_LOCAL)]
    seated = jnp.logical_or(seq == seats[0], jnp.logical_or(seq == seats[1], seq == seats[2]))
    my_place = jnp.where(seq == seats[1], 1, 0) + jnp.where(seq == seats[2], 2, 0)
    my_slot = HEADS_LOCAL * core + my_place
    my_near = head // 2
    own_source = jnp.logical_and(seated, near == my_near)

    targets = [
        (
            2 * near + slot // HEADS_LOCAL,
            seat_of(near // 4, slot // HEADS_LOCAL, slot % HEADS_LOCAL),
        )
        for slot in range(HEADS_NEAR)
    ]

    def other(device):
        return jnp.logical_or(device[0] != head, device[1] != seq)

    def neighbour(step):
        return lax.rem(near + step, NEAR)

    barrier = pltpu.get_barrier_semaphore()

    def greet(device):
        pl.semaphore_signal(barrier, inc=1, device_id=device, device_id_type=MESH)

    @pl.when(seated)
    def _():
        @pl.loop(0, STEPS)
        def _(turn):
            mini = jnp.where(lax.rem(turn, 2) == 0, turn // 2, STEPS - 1 - turn // 2)
            device = (lax.rem(mini, 2) * NEAR + my_near, mini // 2)

            @pl.when(other(device))
            def _():
                greet(device)

        @pl.loop(1, CHAIN)
        def _(step):
            greet((head, lax.rem(seq + step, CHAIN)))

    for device in targets:

        @pl.when(other(device))
        def _():
            greet(device)

    @pl.loop(1, NEAR)
    def _(step):
        greet((upper * NEAR + neighbour(step), seq))

    fetches[0].wait()
    left_lanes = lanes_left(MINI)
    for place in range(HEADS_LOCAL):
        row = jnp.broadcast_to(rates_ref[place : place + 1], (8, LANES))
        turned_row = pltpu.roll(row, D_HEAD, 1)
        rates_out[place, 0] = jnp.where(left_lanes[:8], row, turned_row)
        rates_out[place, 1] = jnp.where(left_lanes[:8], turned_row, row)

    expected = NEAR - 1 + HEADS_NEAR + HEADS_LOCAL
    expected = expected + jnp.where(seated, STEPS - 1, 0) - jnp.where(own_source, 2, 0)
    pl.semaphore_wait(barrier, expected)

    sources = (query_ref, key_ref, value_ref)

    def wide(index):
        return pl.ds(pl.multiple_of(index * WIDE, LANES), WIDE)

    def rows_of(index):
        return pl.ds(pl.multiple_of(index * 8, 8), 8)

    def exchange_copy(array, step):
        target = neighbour(step)
        return pltpu.make_async_remote_copy(
            src_ref=sources[array].at[:, wide(target)],
            dst_ref=gathered.at[array, rows_of(near)],
            send_sem=send_a.at[array],
            recv_sem=recv_a.at[array],
            device_id=(upper * NEAR + target, seq),
            device_id_type=MESH,
        )

    def own_exchange(array):
        return pltpu.make_async_copy(
            sources[array].at[:, wide(near)], gathered.at[array, rows_of(near)], recv_a.at[array]
        )

    @pl.loop(1, NEAR)
    def _(step):
        for array in range(3):
            exchange_copy(array, step).start()

    for array in range(3):
        own_exchange(array).start()

    def rates_copy(place):
        return pltpu.make_async_remote_copy(
            src_ref=rates_out.at[place],
            dst_ref=rates_in.at[pl.ds(2 * seq, 2)],
            send_sem=send_r.at[place],
            recv_sem=recv_r.at[seq],
            device_id=(head, seats[place]),
            device_id_type=MESH,
        )

    for place in range(HEADS_LOCAL):

        @pl.when(seq != seats[place])
        def _():
            rates_copy(place).start()

    for array in range(3):
        pltpu.make_async_remote_copy(
            src_ref=gathered.at[array],
            dst_ref=gathered.at[array],
            send_sem=send_a.at[array],
            recv_sem=recv_a.at[array],
            device_id=(upper * NEAR + neighbour(1), seq),
            device_id_type=MESH,
        ).wait_recv()

    def relay_copy(slot):
        return pltpu.make_async_remote_copy(
            src_ref=packed.at[slot],
            dst_ref=tokens.at[own_mini],
            send_sem=send_b.at[slot],
            recv_sem=recv_b.at[own_mini],
            device_id=targets[slot],
            device_id_type=MESH,
        )

    for tile in range(HEADS_NEAR // 2):
        columns = slice(tile * LANES, (tile + 1) * LANES)
        queries, keys, values = [gathered[array, :, columns].astype(F32) for array in range(3)]
        queries_turned, keys_turned, values_turned = [
            pltpu.roll(rows, D_HEAD, 1) for rows in (queries, keys, values)
        ]
        first_keys = jnp.where(left_lanes, keys, values_turned)
        second_keys = jnp.where(left_lanes, keys_turned, values)
        half = MINI // 2
        first_queries = jnp.where(left_lanes[:half], queries[:half], queries_turned[half:])
        second_queries = jnp.where(left_lanes[:half], queries_turned[:half], queries[half:])
        packed[2 * tile, :MINI] = first_keys.astype(BF16)
        packed[2 * tile, MINI:] = first_queries.astype(BF16)
        packed[2 * tile + 1, :MINI] = second_keys.astype(BF16)
        packed[2 * tile + 1, MINI:] = second_queries.astype(BF16)

    late = jnp.minimum(own_mini, STEPS - 1 - own_mini)
    pl.delay(jnp.where(seated, 0, late) * SPACING_NS)

    for slot in range(HEADS_NEAR):

        @pl.when(other(targets[slot]))
        def _():
            relay_copy(slot).start()

    for fetch in fetches[1:]:
        fetch.wait()

    @pl.when(seated)
    def _():
        @pl.when(own_source)
        def _():
            tokens[own_mini] = packed[my_slot]

        rates_in[pl.ds(2 * seq, 2)] = rates_out[my_place]

        row = lax.broadcasted_iota(jnp.int32, (LANES, LANES), 0)
        col = lax.broadcasted_iota(jnp.int32, (LANES, LANES), 1)
        ahead = jnp.logical_and(jnp.logical_and(row < 64, col < 64), row <= col)
        back = jnp.logical_and(jnp.logical_and(row >= 64, col >= 64), row >= col)
        causal[...] = jnp.where(jnp.logical_or(ahead, back), 1.0, 0.0)
        halves[...] = jnp.where((row < 64) == (col < 64), 1.0, 0.0)

        first = first_ref[my_place]
        both = jnp.concatenate([first, first], axis=0)
        state_one[...] = both.T
        second = second_ref[my_place]
        second = second - jnp.mean(second, axis=0, keepdims=True)
        doubled = jnp.concatenate([second, second], axis=0)
        state_two[...] = doubled.T
        second_hist[0] = doubled.astype(BF16)

        def spread_column(row_values, length):
            return jnp.broadcast_to(row_values, (LANES, length)).T

        bias_one[...] = spread_column(first_bias_ref[pl.ds(my_place, 1), :], INNER)
        second_bias = second_bias_ref[pl.ds(my_place, 1), :]
        second_bias = second_bias - jnp.mean(second_bias, axis=1, keepdims=True)
        bias_two[0] = spread_column(second_bias, D_HEAD)
        gain_rows[...] = spread_column(gain_ref[pl.ds(my_place, 1), :], D_HEAD)
        shift_rows[...] = spread_column(shift_ref[pl.ds(my_place, 1), :], D_HEAD)

        def await_step(step):
            for mini in (step, STEPS - 1 - step):

                @pl.when(jnp.logical_not(jnp.logical_and(own_source, mini == own_mini)))
                def _():
                    pltpu.make_async_remote_copy(
                        src_ref=packed.at[0],
                        dst_ref=tokens.at[mini],
                        send_sem=send_b.at[0],
                        recv_sem=recv_b.at[mini],
                        device_id=(lax.rem(mini, 2) * NEAR + my_near, mini // 2),
                        device_id_type=MESH,
                    ).wait_recv()

        def await_rates(block):
            @pl.when(block != seq)
            def _():
                pltpu.make_async_remote_copy(
                    src_ref=rates_out.at[0],
                    dst_ref=rates_in.at[pl.ds(2 * block, 2)],
                    send_sem=send_r.at[0],
                    recv_sem=recv_r.at[block],
                    device_id=(head, block),
                    device_id_type=MESH,
                ).wait_recv()

        def load_step(step):
            back = STEPS - 1 - step
            kv_f = tokens[step, :MINI]
            kv_b = tokens[back, :MINI]
            left = lanes_left(MINI)
            keys_back = pltpu.roll(kv_b.astype(F32), D_HEAD, 1)
            keys_bd = jnp.concatenate(
                [jnp.where(left, kv_f.astype(F32), 0.0), jnp.where(left, 0.0, keys_back)], axis=0
            ).astype(BF16)
            pieces = []
            for mini in (step, back):
                pair = tokens[mini, MINI:].astype(F32)
                pieces += [pair, pltpu.roll(pair, D_HEAD, 1)]
            kv_turned = jnp.concatenate([kv_f, kv_b], axis=0).T.astype(F32)
            queries = jnp.concatenate(pieces, axis=0).astype(BF16).T.astype(F32)[:D_HEAD]
            target = kv_turned[D_HEAD:] - kv_turned[:D_HEAD]
            rate = jnp.where(left[:8], rates_in[step], rates_in[back])
            keys_turned = spread_halves(kv_turned[:D_HEAD]).astype(BF16)
            queries_turned = spread_halves(queries).astype(BF16)
            return (keys_bd, keys_turned, queries_turned, target, rate)

        def store_step(loaded):
            bd_key[...] = loaded[0]
            turned_query[...] = loaded[2]
            target_rows[...] = gain_rows[...] * (shift_rows[...] - loaded[3])
            rate_rows[...] = loaded[4]

        def finish(step, dual_two):
            mean = row_mean(dual_two)
            spread = lax.rsqrt(row_mean(dual_two * dual_two) - mean * mean + EPS)
            fitted = gain_rows[...] * ((dual_two - mean) * spread) + shift_rows[...]
            kept_rows[step] = fitted
            total = fitted + pltpu.roll(kept_rows[STEPS - 1 - step], D_HEAD, 1)
            at_left = lax.rem(my_slot, 2) == 0
            total = jnp.concatenate(
                [jnp.where(at_left, total, 0.0), jnp.where(at_left, 0.0, total)], axis=0
            )
            turned = total.astype(BF16).T
            blocks_out[step] = turned[:MINI]
            blocks_out[STEPS - 1 - step] = turned[MINI:]

        def slot_of(step):
            return lax.rem(step, HISTORY)

        def attend_dual(step):
            slot = slot_of(step)
            dual_act = dual_act_ref[lax.rem(step, 2)]
            mask = causal[...]
            read = dot(second_hist[slot], dual_act, (1, 0))
            attend = dot(act_ref[slot].T, dual_act, (1, 0))
            return (own_half(read) + bias_two[slot], (attend * mask + mask).astype(BF16))

        half = INNER // 2
        row_halves = (slice(0, half), slice(half, INNER))

        def widen(grad_one, within, base, bias, ones_bf):
            sums = jnp.concatenate([within, ones_bf], axis=1)
            falls = [dot(grad_one[rows], sums, (1, 0)) for rows in row_halves]
            acts = [
                gelu(base[rows] - fall[:, :LANES]).astype(BF16)
                for rows, fall in zip(row_halves, falls)
            ]
            biases = [bias[rows] - fall[:, LANES:] for rows, fall in zip(row_halves, falls)]
            return (acts, biases)

        def advance(step):
            slot = slot_of(step)
            before = step + HISTORY - 2
            act = act_ref[slot]
            second_turned = second_hist[slot]
            target = target_rows[...]
            gain = gain_rows[...]
            gain_sq = gain * gain
            rate = rate_rows[0:1]
            bias_two_now = bias_two[slot]
            ones_bd = halves[...]
            ones_bf = ones_bd.astype(BF16)
            mask = causal[...]

            pre_two = (
                jnp.where(
                    lanes_left(D_HEAD),
                    dot(second_turned[:D_HEAD], act, (1, 0)),
                    dot(second_turned[D_HEAD:], act, (1, 0)),
                )
                + bias_two_now
            )

            last_read = read_ref[...]
            last_fall = dot(grad_two_ref[slot_of(step + HISTORY - 3)], attend_ref[...], (1, 0))
            dual_acts, biases = widen(
                grad_one_ref[...], within_ref[...], dual_base[...], bias_one[...], ones_bf
            )

            later = jnp.minimum(step + 1, STEPS - 1)
            loaded = load_step(later)
            keys_bd = bd_key[...]
            queries_turned = turned_query[...]
            state_one_now = state_one[...]
            high = state_one_now.astype(BF16)
            low = (state_one_now - high.astype(F32)).astype(BF16)
            reads = jnp.concatenate([loaded[1], queries_turned], axis=1)
            reads = jnp.concatenate([reads, reads], axis=0)
            within_both = dot(
                jnp.concatenate([keys_bd, jnp.zeros_like(keys_bd)], axis=1), reads, (1, 0)
            )
            between = (within_both[:, :LANES] + ones_bd).astype(BF16)
            within = (within_both[:, LANES:] * mask + mask).astype(BF16)

            scaled = gain_sq * pre_two
            mean = row_mean(pre_two)
            sum_scaled = row_mean(scaled)
            sum_square = row_mean(pre_two * pre_two)
            sum_scaled_sq = row_mean(scaled * pre_two)
            sum_target = row_mean(target * pre_two)
            mean_gain = row_mean(gain_sq)
            mean_target = row_mean(target)
            inverse = lax.rsqrt(sum_square - mean * mean + EPS)
            centred_scaled = sum_scaled - mean * mean_gain
            mean_a = inverse * centred_scaled + mean_target
            mean_an = inverse * (
                inverse * (sum_scaled_sq - mean * (sum_scaled + centred_scaled))
                + (sum_target - mean * mean_target)
            )
            weight = inverse * rate
            grad_two = (
                (pre_two - mean) * (inverse * gain_sq - inverse * mean_an) + (target - mean_a)
            ) * weight
            grad_two = grad_two.astype(BF16)
            grad_two_bd = spread_halves(grad_two)
            state_two_now = state_two[...]
            state_two_bf = state_two_now.astype(BF16)
            grads_one = [
                (dot(state_two_bf[rows], grad_two_bd, (1, 0)) * slope_ref[rows, :]).astype(BF16)
                for rows in row_halves
            ]

            finish(jnp.maximum(step - 3, 0), last_read - last_fall)

            state_two_new = state_two_now - dot(act, grad_two_bd.T, (1, 0))
            bias_two_new = bias_two_now - dot(grad_two, ones_bf, (1, 0))
            dual_read, attend = attend_dual(before)
            read_ref[...] = dual_read
            attend_ref[...] = attend

            seen = dot(jnp.concatenate([high, low], axis=1), reads, (1, 0))
            moves = jnp.concatenate([between, keys_bd], axis=1)
            next_slot = slot_of(step + 1)
            for part in range(2):
                rows = row_halves[part]
                fall = dot(grads_one[part], moves, (1, 0))
                state_one[rows, :] = state_one_now[rows] - fall[:, LANES:]
                pre_one = seen[rows, :LANES] + biases[part] - fall[:, :LANES]
                act_next, slope_next = gelu_and_slope(pre_one)
                act_ref[next_slot, rows, :] = act_next.astype(BF16)
                slope_ref[rows, :] = slope_next
                dual_base[rows, :] = seen[rows, LANES:] + biases[part]
                bias_one[rows, :] = biases[part]
                grad_one_ref[rows, :] = grads_one[part]
                dual_act_ref[lax.rem(step + 1, 2), rows, :] = dual_acts[part]

            state_two[...] = state_two_new
            second_hist[next_slot] = state_two_new.astype(BF16).T
            bias_two[next_slot] = bias_two_new
            grad_two_ref[slot] = grad_two
            within_ref[...] = within
            store_step(loaded)

        def emit(step, read, attend):
            finish(step, read - dot(grad_two_ref[slot_of(step)], attend, (1, 0)))

        def return_copy(mini):
            return pltpu.make_async_remote_copy(
                src_ref=blocks_out.at[mini],
                dst_ref=returned.at[my_slot],
                send_sem=send_c.at[mini],
                recv_sem=recv_c.at[my_slot],
                device_id=(lax.rem(mini, 2) * NEAR + my_near, mini // 2),
                device_id_type=MESH,
            )

        def is_own(mini):
            return jnp.logical_and(own_source, mini == own_mini)

        def give_back(mini):
            @pl.when(jnp.logical_not(is_own(mini)))
            def _():
                return_copy(mini).start()

            @pl.when(is_own(mini))
            def _():
                returned[my_slot] = blocks_out[mini]

        await_rates(0)
        await_rates(CHAIN - 1)
        await_step(0)
        begun = load_step(0)
        store_step(begun)
        high = state_one[...].astype(BF16)
        low = (state_one[...] - high.astype(F32)).astype(BF16)
        act, slope = gelu_and_slope(
            dot(high, begun[1], (1, 0)) + dot(low, begun[1], (1, 0)) + bias_one[...]
        )
        act_ref[0] = act.astype(BF16)
        slope_ref[...] = slope
        grad_one_ref[...] = jnp.zeros_like(grad_one_ref)
        within_ref[...] = jnp.zeros_like(within_ref)

        @pl.loop(0, STEPS)
        def _(step):
            later = step + 1

            @pl.when(later < STEPS // 2)
            def _():
                await_step(later)

                @pl.when(lax.rem(later, 2) == 0)
                def _():
                    await_rates(later // 2)
                    await_rates(CHAIN - 1 - later // 2)

            advance(step)
            done = step - 3

            @pl.when(done >= STEPS // 2)
            def _():
                give_back(done)
                give_back(STEPS - 1 - done)

        last = STEPS - 1
        dual_acts, _ = widen(
            grad_one_ref[...],
            within_ref[...],
            dual_base[...],
            bias_one[...],
            halves[...].astype(BF16),
        )
        later = attend_dual(last - 1)
        emit(last - 2, read_ref[...], attend_ref[...])
        for part in range(2):
            dual_act_ref[last % 2, row_halves[part], :] = dual_acts[part]
        latest = attend_dual(last)
        emit(last - 1, *later)
        emit(last, *latest)
        for step in (last, last - 1, last - 2):
            give_back(step)
            give_back(STEPS - 1 - step)

    for slot in range(HEADS_NEAR):

        @pl.when(other(targets[slot]))
        def _():
            pltpu.make_async_remote_copy(
                src_ref=blocks_out.at[0],
                dst_ref=returned.at[slot],
                send_sem=send_c.at[0],
                recv_sem=recv_c.at[slot],
                device_id=targets[slot],
                device_id_type=MESH,
            ).wait_recv()

    for tile in range(HEADS_NEAR // 2):
        columns = slice(tile * LANES, (tile + 1) * LANES)
        relay_out[:, columns] = jnp.where(left_lanes, returned[2 * tile], returned[2 * tile + 1])

    def spread_copy(step):
        target = neighbour(step)
        return pltpu.make_async_remote_copy(
            src_ref=relay_out.at[rows_of(target)],
            dst_ref=landed.at[:, wide(near)],
            send_sem=send_d.at[0],
            recv_sem=recv_d.at[0],
            device_id=(upper * NEAR + target, seq),
            device_id_type=MESH,
        )

    @pl.loop(1, NEAR)
    def _(step):
        spread_copy(step).start()

    pltpu.make_async_copy(
        relay_out.at[rows_of(near)], landed.at[:, wide(near)], recv_d.at[0]
    ).start()
    pltpu.make_async_remote_copy(
        src_ref=landed,
        dst_ref=landed,
        send_sem=send_d.at[0],
        recv_sem=recv_d.at[0],
        device_id=(upper * NEAR + neighbour(1), seq),
        device_id_type=MESH,
    ).wait_recv()

    sent = pl.ds(0, (NEAR - 1) * WIDE)
    for array in range(3):
        pltpu.make_async_remote_copy(
            src_ref=sources[array].at[:, sent],
            dst_ref=sources[array].at[:, sent],
            send_sem=send_a.at[array],
            recv_sem=recv_a.at[array],
            device_id=(upper * NEAR + neighbour(1), seq),
            device_id_type=MESH,
        ).wait_send()
    pltpu.make_async_remote_copy(
        src_ref=relay_out.at[pl.ds(0, 8 * (NEAR - 1))],
        dst_ref=relay_out.at[pl.ds(0, 8 * (NEAR - 1))],
        send_sem=send_d.at[0],
        recv_sem=recv_d.at[0],
        device_id=(upper * NEAR + neighbour(1), seq),
        device_id_type=MESH,
    ).wait_send()

    for place in range(HEADS_LOCAL):

        @pl.when(seq != seats[place])
        def _():
            rates_copy(place).wait_send()

    for slot in range(HEADS_NEAR):

        @pl.when(other(targets[slot]))
        def _():
            relay_copy(slot).wait_send()

    @pl.when(seated)
    def _():
        @pl.loop(0, STEPS)
        def _(mini):
            device = (lax.rem(mini, 2) * NEAR + my_near, mini // 2)

            @pl.when(other(device))
            def _():
                pltpu.make_async_remote_copy(
                    src_ref=blocks_out.at[mini],
                    dst_ref=returned.at[my_slot],
                    send_sem=send_c.at[mini],
                    recv_sem=recv_c.at[my_slot],
                    device_id=device,
                    device_id_type=MESH,
                ).wait_send()


def local(*arrays):
    arrays = list(arrays)
    arrays[4] = arrays[4].T
    arrays[7] = jnp.swapaxes(arrays[7], 1, 2)
    gate = arrays.pop(3)
    anywhere = pl.BlockSpec(memory_space=pl.ANY)
    dma = pltpu.SemaphoreType.DMA
    summed = pl.pallas_call(
        kernel,
        out_shape=jax.ShapeDtypeStruct((8, TILES * LANES), BF16),
        in_specs=[anywhere] * len(arrays),
        out_specs=anywhere,
        scratch_shapes=[
            *[pltpu.VMEM(array.shape, array.dtype) for array in arrays[3:]],
            pltpu.VMEM((3, MINI, WIDE), BF16),
            pltpu.VMEM((HEADS_NEAR, PACKED, LANES), BF16),
            pltpu.VMEM((HEADS_LOCAL, 2, 8, LANES), F32),
            pltpu.VMEM((STEPS, 8, LANES), F32),
            pltpu.VMEM((STEPS, PACKED, LANES), BF16),
            pltpu.VMEM((STEPS, MINI, LANES), BF16),
            pltpu.VMEM((HEADS_NEAR, MINI, LANES), BF16),
            pltpu.VMEM((MINI, WIDE), BF16),
            pltpu.VMEM((STEPS, D_HEAD, LANES), F32),
            pltpu.VMEM((LANES, LANES), BF16),
            pltpu.VMEM((LANES, LANES), BF16),
            pltpu.VMEM((8, LANES), F32),
            pltpu.VMEM((D_HEAD, LANES), F32),
            pltpu.VMEM((LANES, LANES), F32),
            pltpu.VMEM((LANES, LANES), F32),
            pltpu.VMEM((INNER, LANES), F32),
            pltpu.VMEM((INNER, LANES), F32),
            pltpu.VMEM((INNER, LANES), F32),
            pltpu.VMEM((HISTORY, LANES, INNER), BF16),
            pltpu.VMEM((HISTORY, D_HEAD, LANES), F32),
            pltpu.VMEM((D_HEAD, LANES), F32),
            pltpu.VMEM((D_HEAD, LANES), F32),
            pltpu.VMEM((INNER, LANES), F32),
            pltpu.VMEM((INNER, LANES), F32),
            pltpu.VMEM((2, INNER, LANES), BF16),
            pltpu.VMEM((HISTORY, INNER, LANES), BF16),
            pltpu.VMEM((HISTORY, D_HEAD, LANES), BF16),
            pltpu.VMEM((INNER, LANES), BF16),
            pltpu.VMEM((LANES, LANES), BF16),
            pltpu.VMEM((D_HEAD, LANES), F32),
            pltpu.VMEM((LANES, LANES), BF16),
            dma((7,)),
            dma((3,)),
            dma((3,)),
            dma((HEADS_NEAR,)),
            dma((STEPS,)),
            dma((HEADS_LOCAL,)),
            dma((CHAIN,)),
            dma((STEPS,)),
            dma((HEADS_NEAR,)),
            dma((1,)),
            dma((1,)),
        ],
        compiler_params=pltpu.CompilerParams(collective_id=0, has_side_effects=True),
    )(*arrays)
    return (gate.astype(F32) * summed.astype(F32)).astype(BF16)


def solution(mesh):
    rows = P(("seq", "head"), None)
    in_specs = (
        rows,
        rows,
        rows,
        rows,
        P("seq", "head"),
        P("head", None, None),
        P("head", None),
        P("head", None, None),
        P("head", None),
        P("head", None),
        P("head", None),
    )
    return jax.shard_map(local, mesh=mesh, in_specs=in_specs, out_specs=rows, check_vma=False)
```

```python
import functools

import jax
import jax.numpy as jnp
from jax import lax
from jax.experimental import pallas as pl
from jax.experimental.pallas import tpu as pltpu
from jax.sharding import PartitionSpec as P

D_HEAD = 64
INNER = 256
MINI = 64
STEPS = 64
LANES = 128
NEAR = 8
CHAIN = 32
HEADS_LOCAL = 3
HEADS_NEAR = 6
WIDE = HEADS_NEAR * D_HEAD
TILES = 24

EPS = 1e-06
ROOT = 0.7978845608028654
CUBE = 0.044715
MESH = pl.DeviceIdType.MESH
F32 = jnp.float32
BF16 = jnp.bfloat16

PACKED = MINI + MINI // 2
HISTORY = 4
SPACING_NS = 640

SEATS = (((1, 7, 12), (2, 4, 15)), ((29, 26, 16), (30, 25, 19)))


def dot(left, right, dims):
    return lax.dot_general(
        left, right, (((dims[0],), (dims[1],)), ((), ())), preferred_element_type=F32
    )


def gelu(values):
    squared = values * values
    tanh_term = jnp.tanh(values * (ROOT + (ROOT * CUBE) * squared))
    return values * (0.5 + 0.5 * tanh_term)


def gelu_and_slope(values):
    squared = values * values
    tanh_term = jnp.tanh(values * (ROOT + (ROOT * CUBE) * squared))
    half = 0.5 + 0.5 * tanh_term
    slope = half + values * (half * (1.0 - tanh_term)) * (ROOT + (3.0 * ROOT * CUBE) * squared)
    return (values * half, slope)


def row_mean(values):
    rows = values.shape[0]
    while rows > 8:
        rows //= 2
        values = values[:rows] + values[rows:]
    return jnp.sum(values, axis=0, keepdims=True) * (1.0 / D_HEAD)


def lanes_left(rows):
    return lax.broadcasted_iota(jnp.int32, (rows, LANES), 1) < D_HEAD


def own_half(stacked):
    return jnp.where(lanes_left(D_HEAD), stacked[:D_HEAD], stacked[D_HEAD:])


def spread_halves(rows):
    left = lanes_left(D_HEAD)
    zero = jnp.zeros_like(rows)
    return jnp.concatenate([jnp.where(left, rows, zero), jnp.where(left, zero, rows)], axis=0)


def seat_of(upper, core, place):
    lower_seat = jnp.where(core == 0, SEATS[0][0][place], SEATS[0][1][place])
    upper_seat = jnp.where(core == 0, SEATS[1][0][place], SEATS[1][1][place])
    return jnp.where(upper == 0, lower_seat, upper_seat)


def kernel(
    query_ref,
    key_ref,
    value_ref,
    rates_far,
    first_far,
    first_bias_far,
    second_far,
    second_bias_far,
    gain_far,
    shift_far,
    landed,
    rates_ref,
    first_ref,
    first_bias_ref,
    second_ref,
    second_bias_ref,
    gain_ref,
    shift_ref,
    gathered,
    packed,
    rates_out,
    rates_in,
    tokens,
    blocks_out,
    returned,
    relay_out,
    kept_rows,
    bd_key,
    turned_query,
    rate_rows,
    target_rows,
    causal,
    halves,
    state_one,
    bias_one,
    state_two,
    second_hist,
    bias_two,
    gain_rows,
    shift_rows,
    slope_ref,
    dual_base,
    dual_act_ref,
    act_ref,
    grad_two_ref,
    grad_one_ref,
    within_ref,
    read_ref,
    attend_ref,
    load_sem,
    send_a,
    recv_a,
    send_b,
    recv_b,
    send_r,
    recv_r,
    send_c,
    recv_c,
    send_d,
    recv_d,
):
    fetches = [
        pltpu.make_async_copy(far, here, load_sem.at[place])
        for place, (far, here) in enumerate(
            (
                (rates_far, rates_ref),
                (first_far, first_ref),
                (first_bias_far, first_bias_ref),
                (second_far, second_ref),
                (second_bias_far, second_bias_ref),
                (gain_far, gain_ref),
                (shift_far, shift_ref),
            )
        )
    ]
    for fetch in fetches:
        fetch.start()

    head = lax.axis_index("head")
    seq = lax.axis_index("seq")
    core = lax.rem(head, 2)
    upper = head // NEAR
    near = lax.rem(head, NEAR)
    own_mini = 2 * seq + upper
    seats = [seat_of(upper, core, place) for place in range(HEADS_LOCAL)]
    seated = jnp.logical_or(seq == seats[0], jnp.logical_or(seq == seats[1], seq == seats[2]))
    my_place = jnp.where(seq == seats[1], 1, 0) + jnp.where(seq == seats[2], 2, 0)
    my_slot = HEADS_LOCAL * core + my_place
    my_near = head // 2
    own_source = jnp.logical_and(seated, near == my_near)

    targets = [
        (
            2 * near + slot // HEADS_LOCAL,
            seat_of(near // 4, slot // HEADS_LOCAL, slot % HEADS_LOCAL),
        )
        for slot in range(HEADS_NEAR)
    ]

    def other(device):
        return jnp.logical_or(device[0] != head, device[1] != seq)

    def neighbour(step):
        return lax.rem(near + step, NEAR)

    barrier = pltpu.get_barrier_semaphore()

    def greet(device):
        pl.semaphore_signal(barrier, inc=1, device_id=device, device_id_type=MESH)

    @pl.when(seated)
    def _():
        @pl.loop(0, STEPS)
        def _(turn):
            mini = jnp.where(lax.rem(turn, 2) == 0, turn // 2, STEPS - 1 - turn // 2)
            device = (lax.rem(mini, 2) * NEAR + my_near, mini // 2)

            @pl.when(other(device))
            def _():
                greet(device)

        @pl.loop(1, CHAIN)
        def _(step):
            greet((head, lax.rem(seq + step, CHAIN)))

    for device in targets:

        @pl.when(other(device))
        def _():
            greet(device)

    @pl.loop(1, NEAR)
    def _(step):
        greet((upper * NEAR + neighbour(step), seq))

    fetches[0].wait()
    left_lanes = lanes_left(MINI)
    for place in range(HEADS_LOCAL):
        row = jnp.broadcast_to(rates_ref[place : place + 1], (8, LANES))
        turned_row = pltpu.roll(row, D_HEAD, 1)
        rates_out[place, 0] = jnp.where(left_lanes[:8], row, turned_row)
        rates_out[place, 1] = jnp.where(left_lanes[:8], turned_row, row)

    expected = NEAR - 1 + HEADS_NEAR + HEADS_LOCAL
    expected = expected + jnp.where(seated, STEPS - 1, 0) - jnp.where(own_source, 2, 0)
    pl.semaphore_wait(barrier, expected)

    sources = (query_ref, key_ref, value_ref)

    def wide(index):
        return pl.ds(pl.multiple_of(index * WIDE, LANES), WIDE)

    def rows_of(index):
        return pl.ds(pl.multiple_of(index * 8, 8), 8)

    def exchange_copy(array, step):
        target = neighbour(step)
        return pltpu.make_async_remote_copy(
            src_ref=sources[array].at[:, wide(target)],
            dst_ref=gathered.at[array, rows_of(near)],
            send_sem=send_a.at[array],
            recv_sem=recv_a.at[array],
            device_id=(upper * NEAR + target, seq),
            device_id_type=MESH,
        )

    def own_exchange(array):
        return pltpu.make_async_copy(
            sources[array].at[:, wide(near)], gathered.at[array, rows_of(near)], recv_a.at[array]
        )

    @pl.loop(1, NEAR)
    def _(step):
        for array in range(3):
            exchange_copy(array, step).start()

    for array in range(3):
        own_exchange(array).start()

    def rates_copy(place):
        return pltpu.make_async_remote_copy(
            src_ref=rates_out.at[place],
            dst_ref=rates_in.at[pl.ds(2 * seq, 2)],
            send_sem=send_r.at[place],
            recv_sem=recv_r.at[seq],
            device_id=(head, seats[place]),
            device_id_type=MESH,
        )

    for place in range(HEADS_LOCAL):

        @pl.when(seq != seats[place])
        def _():
            rates_copy(place).start()

    for array in range(3):
        pltpu.make_async_remote_copy(
            src_ref=gathered.at[array],
            dst_ref=gathered.at[array],
            send_sem=send_a.at[array],
            recv_sem=recv_a.at[array],
            device_id=(upper * NEAR + neighbour(1), seq),
            device_id_type=MESH,
        ).wait_recv()

    def relay_copy(slot):
        return pltpu.make_async_remote_copy(
            src_ref=packed.at[slot],
            dst_ref=tokens.at[own_mini],
            send_sem=send_b.at[slot],
            recv_sem=recv_b.at[own_mini],
            device_id=targets[slot],
            device_id_type=MESH,
        )

    for tile in range(HEADS_NEAR // 2):
        columns = slice(tile * LANES, (tile + 1) * LANES)
        queries, keys, values = [gathered[array, :, columns].astype(F32) for array in range(3)]
        queries_turned, keys_turned, values_turned = [
            pltpu.roll(rows, D_HEAD, 1) for rows in (queries, keys, values)
        ]
        first_keys = jnp.where(left_lanes, keys, values_turned)
        second_keys = jnp.where(left_lanes, keys_turned, values)
        half = MINI // 2
        first_queries = jnp.where(left_lanes[:half], queries[:half], queries_turned[half:])
        second_queries = jnp.where(left_lanes[:half], queries_turned[:half], queries[half:])
        packed[2 * tile, :MINI] = first_keys.astype(BF16)
        packed[2 * tile, MINI:] = first_queries.astype(BF16)
        packed[2 * tile + 1, :MINI] = second_keys.astype(BF16)
        packed[2 * tile + 1, MINI:] = second_queries.astype(BF16)

    late = jnp.minimum(own_mini, STEPS - 1 - own_mini)
    pl.delay(jnp.where(seated, 0, late) * SPACING_NS)

    for slot in range(HEADS_NEAR):

        @pl.when(other(targets[slot]))
        def _():
            relay_copy(slot).start()

    for fetch in fetches[1:]:
        fetch.wait()

    @pl.when(seated)
    def _():
        @pl.when(own_source)
        def _():
            tokens[own_mini] = packed[my_slot]

        rates_in[pl.ds(2 * seq, 2)] = rates_out[my_place]

        row = lax.broadcasted_iota(jnp.int32, (LANES, LANES), 0)
        col = lax.broadcasted_iota(jnp.int32, (LANES, LANES), 1)
        ahead = jnp.logical_and(jnp.logical_and(row < 64, col < 64), row <= col)
        back = jnp.logical_and(jnp.logical_and(row >= 64, col >= 64), row >= col)
        causal[...] = jnp.where(jnp.logical_or(ahead, back), 1.0, 0.0)
        halves[...] = jnp.where((row < 64) == (col < 64), 1.0, 0.0)

        first = first_ref[my_place]
        both = jnp.concatenate([first, first], axis=0)
        state_one[...] = both.T
        second = second_ref[my_place]
        second = second - jnp.mean(second, axis=0, keepdims=True)
        doubled = jnp.concatenate([second, second], axis=0)
        state_two[...] = doubled.T
        second_hist[0] = doubled.astype(BF16)

        def spread_column(row_values, length):
            return jnp.broadcast_to(row_values, (LANES, length)).T

        bias_one[...] = spread_column(first_bias_ref[pl.ds(my_place, 1), :], INNER)
        second_bias = second_bias_ref[pl.ds(my_place, 1), :]
        second_bias = second_bias - jnp.mean(second_bias, axis=1, keepdims=True)
        bias_two[0] = spread_column(second_bias, D_HEAD)
        gain_rows[...] = spread_column(gain_ref[pl.ds(my_place, 1), :], D_HEAD)
        shift_rows[...] = spread_column(shift_ref[pl.ds(my_place, 1), :], D_HEAD)

        def await_step(step):
            for mini in (step, STEPS - 1 - step):

                @pl.when(jnp.logical_not(jnp.logical_and(own_source, mini == own_mini)))
                def _():
                    pltpu.make_async_remote_copy(
                        src_ref=packed.at[0],
                        dst_ref=tokens.at[mini],
                        send_sem=send_b.at[0],
                        recv_sem=recv_b.at[mini],
                        device_id=(lax.rem(mini, 2) * NEAR + my_near, mini // 2),
                        device_id_type=MESH,
                    ).wait_recv()

        def await_rates(block):
            @pl.when(block != seq)
            def _():
                pltpu.make_async_remote_copy(
                    src_ref=rates_out.at[0],
                    dst_ref=rates_in.at[pl.ds(2 * block, 2)],
                    send_sem=send_r.at[0],
                    recv_sem=recv_r.at[block],
                    device_id=(head, block),
                    device_id_type=MESH,
                ).wait_recv()

        def load_step(step):
            back = STEPS - 1 - step
            kv_f = tokens[step, :MINI]
            kv_b = tokens[back, :MINI]
            left = lanes_left(MINI)
            keys_back = pltpu.roll(kv_b.astype(F32), D_HEAD, 1)
            keys_bd = jnp.concatenate(
                [jnp.where(left, kv_f.astype(F32), 0.0), jnp.where(left, 0.0, keys_back)], axis=0
            ).astype(BF16)
            pieces = []
            for mini in (step, back):
                pair = tokens[mini, MINI:].astype(F32)
                pieces += [pair, pltpu.roll(pair, D_HEAD, 1)]
            kv_turned = jnp.concatenate([kv_f, kv_b], axis=0).T.astype(F32)
            queries = jnp.concatenate(pieces, axis=0).astype(BF16).T.astype(F32)[:D_HEAD]
            target = kv_turned[D_HEAD:] - kv_turned[:D_HEAD]
            rate = jnp.where(left[:8], rates_in[step], rates_in[back])
            keys_turned = spread_halves(kv_turned[:D_HEAD]).astype(BF16)
            queries_turned = spread_halves(queries).astype(BF16)
            return (keys_bd, keys_turned, queries_turned, target, rate)

        def store_step(loaded):
            bd_key[...] = loaded[0]
            turned_query[...] = loaded[2]
            target_rows[...] = gain_rows[...] * (shift_rows[...] - loaded[3])
            rate_rows[...] = loaded[4]

        def finish(step, dual_two):
            mean = row_mean(dual_two)
            spread = lax.rsqrt(row_mean(dual_two * dual_two) - mean * mean + EPS)
            fitted = gain_rows[...] * ((dual_two - mean) * spread) + shift_rows[...]
            kept_rows[step] = fitted
            total = fitted + pltpu.roll(kept_rows[STEPS - 1 - step], D_HEAD, 1)
            at_left = lax.rem(my_slot, 2) == 0
            total = jnp.concatenate(
                [jnp.where(at_left, total, 0.0), jnp.where(at_left, 0.0, total)], axis=0
            )
            turned = total.astype(BF16).T
            blocks_out[step] = turned[:MINI]
            blocks_out[STEPS - 1 - step] = turned[MINI:]

        def slot_of(step):
            return lax.rem(step, HISTORY)

        def attend_dual(step):
            slot = slot_of(step)
            dual_act = dual_act_ref[lax.rem(step, 2)]
            mask = causal[...]
            read = dot(second_hist[slot], dual_act, (1, 0))
            attend = dot(act_ref[slot].T, dual_act, (1, 0))
            return (own_half(read) + bias_two[slot], (attend * mask + mask).astype(BF16))

        half = INNER // 2
        row_halves = (slice(0, half), slice(half, INNER))

        def widen(grad_one, within, base, bias, ones_bf):
            sums = jnp.concatenate([within, ones_bf], axis=1)
            falls = [dot(grad_one[rows], sums, (1, 0)) for rows in row_halves]
            acts = [
                gelu(base[rows] - fall[:, :LANES]).astype(BF16)
                for rows, fall in zip(row_halves, falls)
            ]
            biases = [bias[rows] - fall[:, LANES:] for rows, fall in zip(row_halves, falls)]
            return (acts, biases)

        def advance(step):
            slot = slot_of(step)
            before = step + HISTORY - 2
            act = act_ref[slot]
            second_turned = second_hist[slot]
            target = target_rows[...]
            gain = gain_rows[...]
            gain_sq = gain * gain
            rate = rate_rows[0:1]
            bias_two_now = bias_two[slot]
            ones_bd = halves[...]
            ones_bf = ones_bd.astype(BF16)
            mask = causal[...]

            pre_two = (
                jnp.where(
                    lanes_left(D_HEAD),
                    dot(second_turned[:D_HEAD], act, (1, 0)),
                    dot(second_turned[D_HEAD:], act, (1, 0)),
                )
                + bias_two_now
            )

            last_read = read_ref[...]
            last_fall = dot(grad_two_ref[slot_of(step + HISTORY - 3)], attend_ref[...], (1, 0))
            dual_acts, biases = widen(
                grad_one_ref[...], within_ref[...], dual_base[...], bias_one[...], ones_bf
            )

            later = jnp.minimum(step + 1, STEPS - 1)
            loaded = load_step(later)
            keys_bd = bd_key[...]
            queries_turned = turned_query[...]
            state_one_now = state_one[...]
            high = state_one_now.astype(BF16)
            low = (state_one_now - high.astype(F32)).astype(BF16)
            reads = jnp.concatenate([loaded[1], queries_turned], axis=1)
            reads = jnp.concatenate([reads, reads], axis=0)
            within_both = dot(
                jnp.concatenate([keys_bd, jnp.zeros_like(keys_bd)], axis=1), reads, (1, 0)
            )
            between = (within_both[:, :LANES] + ones_bd).astype(BF16)
            within = (within_both[:, LANES:] * mask + mask).astype(BF16)

            scaled = gain_sq * pre_two
            mean = row_mean(pre_two)
            sum_scaled = row_mean(scaled)
            sum_square = row_mean(pre_two * pre_two)
            sum_scaled_sq = row_mean(scaled * pre_two)
            sum_target = row_mean(target * pre_two)
            mean_gain = row_mean(gain_sq)
            mean_target = row_mean(target)
            inverse = lax.rsqrt(sum_square - mean * mean + EPS)
            centred_scaled = sum_scaled - mean * mean_gain
            mean_a = inverse * centred_scaled + mean_target
            mean_an = inverse * (
                inverse * (sum_scaled_sq - mean * (sum_scaled + centred_scaled))
                + (sum_target - mean * mean_target)
            )
            weight = inverse * rate
            grad_two = (
                (pre_two - mean) * (inverse * gain_sq - inverse * mean_an) + (target - mean_a)
            ) * weight
            grad_two = grad_two.astype(BF16)
            grad_two_bd = spread_halves(grad_two)
            state_two_now = state_two[...]
            state_two_bf = state_two_now.astype(BF16)
            grads_one = [
                (dot(state_two_bf[rows], grad_two_bd, (1, 0)) * slope_ref[rows, :]).astype(BF16)
                for rows in row_halves
            ]

            finish(jnp.maximum(step - 3, 0), last_read - last_fall)

            state_two_new = state_two_now - dot(act, grad_two_bd.T, (1, 0))
            bias_two_new = bias_two_now - dot(grad_two, ones_bf, (1, 0))
            dual_read, attend = attend_dual(before)
            read_ref[...] = dual_read
            attend_ref[...] = attend

            seen = dot(jnp.concatenate([high, low], axis=1), reads, (1, 0))
            moves = jnp.concatenate([between, keys_bd], axis=1)
            next_slot = slot_of(step + 1)
            for part in range(2):
                rows = row_halves[part]
                fall = dot(grads_one[part], moves, (1, 0))
                state_one[rows, :] = state_one_now[rows] - fall[:, LANES:]
                pre_one = seen[rows, :LANES] + biases[part] - fall[:, :LANES]
                act_next, slope_next = gelu_and_slope(pre_one)
                act_ref[next_slot, rows, :] = act_next.astype(BF16)
                slope_ref[rows, :] = slope_next
                dual_base[rows, :] = seen[rows, LANES:] + biases[part]
                bias_one[rows, :] = biases[part]
                grad_one_ref[rows, :] = grads_one[part]
                dual_act_ref[lax.rem(step + 1, 2), rows, :] = dual_acts[part]

            state_two[...] = state_two_new
            second_hist[next_slot] = state_two_new.astype(BF16).T
            bias_two[next_slot] = bias_two_new
            grad_two_ref[slot] = grad_two
            within_ref[...] = within
            store_step(loaded)

        def emit(step, read, attend):
            finish(step, read - dot(grad_two_ref[slot_of(step)], attend, (1, 0)))

        def return_copy(mini):
            return pltpu.make_async_remote_copy(
                src_ref=blocks_out.at[mini],
                dst_ref=returned.at[my_slot],
                send_sem=send_c.at[mini],
                recv_sem=recv_c.at[my_slot],
                device_id=(lax.rem(mini, 2) * NEAR + my_near, mini // 2),
                device_id_type=MESH,
            )

        def is_own(mini):
            return jnp.logical_and(own_source, mini == own_mini)

        def give_back(mini):
            @pl.when(jnp.logical_not(is_own(mini)))
            def _():
                return_copy(mini).start()

            @pl.when(is_own(mini))
            def _():
                returned[my_slot] = blocks_out[mini]

        await_rates(0)
        await_rates(CHAIN - 1)
        await_step(0)
        begun = load_step(0)
        store_step(begun)
        high = state_one[...].astype(BF16)
        low = (state_one[...] - high.astype(F32)).astype(BF16)
        act, slope = gelu_and_slope(
            dot(high, begun[1], (1, 0)) + dot(low, begun[1], (1, 0)) + bias_one[...]
        )
        act_ref[0] = act.astype(BF16)
        slope_ref[...] = slope
        grad_one_ref[...] = jnp.zeros_like(grad_one_ref)
        within_ref[...] = jnp.zeros_like(within_ref)

        @pl.loop(0, STEPS)
        def _(step):
            later = step + 1

            @pl.when(later < STEPS // 2)
            def _():
                await_step(later)

                @pl.when(lax.rem(later, 2) == 0)
                def _():
                    await_rates(later // 2)
                    await_rates(CHAIN - 1 - later // 2)

            advance(step)
            done = step - 3

            @pl.when(done >= STEPS // 2)
            def _():
                give_back(done)
                give_back(STEPS - 1 - done)

        last = STEPS - 1
        dual_acts, _ = widen(
            grad_one_ref[...],
            within_ref[...],
            dual_base[...],
            bias_one[...],
            halves[...].astype(BF16),
        )
        later = attend_dual(last - 1)
        emit(last - 2, read_ref[...], attend_ref[...])
        for part in range(2):
            dual_act_ref[last % 2, row_halves[part], :] = dual_acts[part]
        latest = attend_dual(last)
        emit(last - 1, *later)
        emit(last, *latest)
        for step in (last, last - 1, last - 2):
            give_back(step)
            give_back(STEPS - 1 - step)

    for slot in range(HEADS_NEAR):

        @pl.when(other(targets[slot]))
        def _():
            pltpu.make_async_remote_copy(
                src_ref=blocks_out.at[0],
                dst_ref=returned.at[slot],
                send_sem=send_c.at[0],
                recv_sem=recv_c.at[slot],
                device_id=targets[slot],
                device_id_type=MESH,
            ).wait_recv()

    for tile in range(HEADS_NEAR // 2):
        columns = slice(tile * LANES, (tile + 1) * LANES)
        relay_out[:, columns] = jnp.where(left_lanes, returned[2 * tile], returned[2 * tile + 1])

    def spread_copy(step):
        target = neighbour(step)
        return pltpu.make_async_remote_copy(
            src_ref=relay_out.at[rows_of(target)],
            dst_ref=landed.at[:, wide(near)],
            send_sem=send_d.at[0],
            recv_sem=recv_d.at[0],
            device_id=(upper * NEAR + target, seq),
            device_id_type=MESH,
        )

    @pl.loop(1, NEAR)
    def _(step):
        spread_copy(step).start()

    pltpu.make_async_copy(
        relay_out.at[rows_of(near)], landed.at[:, wide(near)], recv_d.at[0]
    ).start()
    pltpu.make_async_remote_copy(
        src_ref=landed,
        dst_ref=landed,
        send_sem=send_d.at[0],
        recv_sem=recv_d.at[0],
        device_id=(upper * NEAR + neighbour(1), seq),
        device_id_type=MESH,
    ).wait_recv()

    sent = pl.ds(0, (NEAR - 1) * WIDE)
    for array in range(3):
        pltpu.make_async_remote_copy(
            src_ref=sources[array].at[:, sent],
            dst_ref=sources[array].at[:, sent],
            send_sem=send_a.at[array],
            recv_sem=recv_a.at[array],
            device_id=(upper * NEAR + neighbour(1), seq),
            device_id_type=MESH,
        ).wait_send()
    pltpu.make_async_remote_copy(
        src_ref=relay_out.at[pl.ds(0, 8 * (NEAR - 1))],
        dst_ref=relay_out.at[pl.ds(0, 8 * (NEAR - 1))],
        send_sem=send_d.at[0],
        recv_sem=recv_d.at[0],
        device_id=(upper * NEAR + neighbour(1), seq),
        device_id_type=MESH,
    ).wait_send()

    for place in range(HEADS_LOCAL):

        @pl.when(seq != seats[place])
        def _():
            rates_copy(place).wait_send()

    for slot in range(HEADS_NEAR):

        @pl.when(other(targets[slot]))
        def _():
            relay_copy(slot).wait_send()

    @pl.when(seated)
    def _():
        @pl.loop(0, STEPS)
        def _(mini):
            device = (lax.rem(mini, 2) * NEAR + my_near, mini // 2)

            @pl.when(other(device))
            def _():
                pltpu.make_async_remote_copy(
                    src_ref=blocks_out.at[mini],
                    dst_ref=returned.at[my_slot],
                    send_sem=send_c.at[mini],
                    recv_sem=recv_c.at[my_slot],
                    device_id=device,
                    device_id_type=MESH,
                ).wait_send()


def local(*arrays):
    arrays = list(arrays)
    arrays[4] = arrays[4].T
    arrays[7] = jnp.swapaxes(arrays[7], 1, 2)
    gate = arrays.pop(3)
    anywhere = pl.BlockSpec(memory_space=pl.ANY)
    dma = pltpu.SemaphoreType.DMA
    summed = pl.pallas_call(
        kernel,
        out_shape=jax.ShapeDtypeStruct((8, TILES * LANES), BF16),
        in_specs=[anywhere] * len(arrays),
        out_specs=anywhere,
        scratch_shapes=[
            *[pltpu.VMEM(array.shape, array.dtype) for array in arrays[3:]],
            pltpu.VMEM((3, MINI, WIDE), BF16),
            pltpu.VMEM((HEADS_NEAR, PACKED, LANES), BF16),
            pltpu.VMEM((HEADS_LOCAL, 2, 8, LANES), F32),
            pltpu.VMEM((STEPS, 8, LANES), F32),
            pltpu.VMEM((STEPS, PACKED, LANES), BF16),
            pltpu.VMEM((STEPS, MINI, LANES), BF16),
            pltpu.VMEM((HEADS_NEAR, MINI, LANES), BF16),
            pltpu.VMEM((MINI, WIDE), BF16),
            pltpu.VMEM((STEPS, D_HEAD, LANES), F32),
            pltpu.VMEM((LANES, LANES), BF16),
            pltpu.VMEM((LANES, LANES), BF16),
            pltpu.VMEM((8, LANES), F32),
            pltpu.VMEM((D_HEAD, LANES), F32),
            pltpu.VMEM((LANES, LANES), F32),
            pltpu.VMEM((LANES, LANES), F32),
            pltpu.VMEM((INNER, LANES), F32),
            pltpu.VMEM((INNER, LANES), F32),
            pltpu.VMEM((INNER, LANES), F32),
            pltpu.VMEM((HISTORY, LANES, INNER), BF16),
            pltpu.VMEM((HISTORY, D_HEAD, LANES), F32),
            pltpu.VMEM((D_HEAD, LANES), F32),
            pltpu.VMEM((D_HEAD, LANES), F32),
            pltpu.VMEM((INNER, LANES), F32),
            pltpu.VMEM((INNER, LANES), F32),
            pltpu.VMEM((2, INNER, LANES), BF16),
            pltpu.VMEM((HISTORY, INNER, LANES), BF16),
            pltpu.VMEM((HISTORY, D_HEAD, LANES), BF16),
            pltpu.VMEM((INNER, LANES), BF16),
            pltpu.VMEM((LANES, LANES), BF16),
            pltpu.VMEM((D_HEAD, LANES), F32),
            pltpu.VMEM((LANES, LANES), BF16),
            dma((7,)),
            dma((3,)),
            dma((3,)),
            dma((HEADS_NEAR,)),
            dma((STEPS,)),
            dma((HEADS_LOCAL,)),
            dma((CHAIN,)),
            dma((STEPS,)),
            dma((HEADS_NEAR,)),
            dma((1,)),
            dma((1,)),
        ],
        compiler_params=pltpu.CompilerParams(collective_id=0, has_side_effects=True),
    )(*arrays)
    return (gate.astype(F32) * summed.astype(F32)).astype(BF16)


def solution(mesh):
    rows = P(("seq", "head"), None)
    in_specs = (
        rows,
        rows,
        rows,
        rows,
        P("seq", "head"),
        P("head", None, None),
        P("head", None),
        P("head", None, None),
        P("head", None),
        P("head", None),
        P("head", None),
    )
    return jax.shard_map(local, mesh=mesh, in_specs=in_specs, out_specs=rows, check_vma=False)
```

```python
import functools

import jax
import jax.numpy as jnp
from jax import lax
from jax.experimental import pallas as pl
from jax.experimental.pallas import tpu as pltpu
from jax.sharding import PartitionSpec as P

D_HEAD = 64
INNER = 256
MINI = 64
STEPS = 64
LANES = 128
NEAR = 8
CHAIN = 32
HEADS_LOCAL = 3
HEADS_NEAR = 6
WIDE = HEADS_NEAR * D_HEAD
TILES = 24

EPS = 1e-06
ROOT = 0.7978845608028654
CUBE = 0.044715
MESH = pl.DeviceIdType.MESH
F32 = jnp.float32
BF16 = jnp.bfloat16

PACKED = MINI + MINI // 2
HISTORY = 4
SPACING_NS = 625

SEATS = (((1, 7, 12), (2, 4, 15)), ((29, 26, 16), (30, 25, 19)))


def dot(left, right, dims):
    return lax.dot_general(
        left, right, (((dims[0],), (dims[1],)), ((), ())), preferred_element_type=F32
    )


def gelu(values):
    squared = values * values
    tanh_term = jnp.tanh(values * (ROOT + (ROOT * CUBE) * squared))
    return values * (0.5 + 0.5 * tanh_term)


def gelu_and_slope(values):
    squared = values * values
    tanh_term = jnp.tanh(values * (ROOT + (ROOT * CUBE) * squared))
    half = 0.5 + 0.5 * tanh_term
    slope = half + values * (half * (1.0 - tanh_term)) * (ROOT + (3.0 * ROOT * CUBE) * squared)
    return (values * half, slope)


def row_mean(values):
    rows = values.shape[0]
    while rows > 8:
        rows //= 2
        values = values[:rows] + values[rows:]
    return jnp.sum(values, axis=0, keepdims=True) * (1.0 / D_HEAD)


def lanes_left(rows):
    return lax.broadcasted_iota(jnp.int32, (rows, LANES), 1) < D_HEAD


def own_half(stacked):
    return jnp.where(lanes_left(D_HEAD), stacked[:D_HEAD], stacked[D_HEAD:])


def spread_halves(rows):
    left = lanes_left(D_HEAD)
    zero = jnp.zeros_like(rows)
    return jnp.concatenate([jnp.where(left, rows, zero), jnp.where(left, zero, rows)], axis=0)


def seat_of(upper, core, place):
    lower_seat = jnp.where(core == 0, SEATS[0][0][place], SEATS[0][1][place])
    upper_seat = jnp.where(core == 0, SEATS[1][0][place], SEATS[1][1][place])
    return jnp.where(upper == 0, lower_seat, upper_seat)


def kernel(
    query_ref,
    key_ref,
    value_ref,
    rates_far,
    first_far,
    first_bias_far,
    second_far,
    second_bias_far,
    gain_far,
    shift_far,
    landed,
    rates_ref,
    first_ref,
    first_bias_ref,
    second_ref,
    second_bias_ref,
    gain_ref,
    shift_ref,
    gathered,
    packed,
    rates_out,
    rates_in,
    tokens,
    blocks_out,
    returned,
    relay_out,
    kept_rows,
    bd_key,
    turned_query,
    rate_rows,
    target_rows,
    causal,
    halves,
    state_one,
    bias_one,
    state_two,
    second_hist,
    bias_two,
    gain_rows,
    shift_rows,
    slope_ref,
    dual_base,
    dual_act_ref,
    act_ref,
    grad_two_ref,
    grad_one_ref,
    within_ref,
    read_ref,
    attend_ref,
    load_sem,
    send_a,
    recv_a,
    send_b,
    recv_b,
    send_r,
    recv_r,
    send_c,
    recv_c,
    send_d,
    recv_d,
):
    fetches = [
        pltpu.make_async_copy(far, here, load_sem.at[place])
        for place, (far, here) in enumerate(
            (
                (rates_far, rates_ref),
                (first_far, first_ref),
                (first_bias_far, first_bias_ref),
                (second_far, second_ref),
                (second_bias_far, second_bias_ref),
                (gain_far, gain_ref),
                (shift_far, shift_ref),
            )
        )
    ]
    for fetch in fetches:
        fetch.start()

    head = lax.axis_index("head")
    seq = lax.axis_index("seq")
    core = lax.rem(head, 2)
    upper = head // NEAR
    near = lax.rem(head, NEAR)
    own_mini = 2 * seq + upper
    seats = [seat_of(upper, core, place) for place in range(HEADS_LOCAL)]
    seated = jnp.logical_or(seq == seats[0], jnp.logical_or(seq == seats[1], seq == seats[2]))
    my_place = jnp.where(seq == seats[1], 1, 0) + jnp.where(seq == seats[2], 2, 0)
    my_slot = HEADS_LOCAL * core + my_place
    my_near = head // 2
    own_source = jnp.logical_and(seated, near == my_near)

    targets = [
        (
            2 * near + slot // HEADS_LOCAL,
            seat_of(near // 4, slot // HEADS_LOCAL, slot % HEADS_LOCAL),
        )
        for slot in range(HEADS_NEAR)
    ]

    def other(device):
        return jnp.logical_or(device[0] != head, device[1] != seq)

    def neighbour(step):
        return lax.rem(near + step, NEAR)

    barrier = pltpu.get_barrier_semaphore()

    def greet(device):
        pl.semaphore_signal(barrier, inc=1, device_id=device, device_id_type=MESH)

    @pl.when(seated)
    def _():
        @pl.loop(0, STEPS)
        def _(turn):
            mini = jnp.where(lax.rem(turn, 2) == 0, turn // 2, STEPS - 1 - turn // 2)
            device = (lax.rem(mini, 2) * NEAR + my_near, mini // 2)

            @pl.when(other(device))
            def _():
                greet(device)

        @pl.loop(1, CHAIN)
        def _(step):
            greet((head, lax.rem(seq + step, CHAIN)))

    for device in targets:

        @pl.when(other(device))
        def _():
            greet(device)

    @pl.loop(1, NEAR)
    def _(step):
        greet((upper * NEAR + neighbour(step), seq))

    fetches[0].wait()
    left_lanes = lanes_left(MINI)
    for place in range(HEADS_LOCAL):
        row = jnp.broadcast_to(rates_ref[place : place + 1], (8, LANES))
        turned_row = pltpu.roll(row, D_HEAD, 1)
        rates_out[place, 0] = jnp.where(left_lanes[:8], row, turned_row)
        rates_out[place, 1] = jnp.where(left_lanes[:8], turned_row, row)

    expected = NEAR - 1 + HEADS_NEAR + HEADS_LOCAL
    expected = expected + jnp.where(seated, STEPS - 1, 0) - jnp.where(own_source, 2, 0)
    pl.semaphore_wait(barrier, expected)

    sources = (query_ref, key_ref, value_ref)

    def wide(index):
        return pl.ds(pl.multiple_of(index * WIDE, LANES), WIDE)

    def rows_of(index):
        return pl.ds(pl.multiple_of(index * 8, 8), 8)

    def exchange_copy(array, step):
        target = neighbour(step)
        return pltpu.make_async_remote_copy(
            src_ref=sources[array].at[:, wide(target)],
            dst_ref=gathered.at[array, rows_of(near)],
            send_sem=send_a.at[array],
            recv_sem=recv_a.at[array],
            device_id=(upper * NEAR + target, seq),
            device_id_type=MESH,
        )

    def own_exchange(array):
        return pltpu.make_async_copy(
            sources[array].at[:, wide(near)], gathered.at[array, rows_of(near)], recv_a.at[array]
        )

    @pl.loop(1, NEAR)
    def _(step):
        for array in range(3):
            exchange_copy(array, step).start()

    for array in range(3):
        own_exchange(array).start()

    def rates_copy(place):
        return pltpu.make_async_remote_copy(
            src_ref=rates_out.at[place],
            dst_ref=rates_in.at[pl.ds(2 * seq, 2)],
            send_sem=send_r.at[place],
            recv_sem=recv_r.at[seq],
            device_id=(head, seats[place]),
            device_id_type=MESH,
        )

    for place in range(HEADS_LOCAL):

        @pl.when(seq != seats[place])
        def _():
            rates_copy(place).start()

    for array in range(3):
        pltpu.make_async_remote_copy(
            src_ref=gathered.at[array],
            dst_ref=gathered.at[array],
            send_sem=send_a.at[array],
            recv_sem=recv_a.at[array],
            device_id=(upper * NEAR + neighbour(1), seq),
            device_id_type=MESH,
        ).wait_recv()

    def relay_copy(slot):
        return pltpu.make_async_remote_copy(
            src_ref=packed.at[slot],
            dst_ref=tokens.at[own_mini],
            send_sem=send_b.at[slot],
            recv_sem=recv_b.at[own_mini],
            device_id=targets[slot],
            device_id_type=MESH,
        )

    for tile in range(HEADS_NEAR // 2):
        columns = slice(tile * LANES, (tile + 1) * LANES)
        queries, keys, values = [gathered[array, :, columns].astype(F32) for array in range(3)]
        queries_turned, keys_turned, values_turned = [
            pltpu.roll(rows, D_HEAD, 1) for rows in (queries, keys, values)
        ]
        first_keys = jnp.where(left_lanes, keys, values_turned)
        second_keys = jnp.where(left_lanes, keys_turned, values)
        half = MINI // 2
        first_queries = jnp.where(left_lanes[:half], queries[:half], queries_turned[half:])
        second_queries = jnp.where(left_lanes[:half], queries_turned[:half], queries[half:])
        packed[2 * tile, :MINI] = first_keys.astype(BF16)
        packed[2 * tile, MINI:] = first_queries.astype(BF16)
        packed[2 * tile + 1, :MINI] = second_keys.astype(BF16)
        packed[2 * tile + 1, MINI:] = second_queries.astype(BF16)

    late = jnp.minimum(own_mini, STEPS - 1 - own_mini)
    pl.delay(jnp.where(seated, 0, late) * SPACING_NS)

    for slot in range(HEADS_NEAR):

        @pl.when(other(targets[slot]))
        def _():
            relay_copy(slot).start()

    for fetch in fetches[1:]:
        fetch.wait()

    @pl.when(seated)
    def _():
        @pl.when(own_source)
        def _():
            tokens[own_mini] = packed[my_slot]

        rates_in[pl.ds(2 * seq, 2)] = rates_out[my_place]

        row = lax.broadcasted_iota(jnp.int32, (LANES, LANES), 0)
        col = lax.broadcasted_iota(jnp.int32, (LANES, LANES), 1)
        ahead = jnp.logical_and(jnp.logical_and(row < 64, col < 64), row <= col)
        back = jnp.logical_and(jnp.logical_and(row >= 64, col >= 64), row >= col)
        causal[...] = jnp.where(jnp.logical_or(ahead, back), 1.0, 0.0)
        halves[...] = jnp.where((row < 64) == (col < 64), 1.0, 0.0)

        first = first_ref[my_place]
        both = jnp.concatenate([first, first], axis=0)
        state_one[...] = both.T
        second = second_ref[my_place]
        second = second - jnp.mean(second, axis=0, keepdims=True)
        doubled = jnp.concatenate([second, second], axis=0)
        state_two[...] = doubled.T
        second_hist[0] = doubled.astype(BF16)

        def spread_column(row_values, length):
            return jnp.broadcast_to(row_values, (LANES, length)).T

        bias_one[...] = spread_column(first_bias_ref[pl.ds(my_place, 1), :], INNER)
        second_bias = second_bias_ref[pl.ds(my_place, 1), :]
        second_bias = second_bias - jnp.mean(second_bias, axis=1, keepdims=True)
        bias_two[0] = spread_column(second_bias, D_HEAD)
        gain_rows[...] = spread_column(gain_ref[pl.ds(my_place, 1), :], D_HEAD)
        shift_rows[...] = spread_column(shift_ref[pl.ds(my_place, 1), :], D_HEAD)

        def await_step(step):
            for mini in (step, STEPS - 1 - step):

                @pl.when(jnp.logical_not(jnp.logical_and(own_source, mini == own_mini)))
                def _():
                    pltpu.make_async_remote_copy(
                        src_ref=packed.at[0],
                        dst_ref=tokens.at[mini],
                        send_sem=send_b.at[0],
                        recv_sem=recv_b.at[mini],
                        device_id=(lax.rem(mini, 2) * NEAR + my_near, mini // 2),
                        device_id_type=MESH,
                    ).wait_recv()

        def await_rates(block):
            @pl.when(block != seq)
            def _():
                pltpu.make_async_remote_copy(
                    src_ref=rates_out.at[0],
                    dst_ref=rates_in.at[pl.ds(2 * block, 2)],
                    send_sem=send_r.at[0],
                    recv_sem=recv_r.at[block],
                    device_id=(head, block),
                    device_id_type=MESH,
                ).wait_recv()

        def load_step(step):
            back = STEPS - 1 - step
            kv_f = tokens[step, :MINI]
            kv_b = tokens[back, :MINI]
            left = lanes_left(MINI)
            keys_back = pltpu.roll(kv_b.astype(F32), D_HEAD, 1)
            keys_bd = jnp.concatenate(
                [jnp.where(left, kv_f.astype(F32), 0.0), jnp.where(left, 0.0, keys_back)], axis=0
            ).astype(BF16)
            pieces = []
            for mini in (step, back):
                pair = tokens[mini, MINI:].astype(F32)
                pieces += [pair, pltpu.roll(pair, D_HEAD, 1)]
            kv_turned = jnp.concatenate([kv_f, kv_b], axis=0).T.astype(F32)
            queries = jnp.concatenate(pieces, axis=0).astype(BF16).T.astype(F32)[:D_HEAD]
            target = kv_turned[D_HEAD:] - kv_turned[:D_HEAD]
            rate = jnp.where(left[:8], rates_in[step], rates_in[back])
            keys_turned = spread_halves(kv_turned[:D_HEAD]).astype(BF16)
            queries_turned = spread_halves(queries).astype(BF16)
            return (keys_bd, keys_turned, queries_turned, target, rate)

        def store_step(loaded):
            bd_key[...] = loaded[0]
            turned_query[...] = loaded[2]
            target_rows[...] = gain_rows[...] * (shift_rows[...] - loaded[3])
            rate_rows[...] = loaded[4]

        def finish(step, dual_two):
            mean = row_mean(dual_two)
            spread = lax.rsqrt(row_mean(dual_two * dual_two) - mean * mean + EPS)
            fitted = gain_rows[...] * ((dual_two - mean) * spread) + shift_rows[...]
            kept_rows[step] = fitted
            total = fitted + pltpu.roll(kept_rows[STEPS - 1 - step], D_HEAD, 1)
            at_left = lax.rem(my_slot, 2) == 0
            total = jnp.concatenate(
                [jnp.where(at_left, total, 0.0), jnp.where(at_left, 0.0, total)], axis=0
            )
            turned = total.astype(BF16).T
            blocks_out[step] = turned[:MINI]
            blocks_out[STEPS - 1 - step] = turned[MINI:]

        def slot_of(step):
            return lax.rem(step, HISTORY)

        def attend_dual(step):
            slot = slot_of(step)
            dual_act = dual_act_ref[lax.rem(step, 2)]
            mask = causal[...]
            read = dot(second_hist[slot], dual_act, (1, 0))
            attend = dot(act_ref[slot].T, dual_act, (1, 0))
            return (own_half(read) + bias_two[slot], (attend * mask + mask).astype(BF16))

        half = INNER // 2
        row_halves = (slice(0, half), slice(half, INNER))

        def widen(grad_one, within, base, bias, ones_bf):
            sums = jnp.concatenate([within, ones_bf], axis=1)
            falls = [dot(grad_one[rows], sums, (1, 0)) for rows in row_halves]
            acts = [
                gelu(base[rows] - fall[:, :LANES]).astype(BF16)
                for rows, fall in zip(row_halves, falls)
            ]
            biases = [bias[rows] - fall[:, LANES:] for rows, fall in zip(row_halves, falls)]
            return (acts, biases)

        def advance(step):
            slot = slot_of(step)
            before = step + HISTORY - 2
            act = act_ref[slot]
            second_turned = second_hist[slot]
            target = target_rows[...]
            gain = gain_rows[...]
            gain_sq = gain * gain
            rate = rate_rows[0:1]
            bias_two_now = bias_two[slot]
            ones_bd = halves[...]
            ones_bf = ones_bd.astype(BF16)
            mask = causal[...]

            pre_two = (
                jnp.where(
                    lanes_left(D_HEAD),
                    dot(second_turned[:D_HEAD], act, (1, 0)),
                    dot(second_turned[D_HEAD:], act, (1, 0)),
                )
                + bias_two_now
            )

            last_read = read_ref[...]
            last_fall = dot(grad_two_ref[slot_of(step + HISTORY - 3)], attend_ref[...], (1, 0))
            dual_acts, biases = widen(
                grad_one_ref[...], within_ref[...], dual_base[...], bias_one[...], ones_bf
            )

            later = jnp.minimum(step + 1, STEPS - 1)
            loaded = load_step(later)
            keys_bd = bd_key[...]
            queries_turned = turned_query[...]
            state_one_now = state_one[...]
            high = state_one_now.astype(BF16)
            low = (state_one_now - high.astype(F32)).astype(BF16)
            reads = jnp.concatenate([loaded[1], queries_turned], axis=1)
            reads = jnp.concatenate([reads, reads], axis=0)
            within_both = dot(
                jnp.concatenate([keys_bd, jnp.zeros_like(keys_bd)], axis=1), reads, (1, 0)
            )
            between = (within_both[:, :LANES] + ones_bd).astype(BF16)
            within = (within_both[:, LANES:] * mask + mask).astype(BF16)

            scaled = gain_sq * pre_two
            mean = row_mean(pre_two)
            sum_scaled = row_mean(scaled)
            sum_square = row_mean(pre_two * pre_two)
            sum_scaled_sq = row_mean(scaled * pre_two)
            sum_target = row_mean(target * pre_two)
            mean_gain = row_mean(gain_sq)
            mean_target = row_mean(target)
            inverse = lax.rsqrt(sum_square - mean * mean + EPS)
            centred_scaled = sum_scaled - mean * mean_gain
            mean_a = inverse * centred_scaled + mean_target
            mean_an = inverse * (
                inverse * (sum_scaled_sq - mean * (sum_scaled + centred_scaled))
                + (sum_target - mean * mean_target)
            )
            weight = inverse * rate
            grad_two = (
                (pre_two - mean) * (inverse * gain_sq - inverse * mean_an) + (target - mean_a)
            ) * weight
            grad_two = grad_two.astype(BF16)
            grad_two_bd = spread_halves(grad_two)
            state_two_now = state_two[...]
            state_two_bf = state_two_now.astype(BF16)
            grads_one = [
                (dot(state_two_bf[rows], grad_two_bd, (1, 0)) * slope_ref[rows, :]).astype(BF16)
                for rows in row_halves
            ]

            finish(jnp.maximum(step - 3, 0), last_read - last_fall)

            state_two_new = state_two_now - dot(act, grad_two_bd.T, (1, 0))
            bias_two_new = bias_two_now - dot(grad_two, ones_bf, (1, 0))
            dual_read, attend = attend_dual(before)
            read_ref[...] = dual_read
            attend_ref[...] = attend

            seen = dot(jnp.concatenate([high, low], axis=1), reads, (1, 0))
            moves = jnp.concatenate([between, keys_bd], axis=1)
            next_slot = slot_of(step + 1)
            for part in range(2):
                rows = row_halves[part]
                fall = dot(grads_one[part], moves, (1, 0))
                state_one[rows, :] = state_one_now[rows] - fall[:, LANES:]
                pre_one = seen[rows, :LANES] + biases[part] - fall[:, :LANES]
                act_next, slope_next = gelu_and_slope(pre_one)
                act_ref[next_slot, rows, :] = act_next.astype(BF16)
                slope_ref[rows, :] = slope_next
                dual_base[rows, :] = seen[rows, LANES:] + biases[part]
                bias_one[rows, :] = biases[part]
                grad_one_ref[rows, :] = grads_one[part]
                dual_act_ref[lax.rem(step + 1, 2), rows, :] = dual_acts[part]

            state_two[...] = state_two_new
            second_hist[next_slot] = state_two_new.astype(BF16).T
            bias_two[next_slot] = bias_two_new
            grad_two_ref[slot] = grad_two
            within_ref[...] = within
            store_step(loaded)

        def emit(step, read, attend):
            finish(step, read - dot(grad_two_ref[slot_of(step)], attend, (1, 0)))

        def return_copy(mini):
            return pltpu.make_async_remote_copy(
                src_ref=blocks_out.at[mini],
                dst_ref=returned.at[my_slot],
                send_sem=send_c.at[mini],
                recv_sem=recv_c.at[my_slot],
                device_id=(lax.rem(mini, 2) * NEAR + my_near, mini // 2),
                device_id_type=MESH,
            )

        def is_own(mini):
            return jnp.logical_and(own_source, mini == own_mini)

        def give_back(mini):
            @pl.when(jnp.logical_not(is_own(mini)))
            def _():
                return_copy(mini).start()

            @pl.when(is_own(mini))
            def _():
                returned[my_slot] = blocks_out[mini]

        await_rates(0)
        await_rates(CHAIN - 1)
        await_step(0)
        begun = load_step(0)
        store_step(begun)
        high = state_one[...].astype(BF16)
        low = (state_one[...] - high.astype(F32)).astype(BF16)
        act, slope = gelu_and_slope(
            dot(high, begun[1], (1, 0)) + dot(low, begun[1], (1, 0)) + bias_one[...]
        )
        act_ref[0] = act.astype(BF16)
        slope_ref[...] = slope
        grad_one_ref[...] = jnp.zeros_like(grad_one_ref)
        within_ref[...] = jnp.zeros_like(within_ref)

        @pl.loop(0, STEPS)
        def _(step):
            later = step + 1

            @pl.when(later < STEPS // 2)
            def _():
                await_step(later)

                @pl.when(lax.rem(later, 2) == 0)
                def _():
                    await_rates(later // 2)
                    await_rates(CHAIN - 1 - later // 2)

            advance(step)
            done = step - 3

            @pl.when(done >= STEPS // 2)
            def _():
                give_back(done)
                give_back(STEPS - 1 - done)

        last = STEPS - 1
        dual_acts, _ = widen(
            grad_one_ref[...],
            within_ref[...],
            dual_base[...],
            bias_one[...],
            halves[...].astype(BF16),
        )
        later = attend_dual(last - 1)
        emit(last - 2, read_ref[...], attend_ref[...])
        for part in range(2):
            dual_act_ref[last % 2, row_halves[part], :] = dual_acts[part]
        latest = attend_dual(last)
        emit(last - 1, *later)
        emit(last, *latest)
        for step in (last, last - 1, last - 2):
            give_back(step)
            give_back(STEPS - 1 - step)

    for slot in range(HEADS_NEAR):

        @pl.when(other(targets[slot]))
        def _():
            pltpu.make_async_remote_copy(
                src_ref=blocks_out.at[0],
                dst_ref=returned.at[slot],
                send_sem=send_c.at[0],
                recv_sem=recv_c.at[slot],
                device_id=targets[slot],
                device_id_type=MESH,
            ).wait_recv()

    for tile in range(HEADS_NEAR // 2):
        columns = slice(tile * LANES, (tile + 1) * LANES)
        relay_out[:, columns] = jnp.where(left_lanes, returned[2 * tile], returned[2 * tile + 1])

    def spread_copy(step):
        target = neighbour(step)
        return pltpu.make_async_remote_copy(
            src_ref=relay_out.at[rows_of(target)],
            dst_ref=landed.at[:, wide(near)],
            send_sem=send_d.at[0],
            recv_sem=recv_d.at[0],
            device_id=(upper * NEAR + target, seq),
            device_id_type=MESH,
        )

    @pl.loop(1, NEAR)
    def _(step):
        spread_copy(step).start()

    pltpu.make_async_copy(
        relay_out.at[rows_of(near)], landed.at[:, wide(near)], recv_d.at[0]
    ).start()
    pltpu.make_async_remote_copy(
        src_ref=landed,
        dst_ref=landed,
        send_sem=send_d.at[0],
        recv_sem=recv_d.at[0],
        device_id=(upper * NEAR + neighbour(1), seq),
        device_id_type=MESH,
    ).wait_recv()

    sent = pl.ds(0, (NEAR - 1) * WIDE)
    for array in range(3):
        pltpu.make_async_remote_copy(
            src_ref=sources[array].at[:, sent],
            dst_ref=sources[array].at[:, sent],
            send_sem=send_a.at[array],
            recv_sem=recv_a.at[array],
            device_id=(upper * NEAR + neighbour(1), seq),
            device_id_type=MESH,
        ).wait_send()
    pltpu.make_async_remote_copy(
        src_ref=relay_out.at[pl.ds(0, 8 * (NEAR - 1))],
        dst_ref=relay_out.at[pl.ds(0, 8 * (NEAR - 1))],
        send_sem=send_d.at[0],
        recv_sem=recv_d.at[0],
        device_id=(upper * NEAR + neighbour(1), seq),
        device_id_type=MESH,
    ).wait_send()

    for place in range(HEADS_LOCAL):

        @pl.when(seq != seats[place])
        def _():
            rates_copy(place).wait_send()

    for slot in range(HEADS_NEAR):

        @pl.when(other(targets[slot]))
        def _():
            relay_copy(slot).wait_send()

    @pl.when(seated)
    def _():
        @pl.loop(0, STEPS)
        def _(mini):
            device = (lax.rem(mini, 2) * NEAR + my_near, mini // 2)

            @pl.when(other(device))
            def _():
                pltpu.make_async_remote_copy(
                    src_ref=blocks_out.at[mini],
                    dst_ref=returned.at[my_slot],
                    send_sem=send_c.at[mini],
                    recv_sem=recv_c.at[my_slot],
                    device_id=device,
                    device_id_type=MESH,
                ).wait_send()


def local(*arrays):
    arrays = list(arrays)
    arrays[4] = arrays[4].T
    arrays[7] = jnp.swapaxes(arrays[7], 1, 2)
    gate = arrays.pop(3)
    anywhere = pl.BlockSpec(memory_space=pl.ANY)
    dma = pltpu.SemaphoreType.DMA
    summed = pl.pallas_call(
        kernel,
        out_shape=jax.ShapeDtypeStruct((8, TILES * LANES), BF16),
        in_specs=[anywhere] * len(arrays),
        out_specs=anywhere,
        scratch_shapes=[
            *[pltpu.VMEM(array.shape, array.dtype) for array in arrays[3:]],
            pltpu.VMEM((3, MINI, WIDE), BF16),
            pltpu.VMEM((HEADS_NEAR, PACKED, LANES), BF16),
            pltpu.VMEM((HEADS_LOCAL, 2, 8, LANES), F32),
            pltpu.VMEM((STEPS, 8, LANES), F32),
            pltpu.VMEM((STEPS, PACKED, LANES), BF16),
            pltpu.VMEM((STEPS, MINI, LANES), BF16),
            pltpu.VMEM((HEADS_NEAR, MINI, LANES), BF16),
            pltpu.VMEM((MINI, WIDE), BF16),
            pltpu.VMEM((STEPS, D_HEAD, LANES), F32),
            pltpu.VMEM((LANES, LANES), BF16),
            pltpu.VMEM((LANES, LANES), BF16),
            pltpu.VMEM((8, LANES), F32),
            pltpu.VMEM((D_HEAD, LANES), F32),
            pltpu.VMEM((LANES, LANES), F32),
            pltpu.VMEM((LANES, LANES), F32),
            pltpu.VMEM((INNER, LANES), F32),
            pltpu.VMEM((INNER, LANES), F32),
            pltpu.VMEM((INNER, LANES), F32),
            pltpu.VMEM((HISTORY, LANES, INNER), BF16),
            pltpu.VMEM((HISTORY, D_HEAD, LANES), F32),
            pltpu.VMEM((D_HEAD, LANES), F32),
            pltpu.VMEM((D_HEAD, LANES), F32),
            pltpu.VMEM((INNER, LANES), F32),
            pltpu.VMEM((INNER, LANES), F32),
            pltpu.VMEM((2, INNER, LANES), BF16),
            pltpu.VMEM((HISTORY, INNER, LANES), BF16),
            pltpu.VMEM((HISTORY, D_HEAD, LANES), BF16),
            pltpu.VMEM((INNER, LANES), BF16),
            pltpu.VMEM((LANES, LANES), BF16),
            pltpu.VMEM((D_HEAD, LANES), F32),
            pltpu.VMEM((LANES, LANES), BF16),
            dma((7,)),
            dma((3,)),
            dma((3,)),
            dma((HEADS_NEAR,)),
            dma((STEPS,)),
            dma((HEADS_LOCAL,)),
            dma((CHAIN,)),
            dma((STEPS,)),
            dma((HEADS_NEAR,)),
            dma((1,)),
            dma((1,)),
        ],
        compiler_params=pltpu.CompilerParams(collective_id=0, has_side_effects=True),
    )(*arrays)
    return (gate.astype(F32) * summed.astype(F32)).astype(BF16)


def solution(mesh):
    rows = P(("seq", "head"), None)
    in_specs = (
        rows,
        rows,
        rows,
        rows,
        P("seq", "head"),
        P("head", None, None),
        P("head", None),
        P("head", None, None),
        P("head", None),
        P("head", None),
        P("head", None),
    )
    return jax.shard_map(local, mesh=mesh, in_specs=in_specs, out_specs=rows, check_vma=False)
```

```python
import functools

import jax
import jax.numpy as jnp
from jax import lax
from jax.experimental import pallas as pl
from jax.experimental.pallas import tpu as pltpu
from jax.sharding import PartitionSpec as P

D_HEAD = 64
INNER = 256
MINI = 64
STEPS = 64
LANES = 128
NEAR = 8
CHAIN = 32
HEADS_LOCAL = 3
HEADS_NEAR = 6
WIDE = HEADS_NEAR * D_HEAD
TILES = 24

EPS = 1e-06
ROOT = 0.7978845608028654
CUBE = 0.044715
MESH = pl.DeviceIdType.MESH
F32 = jnp.float32
BF16 = jnp.bfloat16

PACKED = MINI + MINI // 2
HISTORY = 4
SPACING_NS = 612

SEATS = (((1, 7, 12), (2, 4, 15)), ((29, 26, 16), (30, 25, 19)))


def dot(left, right, dims):
    return lax.dot_general(
        left, right, (((dims[0],), (dims[1],)), ((), ())), preferred_element_type=F32
    )


def gelu(values):
    squared = values * values
    tanh_term = jnp.tanh(values * (ROOT + (ROOT * CUBE) * squared))
    return values * (0.5 + 0.5 * tanh_term)


def gelu_and_slope(values):
    squared = values * values
    tanh_term = jnp.tanh(values * (ROOT + (ROOT * CUBE) * squared))
    half = 0.5 + 0.5 * tanh_term
    slope = half + values * (half * (1.0 - tanh_term)) * (ROOT + (3.0 * ROOT * CUBE) * squared)
    return (values * half, slope)


def row_mean(values):
    rows = values.shape[0]
    while rows > 8:
        rows //= 2
        values = values[:rows] + values[rows:]
    return jnp.sum(values, axis=0, keepdims=True) * (1.0 / D_HEAD)


def lanes_left(rows):
    return lax.broadcasted_iota(jnp.int32, (rows, LANES), 1) < D_HEAD


def own_half(stacked):
    return jnp.where(lanes_left(D_HEAD), stacked[:D_HEAD], stacked[D_HEAD:])


def spread_halves(rows):
    left = lanes_left(D_HEAD)
    zero = jnp.zeros_like(rows)
    return jnp.concatenate([jnp.where(left, rows, zero), jnp.where(left, zero, rows)], axis=0)


def seat_of(upper, core, place):
    lower_seat = jnp.where(core == 0, SEATS[0][0][place], SEATS[0][1][place])
    upper_seat = jnp.where(core == 0, SEATS[1][0][place], SEATS[1][1][place])
    return jnp.where(upper == 0, lower_seat, upper_seat)


def kernel(
    query_ref,
    key_ref,
    value_ref,
    rates_far,
    first_far,
    first_bias_far,
    second_far,
    second_bias_far,
    gain_far,
    shift_far,
    landed,
    rates_ref,
    first_ref,
    first_bias_ref,
    second_ref,
    second_bias_ref,
    gain_ref,
    shift_ref,
    gathered,
    packed,
    rates_out,
    rates_in,
    tokens,
    blocks_out,
    returned,
    relay_out,
    kept_rows,
    bd_key,
    turned_query,
    rate_rows,
    target_rows,
    causal,
    halves,
    state_one,
    bias_one,
    state_two,
    second_hist,
    bias_two,
    gain_rows,
    shift_rows,
    slope_ref,
    dual_base,
    dual_act_ref,
    act_ref,
    grad_two_ref,
    grad_one_ref,
    within_ref,
    read_ref,
    attend_ref,
    load_sem,
    send_a,
    recv_a,
    send_b,
    recv_b,
    send_r,
    recv_r,
    send_c,
    recv_c,
    send_d,
    recv_d,
):
    fetches = [
        pltpu.make_async_copy(far, here, load_sem.at[place])
        for place, (far, here) in enumerate(
            (
                (rates_far, rates_ref),
                (first_far, first_ref),
                (first_bias_far, first_bias_ref),
                (second_far, second_ref),
                (second_bias_far, second_bias_ref),
                (gain_far, gain_ref),
                (shift_far, shift_ref),
            )
        )
    ]
    for fetch in fetches:
        fetch.start()

    head = lax.axis_index("head")
    seq = lax.axis_index("seq")
    core = lax.rem(head, 2)
    upper = head // NEAR
    near = lax.rem(head, NEAR)
    own_mini = 2 * seq + upper
    seats = [seat_of(upper, core, place) for place in range(HEADS_LOCAL)]
    seated = jnp.logical_or(seq == seats[0], jnp.logical_or(seq == seats[1], seq == seats[2]))
    my_place = jnp.where(seq == seats[1], 1, 0) + jnp.where(seq == seats[2], 2, 0)
    my_slot = HEADS_LOCAL * core + my_place
    my_near = head // 2
    own_source = jnp.logical_and(seated, near == my_near)

    targets = [
        (
            2 * near + slot // HEADS_LOCAL,
            seat_of(near // 4, slot // HEADS_LOCAL, slot % HEADS_LOCAL),
        )
        for slot in range(HEADS_NEAR)
    ]

    def other(device):
        return jnp.logical_or(device[0] != head, device[1] != seq)

    def neighbour(step):
        return lax.rem(near + step, NEAR)

    barrier = pltpu.get_barrier_semaphore()

    def greet(device):
        pl.semaphore_signal(barrier, inc=1, device_id=device, device_id_type=MESH)

    @pl.when(seated)
    def _():
        @pl.loop(0, STEPS)
        def _(turn):
            mini = jnp.where(lax.rem(turn, 2) == 0, turn // 2, STEPS - 1 - turn // 2)
            device = (lax.rem(mini, 2) * NEAR + my_near, mini // 2)

            @pl.when(other(device))
            def _():
                greet(device)

        @pl.loop(1, CHAIN)
        def _(step):
            greet((head, lax.rem(seq + step, CHAIN)))

    for device in targets:

        @pl.when(other(device))
        def _():
            greet(device)

    @pl.loop(1, NEAR)
    def _(step):
        greet((upper * NEAR + neighbour(step), seq))

    fetches[0].wait()
    left_lanes = lanes_left(MINI)
    for place in range(HEADS_LOCAL):
        row = jnp.broadcast_to(rates_ref[place : place + 1], (8, LANES))
        turned_row = pltpu.roll(row, D_HEAD, 1)
        rates_out[place, 0] = jnp.where(left_lanes[:8], row, turned_row)
        rates_out[place, 1] = jnp.where(left_lanes[:8], turned_row, row)

    expected = NEAR - 1 + HEADS_NEAR + HEADS_LOCAL
    expected = expected + jnp.where(seated, STEPS - 1, 0) - jnp.where(own_source, 2, 0)
    pl.semaphore_wait(barrier, expected)

    sources = (query_ref, key_ref, value_ref)

    def wide(index):
        return pl.ds(pl.multiple_of(index * WIDE, LANES), WIDE)

    def rows_of(index):
        return pl.ds(pl.multiple_of(index * 8, 8), 8)

    def exchange_copy(array, step):
        target = neighbour(step)
        return pltpu.make_async_remote_copy(
            src_ref=sources[array].at[:, wide(target)],
            dst_ref=gathered.at[array, rows_of(near)],
            send_sem=send_a.at[array],
            recv_sem=recv_a.at[array],
            device_id=(upper * NEAR + target, seq),
            device_id_type=MESH,
        )

    def own_exchange(array):
        return pltpu.make_async_copy(
            sources[array].at[:, wide(near)], gathered.at[array, rows_of(near)], recv_a.at[array]
        )

    @pl.loop(1, NEAR)
    def _(step):
        for array in range(3):
            exchange_copy(array, step).start()

    for array in range(3):
        own_exchange(array).start()

    def rates_copy(place):
        return pltpu.make_async_remote_copy(
            src_ref=rates_out.at[place],
            dst_ref=rates_in.at[pl.ds(2 * seq, 2)],
            send_sem=send_r.at[place],
            recv_sem=recv_r.at[seq],
            device_id=(head, seats[place]),
            device_id_type=MESH,
        )

    for place in range(HEADS_LOCAL):

        @pl.when(seq != seats[place])
        def _():
            rates_copy(place).start()

    for array in range(3):
        pltpu.make_async_remote_copy(
            src_ref=gathered.at[array],
            dst_ref=gathered.at[array],
            send_sem=send_a.at[array],
            recv_sem=recv_a.at[array],
            device_id=(upper * NEAR + neighbour(1), seq),
            device_id_type=MESH,
        ).wait_recv()

    def relay_copy(slot):
        return pltpu.make_async_remote_copy(
            src_ref=packed.at[slot],
            dst_ref=tokens.at[own_mini],
            send_sem=send_b.at[slot],
            recv_sem=recv_b.at[own_mini],
            device_id=targets[slot],
            device_id_type=MESH,
        )

    for tile in range(HEADS_NEAR // 2):
        columns = slice(tile * LANES, (tile + 1) * LANES)
        queries, keys, values = [gathered[array, :, columns].astype(F32) for array in range(3)]
        queries_turned, keys_turned, values_turned = [
            pltpu.roll(rows, D_HEAD, 1) for rows in (queries, keys, values)
        ]
        first_keys = jnp.where(left_lanes, keys, values_turned)
        second_keys = jnp.where(left_lanes, keys_turned, values)
        half = MINI // 2
        first_queries = jnp.where(left_lanes[:half], queries[:half], queries_turned[half:])
        second_queries = jnp.where(left_lanes[:half], queries_turned[:half], queries[half:])
        packed[2 * tile, :MINI] = first_keys.astype(BF16)
        packed[2 * tile, MINI:] = first_queries.astype(BF16)
        packed[2 * tile + 1, :MINI] = second_keys.astype(BF16)
        packed[2 * tile + 1, MINI:] = second_queries.astype(BF16)

    late = jnp.minimum(own_mini, STEPS - 1 - own_mini)
    pl.delay(jnp.where(seated, 0, late) * SPACING_NS)

    for slot in range(HEADS_NEAR):

        @pl.when(other(targets[slot]))
        def _():
            relay_copy(slot).start()

    for fetch in fetches[1:]:
        fetch.wait()

    @pl.when(seated)
    def _():
        @pl.when(own_source)
        def _():
            tokens[own_mini] = packed[my_slot]

        rates_in[pl.ds(2 * seq, 2)] = rates_out[my_place]

        row = lax.broadcasted_iota(jnp.int32, (LANES, LANES), 0)
        col = lax.broadcasted_iota(jnp.int32, (LANES, LANES), 1)
        ahead = jnp.logical_and(jnp.logical_and(row < 64, col < 64), row <= col)
        back = jnp.logical_and(jnp.logical_and(row >= 64, col >= 64), row >= col)
        causal[...] = jnp.where(jnp.logical_or(ahead, back), 1.0, 0.0)
        halves[...] = jnp.where((row < 64) == (col < 64), 1.0, 0.0)

        first = first_ref[my_place]
        both = jnp.concatenate([first, first], axis=0)
        state_one[...] = both.T
        second = second_ref[my_place]
        second = second - jnp.mean(second, axis=0, keepdims=True)
        doubled = jnp.concatenate([second, second], axis=0)
        state_two[...] = doubled.T
        second_hist[0] = doubled.astype(BF16)

        def spread_column(row_values, length):
            return jnp.broadcast_to(row_values, (LANES, length)).T

        bias_one[...] = spread_column(first_bias_ref[pl.ds(my_place, 1), :], INNER)
        second_bias = second_bias_ref[pl.ds(my_place, 1), :]
        second_bias = second_bias - jnp.mean(second_bias, axis=1, keepdims=True)
        bias_two[0] = spread_column(second_bias, D_HEAD)
        gain_rows[...] = spread_column(gain_ref[pl.ds(my_place, 1), :], D_HEAD)
        shift_rows[...] = spread_column(shift_ref[pl.ds(my_place, 1), :], D_HEAD)

        def await_step(step):
            for mini in (step, STEPS - 1 - step):

                @pl.when(jnp.logical_not(jnp.logical_and(own_source, mini == own_mini)))
                def _():
                    pltpu.make_async_remote_copy(
                        src_ref=packed.at[0],
                        dst_ref=tokens.at[mini],
                        send_sem=send_b.at[0],
                        recv_sem=recv_b.at[mini],
                        device_id=(lax.rem(mini, 2) * NEAR + my_near, mini // 2),
                        device_id_type=MESH,
                    ).wait_recv()

        def await_rates(block):
            @pl.when(block != seq)
            def _():
                pltpu.make_async_remote_copy(
                    src_ref=rates_out.at[0],
                    dst_ref=rates_in.at[pl.ds(2 * block, 2)],
                    send_sem=send_r.at[0],
                    recv_sem=recv_r.at[block],
                    device_id=(head, block),
                    device_id_type=MESH,
                ).wait_recv()

        def load_step(step):
            back = STEPS - 1 - step
            kv_f = tokens[step, :MINI]
            kv_b = tokens[back, :MINI]
            left = lanes_left(MINI)
            keys_back = pltpu.roll(kv_b.astype(F32), D_HEAD, 1)
            keys_bd = jnp.concatenate(
                [jnp.where(left, kv_f.astype(F32), 0.0), jnp.where(left, 0.0, keys_back)], axis=0
            ).astype(BF16)
            pieces = []
            for mini in (step, back):
                pair = tokens[mini, MINI:].astype(F32)
                pieces += [pair, pltpu.roll(pair, D_HEAD, 1)]
            kv_turned = jnp.concatenate([kv_f, kv_b], axis=0).T.astype(F32)
            queries = jnp.concatenate(pieces, axis=0).astype(BF16).T.astype(F32)[:D_HEAD]
            target = kv_turned[D_HEAD:] - kv_turned[:D_HEAD]
            rate = jnp.where(left[:8], rates_in[step], rates_in[back])
            keys_turned = spread_halves(kv_turned[:D_HEAD]).astype(BF16)
            queries_turned = spread_halves(queries).astype(BF16)
            return (keys_bd, keys_turned, queries_turned, target, rate)

        def store_step(loaded):
            bd_key[...] = loaded[0]
            turned_query[...] = loaded[2]
            target_rows[...] = gain_rows[...] * (shift_rows[...] - loaded[3])
            rate_rows[...] = loaded[4]

        def finish(step, dual_two):
            mean = row_mean(dual_two)
            spread = lax.rsqrt(row_mean(dual_two * dual_two) - mean * mean + EPS)
            fitted = gain_rows[...] * ((dual_two - mean) * spread) + shift_rows[...]
            kept_rows[step] = fitted
            total = fitted + pltpu.roll(kept_rows[STEPS - 1 - step], D_HEAD, 1)
            at_left = lax.rem(my_slot, 2) == 0
            total = jnp.concatenate(
                [jnp.where(at_left, total, 0.0), jnp.where(at_left, 0.0, total)], axis=0
            )
            turned = total.astype(BF16).T
            blocks_out[step] = turned[:MINI]
            blocks_out[STEPS - 1 - step] = turned[MINI:]

        def slot_of(step):
            return lax.rem(step, HISTORY)

        def attend_dual(step):
            slot = slot_of(step)
            dual_act = dual_act_ref[lax.rem(step, 2)]
            mask = causal[...]
            read = dot(second_hist[slot], dual_act, (1, 0))
            attend = dot(act_ref[slot].T, dual_act, (1, 0))
            return (own_half(read) + bias_two[slot], (attend * mask + mask).astype(BF16))

        half = INNER // 2
        row_halves = (slice(0, half), slice(half, INNER))

        def widen(grad_one, within, base, bias, ones_bf):
            sums = jnp.concatenate([within, ones_bf], axis=1)
            falls = [dot(grad_one[rows], sums, (1, 0)) for rows in row_halves]
            acts = [
                gelu(base[rows] - fall[:, :LANES]).astype(BF16)
                for rows, fall in zip(row_halves, falls)
            ]
            biases = [bias[rows] - fall[:, LANES:] for rows, fall in zip(row_halves, falls)]
            return (acts, biases)

        def advance(step):
            slot = slot_of(step)
            before = step + HISTORY - 2
            act = act_ref[slot]
            second_turned = second_hist[slot]
            target = target_rows[...]
            gain = gain_rows[...]
            gain_sq = gain * gain
            rate = rate_rows[0:1]
            bias_two_now = bias_two[slot]
            ones_bd = halves[...]
            ones_bf = ones_bd.astype(BF16)
            mask = causal[...]

            pre_two = (
                jnp.where(
                    lanes_left(D_HEAD),
                    dot(second_turned[:D_HEAD], act, (1, 0)),
                    dot(second_turned[D_HEAD:], act, (1, 0)),
                )
                + bias_two_now
            )

            last_read = read_ref[...]
            last_fall = dot(grad_two_ref[slot_of(step + HISTORY - 3)], attend_ref[...], (1, 0))
            dual_acts, biases = widen(
                grad_one_ref[...], within_ref[...], dual_base[...], bias_one[...], ones_bf
            )

            later = jnp.minimum(step + 1, STEPS - 1)
            loaded = load_step(later)
            keys_bd = bd_key[...]
            queries_turned = turned_query[...]
            state_one_now = state_one[...]
            high = state_one_now.astype(BF16)
            low = (state_one_now - high.astype(F32)).astype(BF16)
            reads = jnp.concatenate([loaded[1], queries_turned], axis=1)
            reads = jnp.concatenate([reads, reads], axis=0)
            within_both = dot(
                jnp.concatenate([keys_bd, jnp.zeros_like(keys_bd)], axis=1), reads, (1, 0)
            )
            between = (within_both[:, :LANES] + ones_bd).astype(BF16)
            within = (within_both[:, LANES:] * mask + mask).astype(BF16)

            scaled = gain_sq * pre_two
            mean = row_mean(pre_two)
            sum_scaled = row_mean(scaled)
            sum_square = row_mean(pre_two * pre_two)
            sum_scaled_sq = row_mean(scaled * pre_two)
            sum_target = row_mean(target * pre_two)
            mean_gain = row_mean(gain_sq)
            mean_target = row_mean(target)
            inverse = lax.rsqrt(sum_square - mean * mean + EPS)
            centred_scaled = sum_scaled - mean * mean_gain
            mean_a = inverse * centred_scaled + mean_target
            mean_an = inverse * (
                inverse * (sum_scaled_sq - mean * (sum_scaled + centred_scaled))
                + (sum_target - mean * mean_target)
            )
            weight = inverse * rate
            grad_two = (
                (pre_two - mean) * (inverse * gain_sq - inverse * mean_an) + (target - mean_a)
            ) * weight
            grad_two = grad_two.astype(BF16)
            grad_two_bd = spread_halves(grad_two)
            state_two_now = state_two[...]
            state_two_bf = state_two_now.astype(BF16)
            grads_one = [
                (dot(state_two_bf[rows], grad_two_bd, (1, 0)) * slope_ref[rows, :]).astype(BF16)
                for rows in row_halves
            ]

            finish(jnp.maximum(step - 3, 0), last_read - last_fall)

            state_two_new = state_two_now - dot(act, grad_two_bd.T, (1, 0))
            bias_two_new = bias_two_now - dot(grad_two, ones_bf, (1, 0))
            dual_read, attend = attend_dual(before)
            read_ref[...] = dual_read
            attend_ref[...] = attend

            seen = dot(jnp.concatenate([high, low], axis=1), reads, (1, 0))
            moves = jnp.concatenate([between, keys_bd], axis=1)
            next_slot = slot_of(step + 1)
            for part in range(2):
                rows = row_halves[part]
                fall = dot(grads_one[part], moves, (1, 0))
                state_one[rows, :] = state_one_now[rows] - fall[:, LANES:]
                pre_one = seen[rows, :LANES] + biases[part] - fall[:, :LANES]
                act_next, slope_next = gelu_and_slope(pre_one)
                act_ref[next_slot, rows, :] = act_next.astype(BF16)
                slope_ref[rows, :] = slope_next
                dual_base[rows, :] = seen[rows, LANES:] + biases[part]
                bias_one[rows, :] = biases[part]
                grad_one_ref[rows, :] = grads_one[part]
                dual_act_ref[lax.rem(step + 1, 2), rows, :] = dual_acts[part]

            state_two[...] = state_two_new
            second_hist[next_slot] = state_two_new.astype(BF16).T
            bias_two[next_slot] = bias_two_new
            grad_two_ref[slot] = grad_two
            within_ref[...] = within
            store_step(loaded)

        def emit(step, read, attend):
            finish(step, read - dot(grad_two_ref[slot_of(step)], attend, (1, 0)))

        def return_copy(mini):
            return pltpu.make_async_remote_copy(
                src_ref=blocks_out.at[mini],
                dst_ref=returned.at[my_slot],
                send_sem=send_c.at[mini],
                recv_sem=recv_c.at[my_slot],
                device_id=(lax.rem(mini, 2) * NEAR + my_near, mini // 2),
                device_id_type=MESH,
            )

        def is_own(mini):
            return jnp.logical_and(own_source, mini == own_mini)

        def give_back(mini):
            @pl.when(jnp.logical_not(is_own(mini)))
            def _():
                return_copy(mini).start()

            @pl.when(is_own(mini))
            def _():
                returned[my_slot] = blocks_out[mini]

        await_rates(0)
        await_rates(CHAIN - 1)
        await_step(0)
        begun = load_step(0)
        store_step(begun)
        high = state_one[...].astype(BF16)
        low = (state_one[...] - high.astype(F32)).astype(BF16)
        act, slope = gelu_and_slope(
            dot(high, begun[1], (1, 0)) + dot(low, begun[1], (1, 0)) + bias_one[...]
        )
        act_ref[0] = act.astype(BF16)
        slope_ref[...] = slope
        grad_one_ref[...] = jnp.zeros_like(grad_one_ref)
        within_ref[...] = jnp.zeros_like(within_ref)

        @pl.loop(0, STEPS)
        def _(step):
            later = step + 1

            @pl.when(later < STEPS // 2)
            def _():
                await_step(later)

                @pl.when(lax.rem(later, 2) == 0)
                def _():
                    await_rates(later // 2)
                    await_rates(CHAIN - 1 - later // 2)

            advance(step)
            done = step - 3

            @pl.when(done >= STEPS // 2)
            def _():
                give_back(done)
                give_back(STEPS - 1 - done)

        last = STEPS - 1
        dual_acts, _ = widen(
            grad_one_ref[...],
            within_ref[...],
            dual_base[...],
            bias_one[...],
            halves[...].astype(BF16),
        )
        later = attend_dual(last - 1)
        emit(last - 2, read_ref[...], attend_ref[...])
        for part in range(2):
            dual_act_ref[last % 2, row_halves[part], :] = dual_acts[part]
        latest = attend_dual(last)
        emit(last - 1, *later)
        emit(last, *latest)
        for step in (last, last - 1, last - 2):
            give_back(step)
            give_back(STEPS - 1 - step)

    for slot in range(HEADS_NEAR):

        @pl.when(other(targets[slot]))
        def _():
            pltpu.make_async_remote_copy(
                src_ref=blocks_out.at[0],
                dst_ref=returned.at[slot],
                send_sem=send_c.at[0],
                recv_sem=recv_c.at[slot],
                device_id=targets[slot],
                device_id_type=MESH,
            ).wait_recv()

    for tile in range(HEADS_NEAR // 2):
        columns = slice(tile * LANES, (tile + 1) * LANES)
        relay_out[:, columns] = jnp.where(left_lanes, returned[2 * tile], returned[2 * tile + 1])

    def spread_copy(step):
        target = neighbour(step)
        return pltpu.make_async_remote_copy(
            src_ref=relay_out.at[rows_of(target)],
            dst_ref=landed.at[:, wide(near)],
            send_sem=send_d.at[0],
            recv_sem=recv_d.at[0],
            device_id=(upper * NEAR + target, seq),
            device_id_type=MESH,
        )

    @pl.loop(1, NEAR)
    def _(step):
        spread_copy(step).start()

    pltpu.make_async_copy(
        relay_out.at[rows_of(near)], landed.at[:, wide(near)], recv_d.at[0]
    ).start()
    pltpu.make_async_remote_copy(
        src_ref=landed,
        dst_ref=landed,
        send_sem=send_d.at[0],
        recv_sem=recv_d.at[0],
        device_id=(upper * NEAR + neighbour(1), seq),
        device_id_type=MESH,
    ).wait_recv()

    sent = pl.ds(0, (NEAR - 1) * WIDE)
    for array in range(3):
        pltpu.make_async_remote_copy(
            src_ref=sources[array].at[:, sent],
            dst_ref=sources[array].at[:, sent],
            send_sem=send_a.at[array],
            recv_sem=recv_a.at[array],
            device_id=(upper * NEAR + neighbour(1), seq),
            device_id_type=MESH,
        ).wait_send()
    pltpu.make_async_remote_copy(
        src_ref=relay_out.at[pl.ds(0, 8 * (NEAR - 1))],
        dst_ref=relay_out.at[pl.ds(0, 8 * (NEAR - 1))],
        send_sem=send_d.at[0],
        recv_sem=recv_d.at[0],
        device_id=(upper * NEAR + neighbour(1), seq),
        device_id_type=MESH,
    ).wait_send()

    for place in range(HEADS_LOCAL):

        @pl.when(seq != seats[place])
        def _():
            rates_copy(place).wait_send()

    for slot in range(HEADS_NEAR):

        @pl.when(other(targets[slot]))
        def _():
            relay_copy(slot).wait_send()

    @pl.when(seated)
    def _():
        @pl.loop(0, STEPS)
        def _(mini):
            device = (lax.rem(mini, 2) * NEAR + my_near, mini // 2)

            @pl.when(other(device))
            def _():
                pltpu.make_async_remote_copy(
                    src_ref=blocks_out.at[mini],
                    dst_ref=returned.at[my_slot],
                    send_sem=send_c.at[mini],
                    recv_sem=recv_c.at[my_slot],
                    device_id=device,
                    device_id_type=MESH,
                ).wait_send()


def local(*arrays):
    arrays = list(arrays)
    arrays[4] = arrays[4].T
    arrays[7] = jnp.swapaxes(arrays[7], 1, 2)
    gate = arrays.pop(3)
    anywhere = pl.BlockSpec(memory_space=pl.ANY)
    dma = pltpu.SemaphoreType.DMA
    summed = pl.pallas_call(
        kernel,
        out_shape=jax.ShapeDtypeStruct((8, TILES * LANES), BF16),
        in_specs=[anywhere] * len(arrays),
        out_specs=anywhere,
        scratch_shapes=[
            *[pltpu.VMEM(array.shape, array.dtype) for array in arrays[3:]],
            pltpu.VMEM((3, MINI, WIDE), BF16),
            pltpu.VMEM((HEADS_NEAR, PACKED, LANES), BF16),
            pltpu.VMEM((HEADS_LOCAL, 2, 8, LANES), F32),
            pltpu.VMEM((STEPS, 8, LANES), F32),
            pltpu.VMEM((STEPS, PACKED, LANES), BF16),
            pltpu.VMEM((STEPS, MINI, LANES), BF16),
            pltpu.VMEM((HEADS_NEAR, MINI, LANES), BF16),
            pltpu.VMEM((MINI, WIDE), BF16),
            pltpu.VMEM((STEPS, D_HEAD, LANES), F32),
            pltpu.VMEM((LANES, LANES), BF16),
            pltpu.VMEM((LANES, LANES), BF16),
            pltpu.VMEM((8, LANES), F32),
            pltpu.VMEM((D_HEAD, LANES), F32),
            pltpu.VMEM((LANES, LANES), F32),
            pltpu.VMEM((LANES, LANES), F32),
            pltpu.VMEM((INNER, LANES), F32),
            pltpu.VMEM((INNER, LANES), F32),
            pltpu.VMEM((INNER, LANES), F32),
            pltpu.VMEM((HISTORY, LANES, INNER), BF16),
            pltpu.VMEM((HISTORY, D_HEAD, LANES), F32),
            pltpu.VMEM((D_HEAD, LANES), F32),
            pltpu.VMEM((D_HEAD, LANES), F32),
            pltpu.VMEM((INNER, LANES), F32),
            pltpu.VMEM((INNER, LANES), F32),
            pltpu.VMEM((2, INNER, LANES), BF16),
            pltpu.VMEM((HISTORY, INNER, LANES), BF16),
            pltpu.VMEM((HISTORY, D_HEAD, LANES), BF16),
            pltpu.VMEM((INNER, LANES), BF16),
            pltpu.VMEM((LANES, LANES), BF16),
            pltpu.VMEM((D_HEAD, LANES), F32),
            pltpu.VMEM((LANES, LANES), BF16),
            dma((7,)),
            dma((3,)),
            dma((3,)),
            dma((HEADS_NEAR,)),
            dma((STEPS,)),
            dma((HEADS_LOCAL,)),
            dma((CHAIN,)),
            dma((STEPS,)),
            dma((HEADS_NEAR,)),
            dma((1,)),
            dma((1,)),
        ],
        compiler_params=pltpu.CompilerParams(collective_id=0, has_side_effects=True),
    )(*arrays)
    return (gate.astype(F32) * summed.astype(F32)).astype(BF16)


def solution(mesh):
    rows = P(("seq", "head"), None)
    in_specs = (
        rows,
        rows,
        rows,
        rows,
        P("seq", "head"),
        P("head", None, None),
        P("head", None),
        P("head", None, None),
        P("head", None),
        P("head", None),
        P("head", None),
    )
    return jax.shard_map(local, mesh=mesh, in_specs=in_specs, out_specs=rows, check_vma=False)
```

```python
import functools

import jax
import jax.numpy as jnp
from jax import lax
from jax.experimental import pallas as pl
from jax.experimental.pallas import tpu as pltpu
from jax.sharding import PartitionSpec as P

D_HEAD = 64
INNER = 256
MINI = 64
STEPS = 64
LANES = 128
NEAR = 8
CHAIN = 32
HEADS_LOCAL = 3
HEADS_NEAR = 6
WIDE = HEADS_NEAR * D_HEAD
TILES = 24

EPS = 1e-06
ROOT = 0.7978845608028654
CUBE = 0.044715
MESH = pl.DeviceIdType.MESH
F32 = jnp.float32
BF16 = jnp.bfloat16

PACKED = MINI + MINI // 2
HISTORY = 4
SPACING_NS = 612

SEATS = (((1, 7, 12), (2, 4, 15)), ((29, 26, 16), (30, 25, 19)))


def dot(left, right, dims):
    return lax.dot_general(
        left, right, (((dims[0],), (dims[1],)), ((), ())), preferred_element_type=F32
    )


def gelu(values):
    squared = values * values
    tanh_term = jnp.tanh(values * (ROOT + (ROOT * CUBE) * squared))
    return values * (0.5 + 0.5 * tanh_term)


def gelu_and_slope(values):
    squared = values * values
    tanh_term = jnp.tanh(values * (ROOT + (ROOT * CUBE) * squared))
    half = 0.5 + 0.5 * tanh_term
    slope = half + values * (half * (1.0 - tanh_term)) * (ROOT + (3.0 * ROOT * CUBE) * squared)
    return (values * half, slope)


def row_mean(values):
    rows = values.shape[0]
    while rows > 8:
        rows //= 2
        values = values[:rows] + values[rows:]
    return jnp.sum(values, axis=0, keepdims=True) * (1.0 / D_HEAD)


def lanes_left(rows):
    return lax.broadcasted_iota(jnp.int32, (rows, LANES), 1) < D_HEAD


def own_half(stacked):
    return jnp.where(lanes_left(D_HEAD), stacked[:D_HEAD], stacked[D_HEAD:])


def spread_halves(rows):
    left = lanes_left(D_HEAD)
    zero = jnp.zeros_like(rows)
    return jnp.concatenate([jnp.where(left, rows, zero), jnp.where(left, zero, rows)], axis=0)


def seat_of(upper, core, place):
    lower_seat = jnp.where(core == 0, SEATS[0][0][place], SEATS[0][1][place])
    upper_seat = jnp.where(core == 0, SEATS[1][0][place], SEATS[1][1][place])
    return jnp.where(upper == 0, lower_seat, upper_seat)


def kernel(
    query_ref,
    key_ref,
    value_ref,
    rates_far,
    first_far,
    first_bias_far,
    second_far,
    second_bias_far,
    gain_far,
    shift_far,
    landed,
    rates_ref,
    first_ref,
    first_bias_ref,
    second_ref,
    second_bias_ref,
    gain_ref,
    shift_ref,
    gathered,
    packed,
    rates_out,
    rates_in,
    tokens,
    blocks_out,
    returned,
    relay_out,
    kept_rows,
    bd_key,
    turned_query,
    rate_rows,
    target_rows,
    causal,
    halves,
    state_one,
    bias_one,
    state_two,
    second_hist,
    bias_two,
    gain_rows,
    shift_rows,
    slope_ref,
    dual_base,
    dual_act_ref,
    act_ref,
    grad_two_ref,
    grad_one_ref,
    within_ref,
    read_ref,
    attend_ref,
    load_sem,
    send_a,
    recv_a,
    send_b,
    recv_b,
    send_r,
    recv_r,
    send_c,
    recv_c,
    send_d,
    recv_d,
):
    fetches = [
        pltpu.make_async_copy(far, here, load_sem.at[place])
        for place, (far, here) in enumerate(
            (
                (rates_far, rates_ref),
                (first_far, first_ref),
                (first_bias_far, first_bias_ref),
                (second_far, second_ref),
                (second_bias_far, second_bias_ref),
                (gain_far, gain_ref),
                (shift_far, shift_ref),
            )
        )
    ]
    for fetch in fetches:
        fetch.start()

    head = lax.axis_index("head")
    seq = lax.axis_index("seq")
    core = lax.rem(head, 2)
    upper = head // NEAR
    near = lax.rem(head, NEAR)
    own_mini = 2 * seq + upper
    seats = [seat_of(upper, core, place) for place in range(HEADS_LOCAL)]
    seated = jnp.logical_or(seq == seats[0], jnp.logical_or(seq == seats[1], seq == seats[2]))
    my_place = jnp.where(seq == seats[1], 1, 0) + jnp.where(seq == seats[2], 2, 0)
    my_slot = HEADS_LOCAL * core + my_place
    my_near = head // 2
    own_source = jnp.logical_and(seated, near == my_near)

    targets = [
        (
            2 * near + slot // HEADS_LOCAL,
            seat_of(near // 4, slot // HEADS_LOCAL, slot % HEADS_LOCAL),
        )
        for slot in range(HEADS_NEAR)
    ]

    def other(device):
        return jnp.logical_or(device[0] != head, device[1] != seq)

    def neighbour(step):
        return lax.rem(near + step, NEAR)

    barrier = pltpu.get_barrier_semaphore()

    def greet(device):
        pl.semaphore_signal(barrier, inc=1, device_id=device, device_id_type=MESH)

    @pl.when(seated)
    def _():
        @pl.loop(0, STEPS)
        def _(turn):
            mini = jnp.where(lax.rem(turn, 2) == 0, turn // 2, STEPS - 1 - turn // 2)
            device = (lax.rem(mini, 2) * NEAR + my_near, mini // 2)

            @pl.when(other(device))
            def _():
                greet(device)

        @pl.loop(1, CHAIN)
        def _(step):
            greet((head, lax.rem(seq + step, CHAIN)))

    for device in targets:

        @pl.when(other(device))
        def _():
            greet(device)

    for step in range(1, NEAR):
        greet((upper * NEAR + neighbour(step), seq))

    fetches[0].wait()
    left_lanes = lanes_left(MINI)
    for place in range(HEADS_LOCAL):
        row = jnp.broadcast_to(rates_ref[place : place + 1], (8, LANES))
        turned_row = pltpu.roll(row, D_HEAD, 1)
        rates_out[place, 0] = jnp.where(left_lanes[:8], row, turned_row)
        rates_out[place, 1] = jnp.where(left_lanes[:8], turned_row, row)

    expected = NEAR - 1 + HEADS_NEAR + HEADS_LOCAL
    expected = expected + jnp.where(seated, STEPS - 1, 0) - jnp.where(own_source, 2, 0)
    pl.semaphore_wait(barrier, expected)

    sources = (query_ref, key_ref, value_ref)

    def wide(index):
        return pl.ds(pl.multiple_of(index * WIDE, LANES), WIDE)

    def rows_of(index):
        return pl.ds(pl.multiple_of(index * 8, 8), 8)

    def exchange_copy(array, step):
        target = neighbour(step)
        return pltpu.make_async_remote_copy(
            src_ref=sources[array].at[:, wide(target)],
            dst_ref=gathered.at[array, rows_of(near)],
            send_sem=send_a.at[array],
            recv_sem=recv_a.at[array],
            device_id=(upper * NEAR + target, seq),
            device_id_type=MESH,
        )

    def own_exchange(array):
        return pltpu.make_async_copy(
            sources[array].at[:, wide(near)], gathered.at[array, rows_of(near)], recv_a.at[array]
        )

    for step in range(1, NEAR):
        for array in range(3):
            exchange_copy(array, step).start()

    for array in range(3):
        own_exchange(array).start()

    def rates_copy(place):
        return pltpu.make_async_remote_copy(
            src_ref=rates_out.at[place],
            dst_ref=rates_in.at[pl.ds(2 * seq, 2)],
            send_sem=send_r.at[place],
            recv_sem=recv_r.at[seq],
            device_id=(head, seats[place]),
            device_id_type=MESH,
        )

    for place in range(HEADS_LOCAL):

        @pl.when(seq != seats[place])
        def _():
            rates_copy(place).start()

    for array in range(3):
        pltpu.make_async_remote_copy(
            src_ref=gathered.at[array],
            dst_ref=gathered.at[array],
            send_sem=send_a.at[array],
            recv_sem=recv_a.at[array],
            device_id=(upper * NEAR + neighbour(1), seq),
            device_id_type=MESH,
        ).wait_recv()

    def relay_copy(slot):
        return pltpu.make_async_remote_copy(
            src_ref=packed.at[slot],
            dst_ref=tokens.at[own_mini],
            send_sem=send_b.at[slot],
            recv_sem=recv_b.at[own_mini],
            device_id=targets[slot],
            device_id_type=MESH,
        )

    for tile in range(HEADS_NEAR // 2):
        columns = slice(tile * LANES, (tile + 1) * LANES)
        queries, keys, values = [gathered[array, :, columns].astype(F32) for array in range(3)]
        queries_turned, keys_turned, values_turned = [
            pltpu.roll(rows, D_HEAD, 1) for rows in (queries, keys, values)
        ]
        first_keys = jnp.where(left_lanes, keys, values_turned)
        second_keys = jnp.where(left_lanes, keys_turned, values)
        half = MINI // 2
        first_queries = jnp.where(left_lanes[:half], queries[:half], queries_turned[half:])
        second_queries = jnp.where(left_lanes[:half], queries_turned[:half], queries[half:])
        packed[2 * tile, :MINI] = first_keys.astype(BF16)
        packed[2 * tile, MINI:] = first_queries.astype(BF16)
        packed[2 * tile + 1, :MINI] = second_keys.astype(BF16)
        packed[2 * tile + 1, MINI:] = second_queries.astype(BF16)

    late = jnp.minimum(own_mini, STEPS - 1 - own_mini)
    pl.delay(jnp.where(seated, 0, late) * SPACING_NS)

    for slot in range(HEADS_NEAR):

        @pl.when(other(targets[slot]))
        def _():
            relay_copy(slot).start()

    for fetch in fetches[1:]:
        fetch.wait()

    @pl.when(seated)
    def _():
        @pl.when(own_source)
        def _():
            tokens[own_mini] = packed[my_slot]

        rates_in[pl.ds(2 * seq, 2)] = rates_out[my_place]

        row = lax.broadcasted_iota(jnp.int32, (LANES, LANES), 0)
        col = lax.broadcasted_iota(jnp.int32, (LANES, LANES), 1)
        ahead = jnp.logical_and(jnp.logical_and(row < 64, col < 64), row <= col)
        back = jnp.logical_and(jnp.logical_and(row >= 64, col >= 64), row >= col)
        causal[...] = jnp.where(jnp.logical_or(ahead, back), 1.0, 0.0)
        halves[...] = jnp.where((row < 64) == (col < 64), 1.0, 0.0)

        first = first_ref[my_place]
        both = jnp.concatenate([first, first], axis=0)
        state_one[...] = both.T
        second = second_ref[my_place]
        second = second - jnp.mean(second, axis=0, keepdims=True)
        doubled = jnp.concatenate([second, second], axis=0)
        state_two[...] = doubled.T
        second_hist[0] = doubled.astype(BF16)

        def spread_column(row_values, length):
            return jnp.broadcast_to(row_values, (LANES, length)).T

        bias_one[...] = spread_column(first_bias_ref[pl.ds(my_place, 1), :], INNER)
        second_bias = second_bias_ref[pl.ds(my_place, 1), :]
        second_bias = second_bias - jnp.mean(second_bias, axis=1, keepdims=True)
        bias_two[0] = spread_column(second_bias, D_HEAD)
        gain_rows[...] = spread_column(gain_ref[pl.ds(my_place, 1), :], D_HEAD)
        shift_rows[...] = spread_column(shift_ref[pl.ds(my_place, 1), :], D_HEAD)

        def await_step(step):
            for mini in (step, STEPS - 1 - step):

                @pl.when(jnp.logical_not(jnp.logical_and(own_source, mini == own_mini)))
                def _():
                    pltpu.make_async_remote_copy(
                        src_ref=packed.at[0],
                        dst_ref=tokens.at[mini],
                        send_sem=send_b.at[0],
                        recv_sem=recv_b.at[mini],
                        device_id=(lax.rem(mini, 2) * NEAR + my_near, mini // 2),
                        device_id_type=MESH,
                    ).wait_recv()

        def await_rates(block):
            @pl.when(block != seq)
            def _():
                pltpu.make_async_remote_copy(
                    src_ref=rates_out.at[0],
                    dst_ref=rates_in.at[pl.ds(2 * block, 2)],
                    send_sem=send_r.at[0],
                    recv_sem=recv_r.at[block],
                    device_id=(head, block),
                    device_id_type=MESH,
                ).wait_recv()

        def load_step(step):
            back = STEPS - 1 - step
            kv_f = tokens[step, :MINI]
            kv_b = tokens[back, :MINI]
            left = lanes_left(MINI)
            keys_back = pltpu.roll(kv_b.astype(F32), D_HEAD, 1)
            keys_bd = jnp.concatenate(
                [jnp.where(left, kv_f.astype(F32), 0.0), jnp.where(left, 0.0, keys_back)], axis=0
            ).astype(BF16)
            pieces = []
            for mini in (step, back):
                pair = tokens[mini, MINI:].astype(F32)
                pieces += [pair, pltpu.roll(pair, D_HEAD, 1)]
            kv_turned = jnp.concatenate([kv_f, kv_b], axis=0).T.astype(F32)
            queries = jnp.concatenate(pieces, axis=0).astype(BF16).T.astype(F32)[:D_HEAD]
            target = kv_turned[D_HEAD:] - kv_turned[:D_HEAD]
            rate = jnp.where(left[:8], rates_in[step], rates_in[back])
            keys_turned = spread_halves(kv_turned[:D_HEAD]).astype(BF16)
            queries_turned = spread_halves(queries).astype(BF16)
            return (keys_bd, keys_turned, queries_turned, target, rate)

        def store_step(loaded):
            bd_key[...] = loaded[0]
            turned_query[...] = loaded[2]
            target_rows[...] = gain_rows[...] * (shift_rows[...] - loaded[3])
            rate_rows[...] = loaded[4]

        def finish(step, dual_two):
            mean = row_mean(dual_two)
            spread = lax.rsqrt(row_mean(dual_two * dual_two) - mean * mean + EPS)
            fitted = gain_rows[...] * ((dual_two - mean) * spread) + shift_rows[...]
            kept_rows[step] = fitted
            total = fitted + pltpu.roll(kept_rows[STEPS - 1 - step], D_HEAD, 1)
            at_left = lax.rem(my_slot, 2) == 0
            total = jnp.concatenate(
                [jnp.where(at_left, total, 0.0), jnp.where(at_left, 0.0, total)], axis=0
            )
            turned = total.astype(BF16).T
            blocks_out[step] = turned[:MINI]
            blocks_out[STEPS - 1 - step] = turned[MINI:]

        def slot_of(step):
            return lax.rem(step, HISTORY)

        def attend_dual(step):
            slot = slot_of(step)
            dual_act = dual_act_ref[lax.rem(step, 2)]
            mask = causal[...]
            read = dot(second_hist[slot], dual_act, (1, 0))
            attend = dot(act_ref[slot].T, dual_act, (1, 0))
            return (own_half(read) + bias_two[slot], (attend * mask + mask).astype(BF16))

        half = INNER // 2
        row_halves = (slice(0, half), slice(half, INNER))

        def widen(grad_one, within, base, bias, ones_bf):
            sums = jnp.concatenate([within, ones_bf], axis=1)
            falls = [dot(grad_one[rows], sums, (1, 0)) for rows in row_halves]
            acts = [
                gelu(base[rows] - fall[:, :LANES]).astype(BF16)
                for rows, fall in zip(row_halves, falls)
            ]
            biases = [bias[rows] - fall[:, LANES:] for rows, fall in zip(row_halves, falls)]
            return (acts, biases)

        def advance(step):
            slot = slot_of(step)
            before = step + HISTORY - 2
            act = act_ref[slot]
            second_turned = second_hist[slot]
            target = target_rows[...]
            gain = gain_rows[...]
            gain_sq = gain * gain
            rate = rate_rows[0:1]
            bias_two_now = bias_two[slot]
            ones_bd = halves[...]
            ones_bf = ones_bd.astype(BF16)
            mask = causal[...]

            pre_two = (
                jnp.where(
                    lanes_left(D_HEAD),
                    dot(second_turned[:D_HEAD], act, (1, 0)),
                    dot(second_turned[D_HEAD:], act, (1, 0)),
                )
                + bias_two_now
            )

            last_read = read_ref[...]
            last_fall = dot(grad_two_ref[slot_of(step + HISTORY - 3)], attend_ref[...], (1, 0))
            dual_acts, biases = widen(
                grad_one_ref[...], within_ref[...], dual_base[...], bias_one[...], ones_bf
            )

            later = jnp.minimum(step + 1, STEPS - 1)
            loaded = load_step(later)
            keys_bd = bd_key[...]
            queries_turned = turned_query[...]
            state_one_now = state_one[...]
            high = state_one_now.astype(BF16)
            low = (state_one_now - high.astype(F32)).astype(BF16)
            reads = jnp.concatenate([loaded[1], queries_turned], axis=1)
            reads = jnp.concatenate([reads, reads], axis=0)
            within_both = dot(
                jnp.concatenate([keys_bd, jnp.zeros_like(keys_bd)], axis=1), reads, (1, 0)
            )
            between = (within_both[:, :LANES] + ones_bd).astype(BF16)
            within = (within_both[:, LANES:] * mask + mask).astype(BF16)

            scaled = gain_sq * pre_two
            mean = row_mean(pre_two)
            sum_scaled = row_mean(scaled)
            sum_square = row_mean(pre_two * pre_two)
            sum_scaled_sq = row_mean(scaled * pre_two)
            sum_target = row_mean(target * pre_two)
            mean_gain = row_mean(gain_sq)
            mean_target = row_mean(target)
            inverse = lax.rsqrt(sum_square - mean * mean + EPS)
            centred_scaled = sum_scaled - mean * mean_gain
            mean_a = inverse * centred_scaled + mean_target
            mean_an = inverse * (
                inverse * (sum_scaled_sq - mean * (sum_scaled + centred_scaled))
                + (sum_target - mean * mean_target)
            )
            weight = inverse * rate
            grad_two = (
                (pre_two - mean) * (inverse * gain_sq - inverse * mean_an) + (target - mean_a)
            ) * weight
            grad_two = grad_two.astype(BF16)
            grad_two_bd = spread_halves(grad_two)
            state_two_now = state_two[...]
            state_two_bf = state_two_now.astype(BF16)
            grads_one = [
                (dot(state_two_bf[rows], grad_two_bd, (1, 0)) * slope_ref[rows, :]).astype(BF16)
                for rows in row_halves
            ]

            finish(jnp.maximum(step - 3, 0), last_read - last_fall)

            state_two_new = state_two_now - dot(act, grad_two_bd.T, (1, 0))
            bias_two_new = bias_two_now - dot(grad_two, ones_bf, (1, 0))
            dual_read, attend = attend_dual(before)
            read_ref[...] = dual_read
            attend_ref[...] = attend

            seen = dot(jnp.concatenate([high, low], axis=1), reads, (1, 0))
            moves = jnp.concatenate([between, keys_bd], axis=1)
            next_slot = slot_of(step + 1)
            for part in range(2):
                rows = row_halves[part]
                fall = dot(grads_one[part], moves, (1, 0))
                state_one[rows, :] = state_one_now[rows] - fall[:, LANES:]
                pre_one = seen[rows, :LANES] + biases[part] - fall[:, :LANES]
                act_next, slope_next = gelu_and_slope(pre_one)
                act_ref[next_slot, rows, :] = act_next.astype(BF16)
                slope_ref[rows, :] = slope_next
                dual_base[rows, :] = seen[rows, LANES:] + biases[part]
                bias_one[rows, :] = biases[part]
                grad_one_ref[rows, :] = grads_one[part]
                dual_act_ref[lax.rem(step + 1, 2), rows, :] = dual_acts[part]

            state_two[...] = state_two_new
            second_hist[next_slot] = state_two_new.astype(BF16).T
            bias_two[next_slot] = bias_two_new
            grad_two_ref[slot] = grad_two
            within_ref[...] = within
            store_step(loaded)

        def emit(step, read, attend):
            finish(step, read - dot(grad_two_ref[slot_of(step)], attend, (1, 0)))

        def return_copy(mini):
            return pltpu.make_async_remote_copy(
                src_ref=blocks_out.at[mini],
                dst_ref=returned.at[my_slot],
                send_sem=send_c.at[mini],
                recv_sem=recv_c.at[my_slot],
                device_id=(lax.rem(mini, 2) * NEAR + my_near, mini // 2),
                device_id_type=MESH,
            )

        def is_own(mini):
            return jnp.logical_and(own_source, mini == own_mini)

        def give_back(mini):
            @pl.when(jnp.logical_not(is_own(mini)))
            def _():
                return_copy(mini).start()

            @pl.when(is_own(mini))
            def _():
                returned[my_slot] = blocks_out[mini]

        await_rates(0)
        await_rates(CHAIN - 1)
        await_step(0)
        begun = load_step(0)
        store_step(begun)
        high = state_one[...].astype(BF16)
        low = (state_one[...] - high.astype(F32)).astype(BF16)
        act, slope = gelu_and_slope(
            dot(high, begun[1], (1, 0)) + dot(low, begun[1], (1, 0)) + bias_one[...]
        )
        act_ref[0] = act.astype(BF16)
        slope_ref[...] = slope
        grad_one_ref[...] = jnp.zeros_like(grad_one_ref)
        within_ref[...] = jnp.zeros_like(within_ref)

        @pl.loop(0, STEPS)
        def _(step):
            later = step + 1

            @pl.when(later < STEPS // 2)
            def _():
                await_step(later)

                @pl.when(lax.rem(later, 2) == 0)
                def _():
                    await_rates(later // 2)
                    await_rates(CHAIN - 1 - later // 2)

            advance(step)
            done = step - 3

            @pl.when(done >= STEPS // 2)
            def _():
                give_back(done)
                give_back(STEPS - 1 - done)

        last = STEPS - 1
        dual_acts, _ = widen(
            grad_one_ref[...],
            within_ref[...],
            dual_base[...],
            bias_one[...],
            halves[...].astype(BF16),
        )
        later = attend_dual(last - 1)
        emit(last - 2, read_ref[...], attend_ref[...])
        for part in range(2):
            dual_act_ref[last % 2, row_halves[part], :] = dual_acts[part]
        latest = attend_dual(last)
        emit(last - 1, *later)
        emit(last, *latest)
        for step in (last, last - 1, last - 2):
            give_back(step)
            give_back(STEPS - 1 - step)

    for slot in range(HEADS_NEAR):

        @pl.when(other(targets[slot]))
        def _():
            pltpu.make_async_remote_copy(
                src_ref=blocks_out.at[0],
                dst_ref=returned.at[slot],
                send_sem=send_c.at[0],
                recv_sem=recv_c.at[slot],
                device_id=targets[slot],
                device_id_type=MESH,
            ).wait_recv()

    for tile in range(HEADS_NEAR // 2):
        columns = slice(tile * LANES, (tile + 1) * LANES)
        relay_out[:, columns] = jnp.where(left_lanes, returned[2 * tile], returned[2 * tile + 1])

    def spread_copy(step):
        target = neighbour(step)
        return pltpu.make_async_remote_copy(
            src_ref=relay_out.at[rows_of(target)],
            dst_ref=landed.at[:, wide(near)],
            send_sem=send_d.at[0],
            recv_sem=recv_d.at[0],
            device_id=(upper * NEAR + target, seq),
            device_id_type=MESH,
        )

    for step in range(1, NEAR):
        spread_copy(step).start()

    pltpu.make_async_copy(
        relay_out.at[rows_of(near)], landed.at[:, wide(near)], recv_d.at[0]
    ).start()
    pltpu.make_async_remote_copy(
        src_ref=landed,
        dst_ref=landed,
        send_sem=send_d.at[0],
        recv_sem=recv_d.at[0],
        device_id=(upper * NEAR + neighbour(1), seq),
        device_id_type=MESH,
    ).wait_recv()

    sent = pl.ds(0, (NEAR - 1) * WIDE)
    for array in range(3):
        pltpu.make_async_remote_copy(
            src_ref=sources[array].at[:, sent],
            dst_ref=sources[array].at[:, sent],
            send_sem=send_a.at[array],
            recv_sem=recv_a.at[array],
            device_id=(upper * NEAR + neighbour(1), seq),
            device_id_type=MESH,
        ).wait_send()
    pltpu.make_async_remote_copy(
        src_ref=relay_out.at[pl.ds(0, 8 * (NEAR - 1))],
        dst_ref=relay_out.at[pl.ds(0, 8 * (NEAR - 1))],
        send_sem=send_d.at[0],
        recv_sem=recv_d.at[0],
        device_id=(upper * NEAR + neighbour(1), seq),
        device_id_type=MESH,
    ).wait_send()

    for place in range(HEADS_LOCAL):

        @pl.when(seq != seats[place])
        def _():
            rates_copy(place).wait_send()

    for slot in range(HEADS_NEAR):

        @pl.when(other(targets[slot]))
        def _():
            relay_copy(slot).wait_send()

    @pl.when(seated)
    def _():
        @pl.loop(0, STEPS)
        def _(mini):
            device = (lax.rem(mini, 2) * NEAR + my_near, mini // 2)

            @pl.when(other(device))
            def _():
                pltpu.make_async_remote_copy(
                    src_ref=blocks_out.at[mini],
                    dst_ref=returned.at[my_slot],
                    send_sem=send_c.at[mini],
                    recv_sem=recv_c.at[my_slot],
                    device_id=device,
                    device_id_type=MESH,
                ).wait_send()


def local(*arrays):
    arrays = list(arrays)
    arrays[4] = arrays[4].T
    arrays[7] = jnp.swapaxes(arrays[7], 1, 2)
    gate = arrays.pop(3)
    anywhere = pl.BlockSpec(memory_space=pl.ANY)
    dma = pltpu.SemaphoreType.DMA
    summed = pl.pallas_call(
        kernel,
        out_shape=jax.ShapeDtypeStruct((8, TILES * LANES), BF16),
        in_specs=[anywhere] * len(arrays),
        out_specs=anywhere,
        scratch_shapes=[
            *[pltpu.VMEM(array.shape, array.dtype) for array in arrays[3:]],
            pltpu.VMEM((3, MINI, WIDE), BF16),
            pltpu.VMEM((HEADS_NEAR, PACKED, LANES), BF16),
            pltpu.VMEM((HEADS_LOCAL, 2, 8, LANES), F32),
            pltpu.VMEM((STEPS, 8, LANES), F32),
            pltpu.VMEM((STEPS, PACKED, LANES), BF16),
            pltpu.VMEM((STEPS, MINI, LANES), BF16),
            pltpu.VMEM((HEADS_NEAR, MINI, LANES), BF16),
            pltpu.VMEM((MINI, WIDE), BF16),
            pltpu.VMEM((STEPS, D_HEAD, LANES), F32),
            pltpu.VMEM((LANES, LANES), BF16),
            pltpu.VMEM((LANES, LANES), BF16),
            pltpu.VMEM((8, LANES), F32),
            pltpu.VMEM((D_HEAD, LANES), F32),
            pltpu.VMEM((LANES, LANES), F32),
            pltpu.VMEM((LANES, LANES), F32),
            pltpu.VMEM((INNER, LANES), F32),
            pltpu.VMEM((INNER, LANES), F32),
            pltpu.VMEM((INNER, LANES), F32),
            pltpu.VMEM((HISTORY, LANES, INNER), BF16),
            pltpu.VMEM((HISTORY, D_HEAD, LANES), F32),
            pltpu.VMEM((D_HEAD, LANES), F32),
            pltpu.VMEM((D_HEAD, LANES), F32),
            pltpu.VMEM((INNER, LANES), F32),
            pltpu.VMEM((INNER, LANES), F32),
            pltpu.VMEM((2, INNER, LANES), BF16),
            pltpu.VMEM((HISTORY, INNER, LANES), BF16),
            pltpu.VMEM((HISTORY, D_HEAD, LANES), BF16),
            pltpu.VMEM((INNER, LANES), BF16),
            pltpu.VMEM((LANES, LANES), BF16),
            pltpu.VMEM((D_HEAD, LANES), F32),
            pltpu.VMEM((LANES, LANES), BF16),
            dma((7,)),
            dma((3,)),
            dma((3,)),
            dma((HEADS_NEAR,)),
            dma((STEPS,)),
            dma((HEADS_LOCAL,)),
            dma((CHAIN,)),
            dma((STEPS,)),
            dma((HEADS_NEAR,)),
            dma((1,)),
            dma((1,)),
        ],
        compiler_params=pltpu.CompilerParams(collective_id=0, has_side_effects=True),
    )(*arrays)
    return (gate.astype(F32) * summed.astype(F32)).astype(BF16)


def solution(mesh):
    rows = P(("seq", "head"), None)
    in_specs = (
        rows,
        rows,
        rows,
        rows,
        P("seq", "head"),
        P("head", None, None),
        P("head", None),
        P("head", None, None),
        P("head", None),
        P("head", None),
        P("head", None),
    )
    return jax.shard_map(local, mesh=mesh, in_specs=in_specs, out_specs=rows, check_vma=False)
```
